128 devices in a mesh: opair: 4 (over x), vpair: 32 (over z, y, core).
Axes of the slice: x: 4, y: 4, z: 4, core: 2. Of those that a mesh axis runs over, the one named last changes fastest.
Arguments:
- grid_tiles: bfloat16 [32768, 128, 128], P(('opair', 'vpair')), may hold values from -6 to 6
- tile_rows: int32 [32768], P(('opair', 'vpair')), may hold values from 0 to 127, as said below
- tile_cols: int32 [32768], P(('opair', 'vpair')), may hold values from 0 to 511, as said below
- tile_owner: int32 [32768], P(('opair', 'vpair')), may hold values from -1 to 16383, as said below
- integrals: bfloat16 [65536, 1024], P('vpair'), may hold values from -0.046875 to 0.046875
Outputs:
- ov_tiles: bfloat16 [16384, 128, 128], P(('opair', 'vpair'))
- cycle: float32 [16384, 1024], P(('opair', 'vpair'))
The draws below stay inside these ranges and needn't reach their ends.
Inputs may be any that keep to these rules, and one draw needn't show every extreme that they name: `tile_owner`: every position 0 to 16383 is named by exactly one slot; the other slots hold -1. Position p belongs to device p // 128. The slots of one device send to each device either no tiles or exactly 2. A device has at most 254 slots that are not -1, and some device has exactly that many. The row tile of a slot that is not empty lies in the opair group of its owner: tile_rows // 32 equals the opair index of device tile_owner // 128. Empty slots hold 0. The (kc) tile of a slot that is not empty lies in the vpair group of its owner: tile_cols // 16 equals the vpair index of device tile_owner // 128. No two slots that are not empty hold the same pair of tile_rows and tile_cols. Empty slots hold 0.
All inputs are finite; a program needn't handle non-finite values.
Results may differ from the reference program's by a relative error of at most 0.001.
Values may be sent and summed in bfloat16 or wider, within the bound.
A program may use at most 256 MiB of HBM per device.

```python
import jax
import jax.numpy as jnp
from jax import lax

TB = 128
RT_OP = 32
TILE_DEV = 128
NK_DEV = 16
JB = 1024
NR = 128
NK = 512
CAP = 2
TMAX = 256
TILES = 16384
DEVICES = 128


def shuffled_rows(key, row_count, length):
    scores = jax.random.randint(key, (row_count, length), 0, 65536) * length + jnp.arange(length)[None, :]
    return jnp.argsort(scores, axis=1).astype(jnp.int32)


def tile_layout(key):
    all_devices = DEVICES
    rounds = all_devices // 2
    vpair_count = NK // NK_DEV
    base = jax.random.fold_in(key, 4242)
    key_order, key_delta, key_destination, key_source, key_owner, key_cells = jax.random.split(base, 6)
    order = jax.random.permutation(key_order, all_devices).astype(jnp.int32)
    delta = jax.random.randint(key_delta, (all_devices // 2,), 0, rounds).at[0].set(rounds - 1)
    counts = jnp.zeros((all_devices,), jnp.int32).at[order[0::2]].set(rounds + delta).at[order[1::2]].set(rounds - delta)
    ends = jnp.cumsum(counts).astype(jnp.int32)
    starts = ends - counts
    entry = jnp.arange(all_devices * rounds, dtype=jnp.int32)
    source = jnp.searchsorted(ends, entry, side='right').astype(jnp.int32)
    within_source = entry - starts[source]
    dest_perm = jax.random.permutation(key_destination, all_devices).astype(jnp.int32)
    target = dest_perm[entry % all_devices]
    within_target = entry // all_devices
    copies = jnp.arange(CAP, dtype=jnp.int32)
    source_perm = shuffled_rows(key_source, all_devices, TMAX)
    owner_perm = shuffled_rows(key_owner, all_devices, TILE_DEV)
    cell_perm = shuffled_rows(key_cells, all_devices, RT_OP * NK_DEV)
    source_slot = source_perm[source[:, None], within_source[:, None] * CAP + copies[None, :]]
    owner_slot = owner_perm[target[:, None], within_target[:, None] * CAP + copies[None, :]]
    cell_index = cell_perm[target[:, None], owner_slot]
    position = target[:, None] * TILE_DEV + owner_slot
    rows_live = (target // vpair_count)[:, None] * RT_OP + cell_index // NK_DEV
    cols_live = (target % vpair_count)[:, None] * NK_DEV + cell_index % NK_DEV
    flat_slot = (source[:, None] * TMAX + source_slot).reshape(-1)
    owner_all = jnp.full((all_devices * TMAX,), -1, jnp.int32).at[flat_slot].set(position.reshape(-1).astype(jnp.int32))
    rows_all = jnp.zeros((all_devices * TMAX,), jnp.int32).at[flat_slot].set(rows_live.reshape(-1).astype(jnp.int32))
    cols_all = jnp.zeros((all_devices * TMAX,), jnp.int32).at[flat_slot].set(cols_live.reshape(-1).astype(jnp.int32))
    return (owner_all, rows_all, cols_all)


def draw_tile_owner(key, part):
    return tile_layout(key)[0]


def draw_tile_rows(key, part):
    return tile_layout(key)[1]


def draw_tile_cols(key, part):
    return tile_layout(key)[2]


def shard_levels(stream_key, shape, cuts, smallest, high):
    gain, own = 1.0, jax.random.fold_in(stream_key, 6)
    for dim, blocks in cuts:
        steps = jnp.exp(jax.random.uniform(jax.random.fold_in(own, dim), (blocks,), jnp.float32, smallest / len(cuts), high / len(cuts)))
        gain = gain * jnp.repeat(steps, shape[dim] // blocks).reshape([-1 if axis == dim else 1 for axis in range(len(shape))])
    return gain


def scatter_about(rng, dims, deviation, limit, cuts=(), kind=jnp.bfloat16):
    gain = shard_levels(rng, dims, cuts, -0.22, 0.18) if cuts else 1.0
    entries = jax.random.normal(rng, dims, jnp.float32) * deviation * gain
    return jnp.minimum(jnp.maximum(entries, -limit), limit).astype(kind)


def setup_inputs(seed: int = 0) -> dict:
    seeds = jax.random.split(jax.random.key(seed), 6)
    grid_tiles = scatter_about(seeds[0], (DEVICES * TMAX, TB, TB), 1.0, 6.0, ((0, 128),))
    tile_rows = draw_tile_rows(jax.random.fold_in(seeds[5], 71), 0)
    tile_cols = draw_tile_cols(jax.random.fold_in(seeds[5], 71), 0)
    tile_owner = draw_tile_owner(jax.random.fold_in(seeds[5], 71), 0)
    integrals = scatter_about(seeds[4], (NK * TB, JB), (NK * TB // 4) ** -0.5, 0.046875, ((0, 32),))
    return {"grid_tiles": grid_tiles, "tile_rows": tile_rows, "tile_cols": tile_cols, "tile_owner": tile_owner, "integrals": integrals}


def reference(grid_tiles, tile_rows, tile_cols, tile_owner, integrals):
    live_slots = tile_owner >= 0
    target = jnp.where(live_slots, tile_owner, TILES).astype(jnp.int32)
    ov_tiles = jnp.zeros((TILES, TB, TB), jnp.bfloat16).at[target].set(jnp.swapaxes(grid_tiles, 1, 2), mode="drop")
    live_index = jnp.nonzero(live_slots, size=TILES, fill_value=0)[0].astype(jnp.int32)
    block_rows = 128
    index_blocks = live_index.reshape(TILES // block_rows, block_rows)
    int_table = integrals.astype(jnp.float32).reshape(NK, TB, JB)

    def accumulate(running, block):
        tiles_subset = grid_tiles[block].astype(jnp.float32)
        rows_part = tile_rows[block].astype(jnp.int32)
        cols_part = tile_cols[block].astype(jnp.int32)
        selected_entries = int_table[cols_part]
        pairwise_products = jnp.einsum("wjf,wjq->wfq", tiles_subset, selected_entries, precision=lax.Precision.HIGHEST)
        return running.at[rows_part].add(pairwise_products), None

    start_sum = jnp.zeros((NR, TB, JB), jnp.float32)
    summed, _ = lax.scan(accumulate, start_sum, index_blocks)
    cycle = summed.reshape(NR * TB, JB)
    return ov_tiles, cycle
```

```python
import jax
import jax.numpy as jnp
from jax import lax
from jax.experimental import pallas as pl
from jax.experimental.pallas import tpu as pltpu
from jax.sharding import PartitionSpec as P

RT_OP = 32
VMEM_LIMIT = 60 * 1024 * 1024


def gather_kernel(src_ref, grid_ref, out_ref):
    zero = jnp.zeros(out_ref.shape[1:], out_ref.dtype)

    def body(j, carry):
        s = src_ref[j]

        @pl.when(s >= 0)
        def _():
            out_ref[j] = grid_ref[jnp.maximum(s, 0)]

        @pl.when(s < 0)
        def _():
            out_ref[j] = zero

        return carry

    lax.fori_loop(0, out_ref.shape[0], body, 0)


def gather_tiles(src, grid_tiles):
    return pl.pallas_call(
        gather_kernel,
        out_shape=jax.ShapeDtypeStruct(grid_tiles.shape, grid_tiles.dtype),
        in_specs=[
            pl.BlockSpec(memory_space=pltpu.SMEM),
            pl.BlockSpec(memory_space=pltpu.VMEM),
        ],
        out_specs=pl.BlockSpec(memory_space=pltpu.VMEM),
        compiler_params=pltpu.CompilerParams(vmem_limit_bytes=VMEM_LIMIT),
    )(src, grid_tiles)


def place_kernel(meta_ref, inc_ref, int_ref, ov_ref, part_ref):
    slots = inc_ref.shape[0]
    part_ref[...] = jnp.zeros(part_ref.shape, part_ref.dtype)

    def body(i, carry):
        pos = meta_ref[i]
        row = meta_ref[slots + i]
        col = meta_ref[2 * slots + i]

        @pl.when(pos >= 0)
        def _():
            tile_t = inc_ref[i].T
            ov_ref[pos] = tile_t
            part_ref[row] += jnp.dot(
                tile_t, int_ref[col], preferred_element_type=jnp.float32
            )

        return carry

    lax.fori_loop(0, slots, body, 0)


def place_and_contract(meta, incoming, int_table, owned, rows):
    tile_width = incoming.shape[1]
    columns = int_table.shape[2]
    return pl.pallas_call(
        place_kernel,
        out_shape=(
            jax.ShapeDtypeStruct((owned, tile_width, tile_width), incoming.dtype),
            jax.ShapeDtypeStruct((rows, tile_width, columns), jnp.float32),
        ),
        in_specs=[
            pl.BlockSpec(memory_space=pltpu.SMEM),
            pl.BlockSpec(memory_space=pltpu.VMEM),
            pl.BlockSpec(memory_space=pltpu.VMEM),
        ],
        out_specs=(
            pl.BlockSpec(memory_space=pltpu.VMEM),
            pl.BlockSpec(memory_space=pltpu.VMEM),
        ),
        compiler_params=pltpu.CompilerParams(vmem_limit_bytes=VMEM_LIMIT),
    )(meta, incoming, int_table)


def on_device(grid_tiles, tile_rows, tile_cols, tile_owner, integrals):
    op_count = lax.axis_size("opair")
    vp_count = lax.axis_size("vpair")
    devices = op_count * vp_count
    slot_count, tile_width, _ = grid_tiles.shape
    owned = slot_count // 2
    capacity = slot_count // devices
    kc_local = integrals.shape[0] // tile_width
    int_table = integrals.reshape(kc_local, tile_width, integrals.shape[1])
    live_slots = tile_owner >= 0
    target = jnp.where(live_slots, tile_owner // owned, devices)
    matches = (target[:, None] == jnp.arange(devices, dtype=jnp.int32)[None, :]).astype(jnp.int32)
    earlier = jnp.sum((jnp.cumsum(matches, axis=0) - matches) * matches, axis=1)
    placing = jnp.where(live_slots, target * capacity + earlier, devices * capacity)
    src = (
        jnp.full((devices * capacity + 1,), -1, jnp.int32)
        .at[placing]
        .set(jnp.arange(slot_count, dtype=jnp.int32))[: devices * capacity]
    )
    departing_tiles = gather_tiles(src, grid_tiles)
    label_rows = jnp.stack([tile_owner % owned, tile_rows % RT_OP, tile_cols % kc_local], axis=1)
    labels = jnp.where((src >= 0)[:, None], jnp.take(label_rows, jnp.maximum(src, 0), axis=0), -1)
    arrived = lax.all_to_all(labels, ("opair", "vpair"), split_axis=0, concat_axis=0, tiled=True)
    incoming = lax.all_to_all(
        departing_tiles, ("opair", "vpair"), split_axis=0, concat_axis=0, tiled=True
    )
    meta = jnp.transpose(arrived).reshape(-1)
    ov_tiles, partial_value = place_and_contract(meta, incoming, int_table, owned, RT_OP)
    partial_value = partial_value.reshape(RT_OP * tile_width, int_table.shape[2])
    cycle_sum = lax.psum_scatter(partial_value, "vpair", scatter_dimension=0, tiled=True)
    return (ov_tiles, cycle_sum)


def solution(mesh):
    in_specs = (
        P(("opair", "vpair"), None, None),
        P(("opair", "vpair")),
        P(("opair", "vpair")),
        P(("opair", "vpair")),
        P("vpair", None),
    )
    out_specs = (P(("opair", "vpair"), None, None), P(("opair", "vpair"), None))
    return jax.shard_map(
        on_device, mesh=mesh, in_specs=in_specs, out_specs=out_specs, check_vma=False
    )
```

```python
import functools

import jax
import jax.numpy as jnp
from jax import lax
from jax.experimental import pallas as pl
from jax.experimental.pallas import tpu as pltpu
from jax.sharding import PartitionSpec as P

RT_OP = 32
CHUNKS = 2
VMEM_LIMIT = 60 * 1024 * 1024


def gather_kernel(src_ref, grid_ref, out_ref):
    zero = jnp.zeros(out_ref.shape[1:], out_ref.dtype)

    def body(j, carry):
        s = src_ref[j]

        @pl.when(s >= 0)
        def _():
            out_ref[j] = grid_ref[jnp.maximum(s, 0)]

        @pl.when(s < 0)
        def _():
            out_ref[j] = zero

        return carry

    lax.fori_loop(0, out_ref.shape[0], body, 0)


def gather_tiles(src, grid_tiles):
    return pl.pallas_call(
        gather_kernel,
        out_shape=jax.ShapeDtypeStruct(grid_tiles.shape, grid_tiles.dtype),
        in_specs=[
            pl.BlockSpec(memory_space=pltpu.SMEM),
            pl.BlockSpec(memory_space=pltpu.VMEM),
        ],
        out_specs=pl.BlockSpec(memory_space=pltpu.VMEM),
        compiler_params=pltpu.CompilerParams(vmem_limit_bytes=VMEM_LIMIT),
    )(src, grid_tiles)


def place_kernel(meta_ref, inc_ref, ov_ref):
    slots = inc_ref.shape[0]

    def body(i, carry):
        pos = meta_ref[i]

        @pl.when(pos >= 0)
        def _():
            ov_ref[pos] = inc_ref[i].T

        return carry

    lax.fori_loop(0, slots, body, 0)


def place_tiles(meta, incoming, owned):
    tile_width = incoming.shape[1]
    return pl.pallas_call(
        place_kernel,
        out_shape=jax.ShapeDtypeStruct((owned, tile_width, tile_width), incoming.dtype),
        in_specs=[
            pl.BlockSpec(memory_space=pltpu.SMEM),
            pl.BlockSpec(memory_space=pltpu.VMEM),
        ],
        out_specs=pl.BlockSpec(memory_space=pltpu.VMEM),
        compiler_params=pltpu.CompilerParams(vmem_limit_bytes=VMEM_LIMIT),
    )(meta, incoming)


def contract_kernel(kc_local, cell_ref, ov_ref, int_ref, part_ref, lhs_ref):
    tile_width = ov_ref.shape[1]
    zero = jnp.zeros((tile_width, tile_width), ov_ref.dtype)

    def body(r, carry):
        for kc in range(kc_local):
            p = cell_ref[r * kc_local + kc]
            block = pl.ds(kc * tile_width, tile_width)

            @pl.when(p >= 0)
            def _():
                lhs_ref[:, block] = ov_ref[jnp.maximum(p, 0)]

            @pl.when(p < 0)
            def _():
                lhs_ref[:, block] = zero

        part_ref[r] = jnp.dot(lhs_ref[...], int_ref[...], preferred_element_type=jnp.float32)
        return carry

    lax.fori_loop(0, part_ref.shape[0], body, 0)


def contract(cell, ov_tiles, int_chunk, rows, kc_local):
    tile_width = ov_tiles.shape[1]
    columns = int_chunk.shape[1]
    return pl.pallas_call(
        functools.partial(contract_kernel, kc_local),
        out_shape=jax.ShapeDtypeStruct((rows, tile_width, columns), jnp.float32),
        in_specs=[
            pl.BlockSpec(memory_space=pltpu.SMEM),
            pl.BlockSpec(memory_space=pltpu.VMEM),
            pl.BlockSpec(memory_space=pltpu.VMEM),
        ],
        out_specs=pl.BlockSpec(memory_space=pltpu.VMEM),
        scratch_shapes=[pltpu.VMEM((tile_width, kc_local * tile_width), ov_tiles.dtype)],
        compiler_params=pltpu.CompilerParams(vmem_limit_bytes=VMEM_LIMIT),
    )(cell, ov_tiles, int_chunk)


def on_device(grid_tiles, tile_rows, tile_cols, tile_owner, integrals):
    op_count = lax.axis_size("opair")
    vp_count = lax.axis_size("vpair")
    devices = op_count * vp_count
    slot_count, tile_width, _ = grid_tiles.shape
    owned = slot_count // 2
    capacity = slot_count // devices
    kc_local = integrals.shape[0] // tile_width
    live_slots = tile_owner >= 0
    target = jnp.where(live_slots, tile_owner // owned, devices)
    matches = (target[:, None] == jnp.arange(devices, dtype=jnp.int32)[None, :]).astype(jnp.int32)
    earlier = jnp.sum((jnp.cumsum(matches, axis=0) - matches) * matches, axis=1)
    placing = jnp.where(live_slots, target * capacity + earlier, devices * capacity)
    src = (
        jnp.full((devices * capacity + 1,), -1, jnp.int32)
        .at[placing]
        .set(jnp.arange(slot_count, dtype=jnp.int32))[: devices * capacity]
    )
    departing_tiles = gather_tiles(src, grid_tiles)
    label_rows = jnp.stack([tile_owner % owned, tile_rows % RT_OP, tile_cols % kc_local], axis=1)
    labels = jnp.where((src >= 0)[:, None], jnp.take(label_rows, jnp.maximum(src, 0), axis=0), -1)
    arrived = lax.all_to_all(labels, ("opair", "vpair"), split_axis=0, concat_axis=0, tiled=True)
    incoming = lax.all_to_all(
        departing_tiles, ("opair", "vpair"), split_axis=0, concat_axis=0, tiled=True
    )
    pos = arrived[:, 0]
    ov_tiles = place_tiles(pos, incoming, owned)
    cell_id = jnp.where(pos >= 0, arrived[:, 1] * kc_local + arrived[:, 2], RT_OP * kc_local)
    cell = jnp.full((RT_OP * kc_local + 1,), -1, jnp.int32).at[cell_id].set(pos)[: RT_OP * kc_local]
    columns = integrals.shape[1]
    width = columns // CHUNKS
    pieces = []
    for c in range(CHUNKS):
        part = contract(cell, ov_tiles, integrals[:, c * width : (c + 1) * width], RT_OP, kc_local)
        part = part.reshape(RT_OP * tile_width, width)
        pieces.append(lax.psum_scatter(part, "vpair", scatter_dimension=0, tiled=True))
    cycle_sum = jnp.concatenate(pieces, axis=1)
    return (ov_tiles, cycle_sum)


def solution(mesh):
    in_specs = (
        P(("opair", "vpair"), None, None),
        P(("opair", "vpair")),
        P(("opair", "vpair")),
        P(("opair", "vpair")),
        P("vpair", None),
    )
    out_specs = (P(("opair", "vpair"), None, None), P(("opair", "vpair"), None))
    return jax.shard_map(
        on_device, mesh=mesh, in_specs=in_specs, out_specs=out_specs, check_vma=False
    )
```

```python
import functools

import jax
import jax.numpy as jnp
from jax import lax
from jax.experimental import pallas as pl
from jax.experimental.pallas import tpu as pltpu
from jax.sharding import PartitionSpec as P

RT_OP = 32
VMEM_LIMIT = 60 * 1024 * 1024


def gather_kernel(src_ref, grid_ref, out_ref):
    zero = jnp.zeros(out_ref.shape[1:], out_ref.dtype)

    def body(j, carry):
        s = src_ref[j]

        @pl.when(s >= 0)
        def _():
            out_ref[j] = grid_ref[jnp.maximum(s, 0)]

        @pl.when(s < 0)
        def _():
            out_ref[j] = zero

        return carry

    lax.fori_loop(0, out_ref.shape[0], body, 0)


def gather_tiles(src, grid_tiles):
    return pl.pallas_call(
        gather_kernel,
        out_shape=jax.ShapeDtypeStruct(grid_tiles.shape, grid_tiles.dtype),
        in_specs=[
            pl.BlockSpec(memory_space=pltpu.SMEM),
            pl.BlockSpec(memory_space=pltpu.VMEM),
        ],
        out_specs=pl.BlockSpec(memory_space=pltpu.VMEM),
        compiler_params=pltpu.CompilerParams(vmem_limit_bytes=VMEM_LIMIT),
    )(src, grid_tiles)


def place_kernel(kc_local, pos_ref, cell_ref, inc_ref, it_ref, ov_ref, part_ref, rhs_ref):
    slots, tile_width, _ = inc_ref.shape
    zero = jnp.zeros((tile_width, tile_width), inc_ref.dtype)

    def place(i, carry):
        pos = pos_ref[i]

        @pl.when(pos >= 0)
        def _():
            ov_ref[jnp.maximum(pos, 0)] = inc_ref[i].T

        return carry

    lax.fori_loop(0, slots, place, 0)

    def row(r, carry):
        for kc in range(kc_local):
            s = cell_ref[r * kc_local + kc]
            block = pl.ds(kc * tile_width, tile_width)

            @pl.when(s >= 0)
            def _():
                rhs_ref[block, :] = inc_ref[jnp.maximum(s, 0)]

            @pl.when(s < 0)
            def _():
                rhs_ref[block, :] = zero

        part_ref[r] = jnp.dot(it_ref[...], rhs_ref[...], preferred_element_type=jnp.float32)
        return carry

    lax.fori_loop(0, part_ref.shape[0], row, 0)


def place_and_contract(pos, cell, incoming, it_all, owned, rows, kc_local):
    tile_width = incoming.shape[1]
    columns = it_all.shape[0]
    return pl.pallas_call(
        functools.partial(place_kernel, kc_local),
        out_shape=(
            jax.ShapeDtypeStruct((owned, tile_width, tile_width), incoming.dtype),
            jax.ShapeDtypeStruct((rows, columns, tile_width), jnp.float32),
        ),
        in_specs=[
            pl.BlockSpec(memory_space=pltpu.SMEM),
            pl.BlockSpec(memory_space=pltpu.SMEM),
            pl.BlockSpec(memory_space=pltpu.VMEM),
            pl.BlockSpec(memory_space=pltpu.VMEM),
        ],
        out_specs=(
            pl.BlockSpec(memory_space=pltpu.VMEM),
            pl.BlockSpec(memory_space=pltpu.VMEM),
        ),
        scratch_shapes=[pltpu.VMEM((kc_local * tile_width, tile_width), incoming.dtype)],
        compiler_params=pltpu.CompilerParams(vmem_limit_bytes=VMEM_LIMIT),
    )(pos, cell, incoming, it_all)


def on_device(grid_tiles, tile_rows, tile_cols, tile_owner, integrals):
    op_count = lax.axis_size("opair")
    vp_count = lax.axis_size("vpair")
    devices = op_count * vp_count
    slot_count, tile_width, _ = grid_tiles.shape
    owned = slot_count // 2
    capacity = slot_count // devices
    kc_local = integrals.shape[0] // tile_width
    live_slots = tile_owner >= 0
    target = jnp.where(live_slots, tile_owner // owned, devices)
    matches = (target[:, None] == jnp.arange(devices, dtype=jnp.int32)[None, :]).astype(jnp.int32)
    earlier = jnp.sum((jnp.cumsum(matches, axis=0) - matches) * matches, axis=1)
    placing = jnp.where(live_slots, target * capacity + earlier, devices * capacity)
    src = (
        jnp.full((devices * capacity + 1,), -1, jnp.int32)
        .at[placing]
        .set(jnp.arange(slot_count, dtype=jnp.int32))[: devices * capacity]
    )
    departing_tiles = gather_tiles(src, grid_tiles)
    label_rows = jnp.stack([tile_owner % owned, tile_rows % RT_OP, tile_cols % kc_local], axis=1)
    labels = jnp.where((src >= 0)[:, None], jnp.take(label_rows, jnp.maximum(src, 0), axis=0), -1)
    arrived = lax.all_to_all(labels, ("opair", "vpair"), split_axis=0, concat_axis=0, tiled=True)
    incoming = lax.all_to_all(
        departing_tiles, ("opair", "vpair"), split_axis=0, concat_axis=0, tiled=True
    )
    pos = arrived[:, 0]
    cell_id = jnp.where(pos >= 0, arrived[:, 1] * kc_local + arrived[:, 2], RT_OP * kc_local)
    slot_ids = jnp.arange(slot_count, dtype=jnp.int32)
    cell = jnp.full((RT_OP * kc_local + 1,), -1, jnp.int32).at[cell_id].set(slot_ids)[: RT_OP * kc_local]
    it_all = jnp.transpose(integrals)
    ov_tiles, partial_t = place_and_contract(pos, cell, incoming, it_all, owned, RT_OP, kc_local)
    columns = integrals.shape[1]
    partial_t = partial_t.reshape(RT_OP * columns, tile_width)
    cycle_t = lax.psum_scatter(partial_t, "vpair", scatter_dimension=0, tiled=True)
    cycle_sum = jnp.transpose(cycle_t)
    return (ov_tiles, cycle_sum)


def solution(mesh):
    in_specs = (
        P(("opair", "vpair"), None, None),
        P(("opair", "vpair")),
        P(("opair", "vpair")),
        P(("opair", "vpair")),
        P("vpair", None),
    )
    out_specs = (P(("opair", "vpair"), None, None), P(("opair", "vpair"), None))
    return jax.shard_map(
        on_device, mesh=mesh, in_specs=in_specs, out_specs=out_specs, check_vma=False
    )
```

```python
import functools

import jax
import jax.numpy as jnp
from jax import lax
from jax.experimental import pallas as pl
from jax.experimental.pallas import tpu as pltpu
from jax.sharding import PartitionSpec as P

RT_OP = 32
QUARTERS = 4
MESH = pl.DeviceIdType.MESH
VMEM_LIMIT = 60 * 1024 * 1024


def gather_kernel(src_ref, grid_ref, out_ref):
    zero = jnp.zeros(out_ref.shape[1:], out_ref.dtype)

    def body(j, carry):
        s = src_ref[j]

        @pl.when(s >= 0)
        def _():
            out_ref[j] = grid_ref[jnp.maximum(s, 0)]

        @pl.when(s < 0)
        def _():
            out_ref[j] = zero

        return carry

    lax.fori_loop(0, out_ref.shape[0], body, 0)


def gather_tiles(src, grid_tiles):
    return pl.pallas_call(
        gather_kernel,
        out_shape=jax.ShapeDtypeStruct(grid_tiles.shape, grid_tiles.dtype),
        in_specs=[
            pl.BlockSpec(memory_space=pltpu.SMEM),
            pl.BlockSpec(memory_space=pltpu.VMEM),
        ],
        out_specs=pl.BlockSpec(memory_space=pltpu.VMEM),
        compiler_params=pltpu.CompilerParams(vmem_limit_bytes=VMEM_LIMIT),
    )(src, grid_tiles)


def storage_row(q, row, ring):
    c = row % 2
    y = (row // 2) % ring
    z = row // (2 * ring)
    half = ring * ring
    if q < 2:
        return c * half + y * ring + z
    return c * half + z * ring + y


def place_kernel(quarters, ring, meta_ref, inc_ref, int_ref, ov_ref, part_ref):
    slots = inc_ref.shape[0]
    width = part_ref.shape[3]
    part_ref[...] = jnp.zeros(part_ref.shape, part_ref.dtype)

    def body(i, carry):
        pos = meta_ref[i]
        row = meta_ref[slots + i]
        col = meta_ref[2 * slots + i]

        @pl.when(pos >= 0)
        def _():
            tile_t = inc_ref[i].T
            ov_ref[jnp.maximum(pos, 0)] = tile_t
            prod = jnp.dot(tile_t, int_ref[jnp.maximum(col, 0)], preferred_element_type=jnp.float32)
            for q in range(quarters):
                s = storage_row(q, jnp.maximum(row, 0), ring)
                part_ref[q, s] += prod[:, q * width : (q + 1) * width]

        return carry

    lax.fori_loop(0, slots, body, 0)


def place_and_contract(meta, incoming, int_table, owned, rows, quarters, ring):
    tile_width = incoming.shape[1]
    columns = int_table.shape[2]
    return pl.pallas_call(
        functools.partial(place_kernel, quarters, ring),
        out_shape=(
            jax.ShapeDtypeStruct((owned, tile_width, tile_width), incoming.dtype),
            jax.ShapeDtypeStruct((quarters, rows, tile_width, columns // quarters), jnp.float32),
        ),
        in_specs=[
            pl.BlockSpec(memory_space=pltpu.SMEM),
            pl.BlockSpec(memory_space=pltpu.VMEM),
            pl.BlockSpec(memory_space=pltpu.VMEM),
        ],
        out_specs=(
            pl.BlockSpec(memory_space=pltpu.VMEM),
            pl.BlockSpec(memory_space=pltpu.VMEM),
        ),
        compiler_params=pltpu.CompilerParams(vmem_limit_bytes=VMEM_LIMIT),
    )(meta, incoming, int_table)


def rs_kernel(ring, part_ref, out_ref, core_buf, red, rbuf1, acc1, fin1, rbuf2, acc2,
              core_send, core_recv, send1, recv1, send2, recv2):
    quarters, rows, tile_width, width = part_ref.shape
    half = rows // 2
    steps = ring - 1
    op = lax.axis_index("opair")
    v = lax.axis_index("vpair")
    c = v % 2
    y = (v // 2) % ring
    z = v // (2 * ring)

    def dev(zz, yy, cc):
        return (op, (zz * ring + yy) * 2 + cc)

    sib = dev(z, y, 1 - c)
    y_up = dev(z, (y + 1) % ring, c)
    y_dn = dev(z, (y + ring - 1) % ring, c)
    z_up = dev((z + 1) % ring, y, c)
    z_dn = dev((z + ring - 1) % ring, y, c)

    barrier = pltpu.get_barrier_semaphore()
    for peer in (sib, y_up, y_dn, z_up, z_dn):
        pl.semaphore_signal(barrier, inc=1, device_id=peer, device_id_type=MESH)
    pl.semaphore_wait(barrier, 5)

    core_copy = pltpu.make_async_remote_copy(
        src_ref=part_ref.at[:, pl.ds((1 - c) * half, half)],
        dst_ref=core_buf,
        send_sem=core_send,
        recv_sem=core_recv,
        device_id=sib,
        device_id_type=MESH,
    )
    core_copy.start()
    core_copy.wait()

    def core_sum(k, carry):
        q = k // half
        i = k % half
        red[q, i] = part_ref[q, c * half + i] + core_buf[q, i]
        return carry

    lax.fori_loop(0, quarters * half, core_sum, 0)

    def plan(q):
        d = 1 if q % 2 == 0 else -1
        if q < 2:
            return d, y, z, (y_up if d > 0 else y_dn), (z_up if d > 0 else z_dn)
        return d, z, y, (z_up if d > 0 else z_dn), (y_up if d > 0 else y_dn)

    for s in range(steps):
        copies = []
        for q in range(quarters):
            d, a, b, first, second = plan(q)
            blk = (a - d * (s + 1) + 2 * ring) % ring
            if s == 0:
                src = red.at[q, pl.ds(blk * ring, ring)]
            else:
                src = acc1.at[q, s - 1]
            cp = pltpu.make_async_remote_copy(
                src_ref=src,
                dst_ref=rbuf1.at[q, s],
                send_sem=send1.at[q, s],
                recv_sem=recv1.at[q, s],
                device_id=first,
                device_id_type=MESH,
            )
            cp.start()
            copies.append(cp)
        for q in range(quarters):
            copies[q].wait()
            d, a, b, first, second = plan(q)
            blk = (a - d * (s + 2) + 3 * ring) % ring
            for j in range(ring):
                total = rbuf1[q, s, j] + red[q, blk * ring + j]
                if s < steps - 1:
                    acc1[q, s, j] = total
                else:
                    fin1[q, j] = total

    for s in range(steps):
        copies = []
        for q in range(quarters):
            d, a, b, first, second = plan(q)
            blk = (b - d * (s + 1) + 2 * ring) % ring
            if s == 0:
                src = fin1.at[q, blk]
            else:
                src = acc2.at[q, s - 1]
            cp = pltpu.make_async_remote_copy(
                src_ref=src,
                dst_ref=rbuf2.at[q, s],
                send_sem=send2.at[q, s],
                recv_sem=recv2.at[q, s],
                device_id=second,
                device_id_type=MESH,
            )
            cp.start()
            copies.append(cp)
        for q in range(quarters):
            copies[q].wait()
            d, a, b, first, second = plan(q)
            blk = (b - d * (s + 2) + 3 * ring) % ring
            total = rbuf2[q, s] + fin1[q, blk]
            if s < steps - 1:
                acc2[q, s] = total
            else:
                out_ref[:, q * width : (q + 1) * width] = total


def reduce_scatter(part, ring):
    quarters, rows, tile_width, width = part.shape
    half = rows // 2
    steps = ring - 1
    f32 = jnp.float32
    return pl.pallas_call(
        functools.partial(rs_kernel, ring),
        out_shape=jax.ShapeDtypeStruct((tile_width, quarters * width), f32),
        in_specs=[pl.BlockSpec(memory_space=pltpu.VMEM)],
        out_specs=pl.BlockSpec(memory_space=pltpu.VMEM),
        scratch_shapes=[
            pltpu.VMEM((quarters, half, tile_width, width), f32),
            pltpu.VMEM((quarters, half, tile_width, width), f32),
            pltpu.VMEM((quarters, steps, ring, tile_width, width), f32),
            pltpu.VMEM((quarters, steps - 1, ring, tile_width, width), f32),
            pltpu.VMEM((quarters, ring, tile_width, width), f32),
            pltpu.VMEM((quarters, steps, tile_width, width), f32),
            pltpu.VMEM((quarters, steps - 1, tile_width, width), f32),
            pltpu.SemaphoreType.DMA(()),
            pltpu.SemaphoreType.DMA(()),
            pltpu.SemaphoreType.DMA((quarters, steps)),
            pltpu.SemaphoreType.DMA((quarters, steps)),
            pltpu.SemaphoreType.DMA((quarters, steps)),
            pltpu.SemaphoreType.DMA((quarters, steps)),
        ],
        compiler_params=pltpu.CompilerParams(
            collective_id=0, has_side_effects=True, vmem_limit_bytes=VMEM_LIMIT
        ),
    )(part)


def on_device(grid_tiles, tile_rows, tile_cols, tile_owner, integrals):
    op_count = lax.axis_size("opair")
    vp_count = lax.axis_size("vpair")
    devices = op_count * vp_count
    slot_count, tile_width, _ = grid_tiles.shape
    owned = slot_count // 2
    capacity = slot_count // devices
    kc_local = integrals.shape[0] // tile_width
    int_table = integrals.reshape(kc_local, tile_width, integrals.shape[1])
    live_slots = tile_owner >= 0
    target = jnp.where(live_slots, tile_owner // owned, devices)
    matches = (target[:, None] == jnp.arange(devices, dtype=jnp.int32)[None, :]).astype(jnp.int32)
    earlier = jnp.sum((jnp.cumsum(matches, axis=0) - matches) * matches, axis=1)
    placing = jnp.where(live_slots, target * capacity + earlier, devices * capacity)
    src = (
        jnp.full((devices * capacity + 1,), -1, jnp.int32)
        .at[placing]
        .set(jnp.arange(slot_count, dtype=jnp.int32))[: devices * capacity]
    )
    departing_tiles = gather_tiles(src, grid_tiles)
    label_rows = jnp.stack([tile_owner % owned, tile_rows % RT_OP, tile_cols % kc_local], axis=1)
    labels = jnp.where((src >= 0)[:, None], jnp.take(label_rows, jnp.maximum(src, 0), axis=0), -1)
    arrived = lax.all_to_all(labels, ("opair", "vpair"), split_axis=0, concat_axis=0, tiled=True)
    incoming = lax.all_to_all(
        departing_tiles, ("opair", "vpair"), split_axis=0, concat_axis=0, tiled=True
    )
    meta = jnp.transpose(arrived).reshape(-1)
    ring = 4
    ov_tiles, partial_value = place_and_contract(
        meta, incoming, int_table, owned, RT_OP, QUARTERS, ring
    )
    cycle_sum = reduce_scatter(partial_value, ring)
    return (ov_tiles, cycle_sum)


def solution(mesh):
    in_specs = (
        P(("opair", "vpair"), None, None),
        P(("opair", "vpair")),
        P(("opair", "vpair")),
        P(("opair", "vpair")),
        P("vpair", None),
    )
    out_specs = (P(("opair", "vpair"), None, None), P(("opair", "vpair"), None))
    return jax.shard_map(
        on_device, mesh=mesh, in_specs=in_specs, out_specs=out_specs, check_vma=False
    )
```

```python
import functools

import jax
import jax.numpy as jnp
from jax import lax
from jax.experimental import pallas as pl
from jax.experimental.pallas import tpu as pltpu
from jax.sharding import PartitionSpec as P

RT_OP = 32
QUARTERS = 4
MESH = pl.DeviceIdType.MESH
VMEM_LIMIT = 60 * 1024 * 1024


def gather_kernel(src_ref, grid_ref, out_ref):
    zero = jnp.zeros(out_ref.shape[1:], out_ref.dtype)

    def body(j, carry):
        s = src_ref[j]

        @pl.when(s >= 0)
        def _():
            out_ref[j] = grid_ref[jnp.maximum(s, 0)]

        @pl.when(s < 0)
        def _():
            out_ref[j] = zero

        return carry

    lax.fori_loop(0, out_ref.shape[0], body, 0)


def gather_tiles(src, grid_tiles):
    return pl.pallas_call(
        gather_kernel,
        out_shape=jax.ShapeDtypeStruct(grid_tiles.shape, grid_tiles.dtype),
        in_specs=[
            pl.BlockSpec(memory_space=pltpu.SMEM),
            pl.BlockSpec(memory_space=pltpu.VMEM),
        ],
        out_specs=pl.BlockSpec(memory_space=pltpu.VMEM),
        compiler_params=pltpu.CompilerParams(vmem_limit_bytes=VMEM_LIMIT),
    )(src, grid_tiles)


def storage_row(q, row, ring):
    c = row % 2
    y = (row // 2) % ring
    z = row // (2 * ring)
    half = ring * ring
    if q < 2:
        return c * half + y * ring + z
    return c * half + z * ring + y


def place_kernel(quarters, ring, meta_ref, inc_ref, int_ref, ov_ref, part_ref):
    slots = inc_ref.shape[0]
    width = part_ref.shape[2]
    part_ref[...] = jnp.zeros(part_ref.shape, part_ref.dtype)

    def body(i, carry):
        pos = meta_ref[i]
        row = meta_ref[slots + i]
        col = meta_ref[2 * slots + i]

        @pl.when(pos >= 0)
        def _():
            tile = inc_ref[i]
            ov_ref[jnp.maximum(pos, 0)] = tile.T
            prod = jnp.dot(int_ref[jnp.maximum(col, 0)], tile, preferred_element_type=jnp.float32)
            for q in range(quarters):
                s = storage_row(q, jnp.maximum(row, 0), ring)
                part_ref[q, s] += prod[q * width : (q + 1) * width, :]

        return carry

    lax.fori_loop(0, slots, body, 0)


def place_and_contract(meta, incoming, int_table, owned, rows, quarters, ring):
    tile_width = incoming.shape[1]
    columns = int_table.shape[1]
    return pl.pallas_call(
        functools.partial(place_kernel, quarters, ring),
        out_shape=(
            jax.ShapeDtypeStruct((owned, tile_width, tile_width), incoming.dtype),
            jax.ShapeDtypeStruct((quarters, rows, columns // quarters, tile_width), jnp.float32),
        ),
        in_specs=[
            pl.BlockSpec(memory_space=pltpu.SMEM),
            pl.BlockSpec(memory_space=pltpu.VMEM),
            pl.BlockSpec(memory_space=pltpu.VMEM),
        ],
        out_specs=(
            pl.BlockSpec(memory_space=pltpu.VMEM),
            pl.BlockSpec(memory_space=pltpu.VMEM),
        ),
        compiler_params=pltpu.CompilerParams(vmem_limit_bytes=VMEM_LIMIT),
    )(meta, incoming, int_table)


def rs_kernel(ring, part_ref, out_ref, core_buf, red, rbuf1, acc1, fin1, rbuf2, acc2,
              core_send, core_recv, send1, recv1, send2, recv2):
    quarters, rows, tile_width, width = part_ref.shape
    half = rows // 2
    steps = ring - 1
    op = lax.axis_index("opair")
    v = lax.axis_index("vpair")
    c = v % 2
    y = (v // 2) % ring
    z = v // (2 * ring)

    def dev(zz, yy, cc):
        return (op, (zz * ring + yy) * 2 + cc)

    sib = dev(z, y, 1 - c)
    y_up = dev(z, (y + 1) % ring, c)
    y_dn = dev(z, (y + ring - 1) % ring, c)
    z_up = dev((z + 1) % ring, y, c)
    z_dn = dev((z + ring - 1) % ring, y, c)

    barrier = pltpu.get_barrier_semaphore()
    for peer in (sib, y_up, y_dn, z_up, z_dn):
        pl.semaphore_signal(barrier, inc=1, device_id=peer, device_id_type=MESH)
    pl.semaphore_wait(barrier, 5)

    core_copy = pltpu.make_async_remote_copy(
        src_ref=part_ref.at[:, pl.ds((1 - c) * half, half)],
        dst_ref=core_buf,
        send_sem=core_send,
        recv_sem=core_recv,
        device_id=sib,
        device_id_type=MESH,
    )
    core_copy.start()
    core_copy.wait()

    def core_sum(k, carry):
        q = k // half
        i = k % half
        red[q, i] = part_ref[q, c * half + i] + core_buf[q, i]
        return carry

    lax.fori_loop(0, quarters * half, core_sum, 0)

    def plan(q):
        d = 1 if q % 2 == 0 else -1
        if q < 2:
            return d, y, z, (y_up if d > 0 else y_dn), (z_up if d > 0 else z_dn)
        return d, z, y, (z_up if d > 0 else z_dn), (y_up if d > 0 else y_dn)

    for s in range(steps):
        copies = []
        for q in range(quarters):
            d, a, b, first, second = plan(q)
            blk = (a - d * (s + 1) + 2 * ring) % ring
            if s == 0:
                src = red.at[q, pl.ds(blk * ring, ring)]
            else:
                src = acc1.at[q, s - 1]
            cp = pltpu.make_async_remote_copy(
                src_ref=src,
                dst_ref=rbuf1.at[q, s],
                send_sem=send1.at[q, s],
                recv_sem=recv1.at[q, s],
                device_id=first,
                device_id_type=MESH,
            )
            cp.start()
            copies.append(cp)
        for q in range(quarters):
            copies[q].wait()
            d, a, b, first, second = plan(q)
            blk = (a - d * (s + 2) + 3 * ring) % ring
            for j in range(ring):
                total = rbuf1[q, s, j] + red[q, blk * ring + j]
                if s < steps - 1:
                    acc1[q, s, j] = total
                else:
                    fin1[q, j] = total

    for s in range(steps):
        copies = []
        for q in range(quarters):
            d, a, b, first, second = plan(q)
            blk = (b - d * (s + 1) + 2 * ring) % ring
            if s == 0:
                src = fin1.at[q, blk]
            else:
                src = acc2.at[q, s - 1]
            cp = pltpu.make_async_remote_copy(
                src_ref=src,
                dst_ref=rbuf2.at[q, s],
                send_sem=send2.at[q, s],
                recv_sem=recv2.at[q, s],
                device_id=second,
                device_id_type=MESH,
            )
            cp.start()
            copies.append(cp)
        for q in range(quarters):
            copies[q].wait()
            d, a, b, first, second = plan(q)
            blk = (b - d * (s + 2) + 3 * ring) % ring
            total = rbuf2[q, s] + fin1[q, blk]
            if s < steps - 1:
                acc2[q, s] = total
            else:
                out_ref[q] = total


def reduce_scatter(part, ring):
    quarters, rows, tile_width, width = part.shape
    half = rows // 2
    steps = ring - 1
    f32 = jnp.float32
    return pl.pallas_call(
        functools.partial(rs_kernel, ring),
        out_shape=jax.ShapeDtypeStruct((quarters, tile_width, width), f32),
        in_specs=[pl.BlockSpec(memory_space=pltpu.VMEM)],
        out_specs=pl.BlockSpec(memory_space=pltpu.VMEM),
        scratch_shapes=[
            pltpu.VMEM((quarters, half, tile_width, width), f32),
            pltpu.VMEM((quarters, half, tile_width, width), f32),
            pltpu.VMEM((quarters, steps, ring, tile_width, width), f32),
            pltpu.VMEM((quarters, steps - 1, ring, tile_width, width), f32),
            pltpu.VMEM((quarters, ring, tile_width, width), f32),
            pltpu.VMEM((quarters, steps, tile_width, width), f32),
            pltpu.VMEM((quarters, steps - 1, tile_width, width), f32),
            pltpu.SemaphoreType.DMA(()),
            pltpu.SemaphoreType.DMA(()),
            pltpu.SemaphoreType.DMA((quarters, steps)),
            pltpu.SemaphoreType.DMA((quarters, steps)),
            pltpu.SemaphoreType.DMA((quarters, steps)),
            pltpu.SemaphoreType.DMA((quarters, steps)),
        ],
        compiler_params=pltpu.CompilerParams(
            collective_id=0, has_side_effects=True, vmem_limit_bytes=VMEM_LIMIT
        ),
    )(part)


def on_device(grid_tiles, tile_rows, tile_cols, tile_owner, integrals):
    op_count = lax.axis_size("opair")
    vp_count = lax.axis_size("vpair")
    devices = op_count * vp_count
    slot_count, tile_width, _ = grid_tiles.shape
    owned = slot_count // 2
    capacity = slot_count // devices
    kc_local = integrals.shape[0] // tile_width
    int_table = jnp.swapaxes(integrals.reshape(kc_local, tile_width, integrals.shape[1]), 1, 2)
    live_slots = tile_owner >= 0
    target = jnp.where(live_slots, tile_owner // owned, devices)
    matches = (target[:, None] == jnp.arange(devices, dtype=jnp.int32)[None, :]).astype(jnp.int32)
    earlier = jnp.sum((jnp.cumsum(matches, axis=0) - matches) * matches, axis=1)
    placing = jnp.where(live_slots, target * capacity + earlier, devices * capacity)
    src = (
        jnp.full((devices * capacity + 1,), -1, jnp.int32)
        .at[placing]
        .set(jnp.arange(slot_count, dtype=jnp.int32))[: devices * capacity]
    )
    departing_tiles = gather_tiles(src, grid_tiles)
    label_rows = jnp.stack([tile_owner % owned, tile_rows % RT_OP, tile_cols % kc_local], axis=1)
    labels = jnp.where((src >= 0)[:, None], jnp.take(label_rows, jnp.maximum(src, 0), axis=0), -1)
    arrived = lax.all_to_all(labels, ("opair", "vpair"), split_axis=0, concat_axis=0, tiled=True)
    incoming = lax.all_to_all(
        departing_tiles, ("opair", "vpair"), split_axis=0, concat_axis=0, tiled=True
    )
    meta = jnp.transpose(arrived).reshape(-1)
    ring = 4
    ov_tiles, partial_value = place_and_contract(
        meta, incoming, int_table, owned, RT_OP, QUARTERS, ring
    )
    cycle_t = reduce_scatter(partial_value, ring)
    cycle_sum = jnp.transpose(cycle_t.reshape(-1, tile_width))
    return (ov_tiles, cycle_sum)


def solution(mesh):
    in_specs = (
        P(("opair", "vpair"), None, None),
        P(("opair", "vpair")),
        P(("opair", "vpair")),
        P(("opair", "vpair")),
        P("vpair", None),
    )
    out_specs = (P(("opair", "vpair"), None, None), P(("opair", "vpair"), None))
    return jax.shard_map(
        on_device, mesh=mesh, in_specs=in_specs, out_specs=out_specs, check_vma=False
    )
```

```python
import functools

import jax
import jax.numpy as jnp
from jax import lax
from jax.experimental import pallas as pl
from jax.experimental.pallas import tpu as pltpu
from jax.sharding import PartitionSpec as P

RT_OP = 32
QUARTERS = 4
MESH = pl.DeviceIdType.MESH
VMEM_LIMIT = 60 * 1024 * 1024


def gather_kernel(src_ref, grid_ref, out_ref):
    zero = jnp.zeros(out_ref.shape[1:], out_ref.dtype)

    def body(j, carry):
        s = src_ref[j]

        @pl.when(s >= 0)
        def _():
            out_ref[j] = grid_ref[jnp.maximum(s, 0)]

        @pl.when(s < 0)
        def _():
            out_ref[j] = zero

        return carry

    lax.fori_loop(0, out_ref.shape[0], body, 0)


def gather_tiles(src, grid_tiles):
    return pl.pallas_call(
        gather_kernel,
        out_shape=jax.ShapeDtypeStruct(grid_tiles.shape, grid_tiles.dtype),
        in_specs=[
            pl.BlockSpec(memory_space=pltpu.SMEM),
            pl.BlockSpec(memory_space=pltpu.VMEM),
        ],
        out_specs=pl.BlockSpec(memory_space=pltpu.VMEM),
        compiler_params=pltpu.CompilerParams(vmem_limit_bytes=VMEM_LIMIT),
    )(src, grid_tiles)


def storage_row(q, row, ring):
    c = row % 2
    y = (row // 2) % ring
    z = row // (2 * ring)
    half = ring * ring
    if q < 2:
        return c * half + y * ring + z
    return c * half + z * ring + y


def place_kernel(quarters, ring, pos_ref, order_ref, starts_ref, col_ref, inc_ref, int_ref, ov_ref, part_ref):
    slots = inc_ref.shape[0]
    rows = part_ref.shape[1]
    width = part_ref.shape[2]

    def place(i, carry):
        pos = pos_ref[i]

        @pl.when(pos >= 0)
        def _():
            ov_ref[jnp.maximum(pos, 0)] = inc_ref[i].T

        return carry

    lax.fori_loop(0, slots, place, 0)

    def row(r, carry):
        lo = starts_ref[r]
        hi = starts_ref[r + 1]
        for q in range(quarters):

            def add(t, acc):
                i = order_ref[t]
                block = int_ref[col_ref[i], pl.ds(q * width, width), :]
                return acc + jnp.dot(block, inc_ref[i], preferred_element_type=jnp.float32)

            acc = lax.fori_loop(lo, hi, add, jnp.zeros(part_ref.shape[2:], jnp.float32))
            part_ref[q, storage_row(q, r, ring)] = acc
        return carry

    lax.fori_loop(0, rows, row, 0)


def place_and_contract(pos, order, starts, col, incoming, int_table, owned, rows, quarters, ring):
    tile_width = incoming.shape[1]
    columns = int_table.shape[1]
    smem = pl.BlockSpec(memory_space=pltpu.SMEM)
    return pl.pallas_call(
        functools.partial(place_kernel, quarters, ring),
        out_shape=(
            jax.ShapeDtypeStruct((owned, tile_width, tile_width), incoming.dtype),
            jax.ShapeDtypeStruct((quarters, rows, columns // quarters, tile_width), jnp.float32),
        ),
        in_specs=[smem, smem, smem, smem,
            pl.BlockSpec(memory_space=pltpu.VMEM),
            pl.BlockSpec(memory_space=pltpu.VMEM),
        ],
        out_specs=(
            pl.BlockSpec(memory_space=pltpu.VMEM),
            pl.BlockSpec(memory_space=pltpu.VMEM),
        ),
        compiler_params=pltpu.CompilerParams(vmem_limit_bytes=VMEM_LIMIT),
    )(pos, order, starts, col, incoming, int_table)


def rs_kernel(ring, part_ref, out_ref, core_buf, red, rbuf1, acc1, fin1, rbuf2, acc2,
              core_send, core_recv, send1, recv1, send2, recv2):
    quarters, rows, tile_width, width = part_ref.shape
    half = rows // 2
    steps = ring - 1
    op = lax.axis_index("opair")
    v = lax.axis_index("vpair")
    c = v % 2
    y = (v // 2) % ring
    z = v // (2 * ring)

    def dev(zz, yy, cc):
        return (op, (zz * ring + yy) * 2 + cc)

    sib = dev(z, y, 1 - c)
    y_up = dev(z, (y + 1) % ring, c)
    y_dn = dev(z, (y + ring - 1) % ring, c)
    z_up = dev((z + 1) % ring, y, c)
    z_dn = dev((z + ring - 1) % ring, y, c)

    barrier = pltpu.get_barrier_semaphore()
    for peer in (sib, y_up, y_dn, z_up, z_dn):
        pl.semaphore_signal(barrier, inc=1, device_id=peer, device_id_type=MESH)
    pl.semaphore_wait(barrier, 5)

    core_copy = pltpu.make_async_remote_copy(
        src_ref=part_ref.at[:, pl.ds((1 - c) * half, half)],
        dst_ref=core_buf,
        send_sem=core_send,
        recv_sem=core_recv,
        device_id=sib,
        device_id_type=MESH,
    )
    core_copy.start()
    core_copy.wait()

    def core_sum(k, carry):
        q = k // half
        i = k % half
        red[q, i] = part_ref[q, c * half + i] + core_buf[q, i]
        return carry

    lax.fori_loop(0, quarters * half, core_sum, 0)

    def plan(q):
        d = 1 if q % 2 == 0 else -1
        if q < 2:
            return d, y, z, (y_up if d > 0 else y_dn), (z_up if d > 0 else z_dn)
        return d, z, y, (z_up if d > 0 else z_dn), (y_up if d > 0 else y_dn)

    for s in range(steps):
        copies = []
        for q in range(quarters):
            d, a, b, first, second = plan(q)
            blk = (a - d * (s + 1) + 2 * ring) % ring
            if s == 0:
                src = red.at[q, pl.ds(blk * ring, ring)]
            else:
                src = acc1.at[q, s - 1]
            cp = pltpu.make_async_remote_copy(
                src_ref=src,
                dst_ref=rbuf1.at[q, s],
                send_sem=send1.at[q, s],
                recv_sem=recv1.at[q, s],
                device_id=first,
                device_id_type=MESH,
            )
            cp.start()
            copies.append(cp)
        for q in range(quarters):
            copies[q].wait()
            d, a, b, first, second = plan(q)
            blk = (a - d * (s + 2) + 3 * ring) % ring
            for j in range(ring):
                total = rbuf1[q, s, j] + red[q, blk * ring + j]
                if s < steps - 1:
                    acc1[q, s, j] = total
                else:
                    fin1[q, j] = total

    for s in range(steps):
        copies = []
        for q in range(quarters):
            d, a, b, first, second = plan(q)
            blk = (b - d * (s + 1) + 2 * ring) % ring
            if s == 0:
                src = fin1.at[q, blk]
            else:
                src = acc2.at[q, s - 1]
            cp = pltpu.make_async_remote_copy(
                src_ref=src,
                dst_ref=rbuf2.at[q, s],
                send_sem=send2.at[q, s],
                recv_sem=recv2.at[q, s],
                device_id=second,
                device_id_type=MESH,
            )
            cp.start()
            copies.append(cp)
        for q in range(quarters):
            copies[q].wait()
            d, a, b, first, second = plan(q)
            blk = (b - d * (s + 2) + 3 * ring) % ring
            total = rbuf2[q, s] + fin1[q, blk]
            if s < steps - 1:
                acc2[q, s] = total
            else:
                out_ref[q] = total


def reduce_scatter(part, ring):
    quarters, rows, tile_width, width = part.shape
    half = rows // 2
    steps = ring - 1
    f32 = jnp.float32
    return pl.pallas_call(
        functools.partial(rs_kernel, ring),
        out_shape=jax.ShapeDtypeStruct((quarters, tile_width, width), f32),
        in_specs=[pl.BlockSpec(memory_space=pltpu.VMEM)],
        out_specs=pl.BlockSpec(memory_space=pltpu.VMEM),
        scratch_shapes=[
            pltpu.VMEM((quarters, half, tile_width, width), f32),
            pltpu.VMEM((quarters, half, tile_width, width), f32),
            pltpu.VMEM((quarters, steps, ring, tile_width, width), f32),
            pltpu.VMEM((quarters, steps - 1, ring, tile_width, width), f32),
            pltpu.VMEM((quarters, ring, tile_width, width), f32),
            pltpu.VMEM((quarters, steps, tile_width, width), f32),
            pltpu.VMEM((quarters, steps - 1, tile_width, width), f32),
            pltpu.SemaphoreType.DMA(()),
            pltpu.SemaphoreType.DMA(()),
            pltpu.SemaphoreType.DMA((quarters, steps)),
            pltpu.SemaphoreType.DMA((quarters, steps)),
            pltpu.SemaphoreType.DMA((quarters, steps)),
            pltpu.SemaphoreType.DMA((quarters, steps)),
        ],
        compiler_params=pltpu.CompilerParams(
            collective_id=0, has_side_effects=True, vmem_limit_bytes=VMEM_LIMIT
        ),
    )(part)


def on_device(grid_tiles, tile_rows, tile_cols, tile_owner, integrals):
    op_count = lax.axis_size("opair")
    vp_count = lax.axis_size("vpair")
    devices = op_count * vp_count
    slot_count, tile_width, _ = grid_tiles.shape
    owned = slot_count // 2
    capacity = slot_count // devices
    kc_local = integrals.shape[0] // tile_width
    int_table = jnp.swapaxes(integrals.reshape(kc_local, tile_width, integrals.shape[1]), 1, 2)
    live_slots = tile_owner >= 0
    target = jnp.where(live_slots, tile_owner // owned, devices)
    matches = (target[:, None] == jnp.arange(devices, dtype=jnp.int32)[None, :]).astype(jnp.int32)
    earlier = jnp.sum((jnp.cumsum(matches, axis=0) - matches) * matches, axis=1)
    placing = jnp.where(live_slots, target * capacity + earlier, devices * capacity)
    src = (
        jnp.full((devices * capacity + 1,), -1, jnp.int32)
        .at[placing]
        .set(jnp.arange(slot_count, dtype=jnp.int32))[: devices * capacity]
    )
    departing_tiles = gather_tiles(src, grid_tiles)
    label_rows = jnp.stack([tile_owner % owned, tile_rows % RT_OP, tile_cols % kc_local], axis=1)
    labels = jnp.where((src >= 0)[:, None], jnp.take(label_rows, jnp.maximum(src, 0), axis=0), -1)
    arrived = lax.all_to_all(labels, ("opair", "vpair"), split_axis=0, concat_axis=0, tiled=True)
    incoming = lax.all_to_all(
        departing_tiles, ("opair", "vpair"), split_axis=0, concat_axis=0, tiled=True
    )
    ring = 4
    pos = arrived[:, 0]
    valid = pos >= 0
    key = jnp.where(valid, arrived[:, 1], RT_OP)
    slot_ids = jnp.arange(slot_count, dtype=jnp.int32)
    before = (key[None, :] < key[:, None]) | ((key[None, :] == key[:, None]) & (slot_ids[None, :] < slot_ids[:, None]))
    rank = jnp.sum(before.astype(jnp.int32), axis=1)
    order = jnp.zeros((slot_count,), jnp.int32).at[rank].set(slot_ids)
    row_ids = jnp.arange(RT_OP + 1, dtype=jnp.int32)
    starts = jnp.sum((key[None, :] < row_ids[:, None]).astype(jnp.int32), axis=1)
    col = jnp.maximum(arrived[:, 2], 0)
    ov_tiles, partial_value = place_and_contract(
        pos, order, starts, col, incoming, int_table, owned, RT_OP, QUARTERS, ring
    )
    cycle_t = reduce_scatter(partial_value, ring)
    cycle_sum = jnp.transpose(cycle_t.reshape(-1, tile_width))
    return (ov_tiles, cycle_sum)


def solution(mesh):
    in_specs = (
        P(("opair", "vpair"), None, None),
        P(("opair", "vpair")),
        P(("opair", "vpair")),
        P(("opair", "vpair")),
        P("vpair", None),
    )
    out_specs = (P(("opair", "vpair"), None, None), P(("opair", "vpair"), None))
    return jax.shard_map(
        on_device, mesh=mesh, in_specs=in_specs, out_specs=out_specs, check_vma=False
    )
```

```python
import functools

import jax
import jax.numpy as jnp
from jax import lax
from jax.experimental import pallas as pl
from jax.experimental.pallas import tpu as pltpu
from jax.sharding import PartitionSpec as P

RT_OP = 32
QUARTERS = 4
MESH = pl.DeviceIdType.MESH
VMEM_LIMIT = 60 * 1024 * 1024


def gather_kernel(src_ref, grid_ref, out_ref):
    zero = jnp.zeros(out_ref.shape[1:], out_ref.dtype)

    def body(j, carry):
        s = src_ref[j]

        @pl.when(s >= 0)
        def _():
            out_ref[j] = grid_ref[jnp.maximum(s, 0)]

        @pl.when(s < 0)
        def _():
            out_ref[j] = zero

        return carry

    lax.fori_loop(0, out_ref.shape[0], body, 0)


def gather_tiles(src, grid_tiles):
    return pl.pallas_call(
        gather_kernel,
        out_shape=jax.ShapeDtypeStruct(grid_tiles.shape, grid_tiles.dtype),
        in_specs=[
            pl.BlockSpec(memory_space=pltpu.SMEM),
            pl.BlockSpec(memory_space=pltpu.VMEM),
        ],
        out_specs=pl.BlockSpec(memory_space=pltpu.VMEM),
        compiler_params=pltpu.CompilerParams(vmem_limit_bytes=VMEM_LIMIT),
    )(src, grid_tiles)


def storage_row(q, row, ring):
    c = row % 2
    y = (row // 2) % ring
    z = row // (2 * ring)
    half = ring * ring
    if q < 2:
        return c * half + y * ring + z
    return c * half + z * ring + y


def place_kernel(quarters, ring, meta_ref, inc_ref, int_ref, ov_ref, part_ref):
    slots = inc_ref.shape[0]
    width = part_ref.shape[2]
    part_ref[...] = jnp.zeros(part_ref.shape, part_ref.dtype)

    def body(i, carry):
        pos = meta_ref[i]
        row = meta_ref[slots + i]
        col = meta_ref[2 * slots + i]

        @pl.when(pos >= 0)
        def _():
            tile = inc_ref[i]
            ov_ref[jnp.maximum(pos, 0)] = tile.T
            prod = jnp.dot(int_ref[jnp.maximum(col, 0)], tile, preferred_element_type=jnp.float32)
            for q in range(quarters):
                s = storage_row(q, jnp.maximum(row, 0), ring)
                part_ref[q, s] += prod[q * width : (q + 1) * width, :]

        return carry

    lax.fori_loop(0, slots, body, 0)


def place_and_contract(meta, incoming, int_table, owned, rows, quarters, ring):
    tile_width = incoming.shape[1]
    columns = int_table.shape[1]
    return pl.pallas_call(
        functools.partial(place_kernel, quarters, ring),
        out_shape=(
            jax.ShapeDtypeStruct((owned, tile_width, tile_width), incoming.dtype),
            jax.ShapeDtypeStruct((quarters, rows, columns // quarters, tile_width), jnp.float32),
        ),
        in_specs=[
            pl.BlockSpec(memory_space=pltpu.SMEM),
            pl.BlockSpec(memory_space=pltpu.VMEM),
            pl.BlockSpec(memory_space=pltpu.VMEM),
        ],
        out_specs=(
            pl.BlockSpec(memory_space=pltpu.VMEM),
            pl.BlockSpec(memory_space=pltpu.VMEM),
        ),
        compiler_params=pltpu.CompilerParams(vmem_limit_bytes=VMEM_LIMIT),
    )(meta, incoming, int_table)


def rs_kernel(ring, part_ref, out_ref, core_buf, red, rbuf1, acc1, fin1, rbuf2, acc2,
              core_send, core_recv, send1, recv1, send2, recv2):
    quarters, rows, tile_width, width = part_ref.shape
    half = rows // 2
    steps = ring - 1
    op = lax.axis_index("opair")
    v = lax.axis_index("vpair")
    c = v % 2
    y = (v // 2) % ring
    z = v // (2 * ring)

    def dev(zz, yy, cc):
        return (op, (zz * ring + yy) * 2 + cc)

    sib = dev(z, y, 1 - c)
    y_up = dev(z, (y + 1) % ring, c)
    y_dn = dev(z, (y + ring - 1) % ring, c)
    z_up = dev((z + 1) % ring, y, c)
    z_dn = dev((z + ring - 1) % ring, y, c)

    barrier = pltpu.get_barrier_semaphore()
    for peer in (sib, y_up, y_dn, z_up, z_dn):
        pl.semaphore_signal(barrier, inc=1, device_id=peer, device_id_type=MESH)
    pl.semaphore_wait(barrier, 5)

    core_copy = pltpu.make_async_remote_copy(
        src_ref=part_ref.at[:, pl.ds((1 - c) * half, half)],
        dst_ref=core_buf,
        send_sem=core_send,
        recv_sem=core_recv,
        device_id=sib,
        device_id_type=MESH,
    )
    core_copy.start()
    core_copy.wait()

    def core_sum(k, carry):
        q = k // half
        i = k % half
        red[q, i] = part_ref[q, c * half + i] + core_buf[q, i]
        return carry

    lax.fori_loop(0, quarters * half, core_sum, 0)

    def plan(q):
        d = 1 if q % 2 == 0 else -1
        if q < 2:
            return d, y, z, (y_up if d > 0 else y_dn), (z_up if d > 0 else z_dn)
        return d, z, y, (z_up if d > 0 else z_dn), (y_up if d > 0 else y_dn)

    for s in range(steps):
        copies = []
        for q in range(quarters):
            d, a, b, first, second = plan(q)
            blk = (a - d * (s + 1) + 2 * ring) % ring
            if s == 0:
                src = red.at[q, pl.ds(blk * ring, ring)]
            else:
                src = acc1.at[q, s - 1]
            cp = pltpu.make_async_remote_copy(
                src_ref=src,
                dst_ref=rbuf1.at[q, s],
                send_sem=send1.at[q, s],
                recv_sem=recv1.at[q, s],
                device_id=first,
                device_id_type=MESH,
            )
            cp.start()
            copies.append(cp)
        for q in range(quarters):
            copies[q].wait()
            d, a, b, first, second = plan(q)
            blk = (a - d * (s + 2) + 3 * ring) % ring
            for j in range(ring):
                total = rbuf1[q, s, j] + red[q, blk * ring + j]
                if s < steps - 1:
                    acc1[q, s, j] = total
                else:
                    fin1[q, j] = total

    for s in range(steps):
        copies = []
        for q in range(quarters):
            d, a, b, first, second = plan(q)
            blk = (b - d * (s + 1) + 2 * ring) % ring
            if s == 0:
                src = fin1.at[q, blk]
            else:
                src = acc2.at[q, s - 1]
            cp = pltpu.make_async_remote_copy(
                src_ref=src,
                dst_ref=rbuf2.at[q, s],
                send_sem=send2.at[q, s],
                recv_sem=recv2.at[q, s],
                device_id=second,
                device_id_type=MESH,
            )
            cp.start()
            copies.append(cp)
        for q in range(quarters):
            copies[q].wait()
            d, a, b, first, second = plan(q)
            blk = (b - d * (s + 2) + 3 * ring) % ring
            total = rbuf2[q, s] + fin1[q, blk]
            if s < steps - 1:
                acc2[q, s] = total
            else:
                out_ref[q] = total


def reduce_scatter(part, ring):
    quarters, rows, tile_width, width = part.shape
    half = rows // 2
    steps = ring - 1
    f32 = jnp.float32
    return pl.pallas_call(
        functools.partial(rs_kernel, ring),
        out_shape=jax.ShapeDtypeStruct((quarters, tile_width, width), f32),
        in_specs=[pl.BlockSpec(memory_space=pltpu.VMEM)],
        out_specs=pl.BlockSpec(memory_space=pltpu.VMEM),
        scratch_shapes=[
            pltpu.VMEM((quarters, half, tile_width, width), f32),
            pltpu.VMEM((quarters, half, tile_width, width), f32),
            pltpu.VMEM((quarters, steps, ring, tile_width, width), f32),
            pltpu.VMEM((quarters, steps - 1, ring, tile_width, width), f32),
            pltpu.VMEM((quarters, ring, tile_width, width), f32),
            pltpu.VMEM((quarters, steps, tile_width, width), f32),
            pltpu.VMEM((quarters, steps - 1, tile_width, width), f32),
            pltpu.SemaphoreType.DMA(()),
            pltpu.SemaphoreType.DMA(()),
            pltpu.SemaphoreType.DMA((quarters, steps)),
            pltpu.SemaphoreType.DMA((quarters, steps)),
            pltpu.SemaphoreType.DMA((quarters, steps)),
            pltpu.SemaphoreType.DMA((quarters, steps)),
        ],
        compiler_params=pltpu.CompilerParams(
            collective_id=0, has_side_effects=True, vmem_limit_bytes=VMEM_LIMIT
        ),
    )(part)


def on_device(grid_tiles, tile_rows, tile_cols, tile_owner, integrals):
    op_count = lax.axis_size("opair")
    vp_count = lax.axis_size("vpair")
    devices = op_count * vp_count
    slot_count, tile_width, _ = grid_tiles.shape
    owned = slot_count // 2
    capacity = slot_count // devices
    kc_local = integrals.shape[0] // tile_width
    int_table = jnp.swapaxes(integrals.reshape(kc_local, tile_width, integrals.shape[1]), 1, 2)
    live_slots = tile_owner >= 0
    target = jnp.where(live_slots, tile_owner // owned, devices)
    matches = (target[:, None] == jnp.arange(devices, dtype=jnp.int32)[None, :]).astype(jnp.int32)
    earlier = jnp.sum((jnp.cumsum(matches, axis=0) - matches) * matches, axis=1)
    placing = jnp.where(live_slots, target * capacity + earlier, devices * capacity)
    src = (
        jnp.full((devices * capacity + 1,), -1, jnp.int32)
        .at[placing]
        .set(jnp.arange(slot_count, dtype=jnp.int32))[: devices * capacity]
    )
    departing_tiles = gather_tiles(src, grid_tiles)
    everything = lax.all_gather(
        jnp.stack([tile_owner, tile_rows, tile_cols]), ("opair", "vpair"), axis=0, tiled=False
    )
    incoming = lax.all_to_all(
        departing_tiles, ("opair", "vpair"), split_axis=0, concat_axis=0, tiled=True
    )
    me = lax.axis_index("opair") * vp_count + lax.axis_index("vpair")
    g_owner = everything[:, 0]
    mine = (g_owner >= 0) & (g_owner // owned == me)
    mine_i = mine.astype(jnp.int32)
    rank = jnp.cumsum(mine_i, axis=1) - mine_i
    source = jnp.arange(devices, dtype=jnp.int32)[:, None]
    landing = jnp.where(mine, source * capacity + rank, slot_count).reshape(-1)
    fields = jnp.stack(
        [g_owner % owned, everything[:, 1] % RT_OP, everything[:, 2] % kc_local], axis=-1
    ).reshape(-1, 3)
    arrived = jnp.full((slot_count + 1, 3), -1, jnp.int32).at[landing].set(fields)[:slot_count]
    meta = jnp.transpose(arrived).reshape(-1)
    ring = 4
    ov_tiles, partial_value = place_and_contract(
        meta, incoming, int_table, owned, RT_OP, QUARTERS, ring
    )
    cycle_t = reduce_scatter(partial_value, ring)
    cycle_sum = jnp.transpose(cycle_t.reshape(-1, tile_width))
    return (ov_tiles, cycle_sum)


def solution(mesh):
    in_specs = (
        P(("opair", "vpair"), None, None),
        P(("opair", "vpair")),
        P(("opair", "vpair")),
        P(("opair", "vpair")),
        P("vpair", None),
    )
    out_specs = (P(("opair", "vpair"), None, None), P(("opair", "vpair"), None))
    return jax.shard_map(
        on_device, mesh=mesh, in_specs=in_specs, out_specs=out_specs, check_vma=False
    )
```

```python
import functools

import jax
import jax.numpy as jnp
from jax import lax
from jax.experimental import pallas as pl
from jax.experimental.pallas import tpu as pltpu
from jax.sharding import PartitionSpec as P

RT_OP = 32
QUARTERS = 4
MESH = pl.DeviceIdType.MESH
VMEM_LIMIT = 60 * 1024 * 1024


def gather_kernel(src_ref, grid_ref, out_ref):
    zero = jnp.zeros(out_ref.shape[1:], out_ref.dtype)

    def body(j, carry):
        s = src_ref[j]

        @pl.when(s >= 0)
        def _():
            out_ref[j] = grid_ref[jnp.maximum(s, 0)]

        @pl.when(s < 0)
        def _():
            out_ref[j] = zero

        return carry

    lax.fori_loop(0, out_ref.shape[0], body, 0)


def gather_tiles(src, grid_tiles):
    return pl.pallas_call(
        gather_kernel,
        out_shape=jax.ShapeDtypeStruct(grid_tiles.shape, grid_tiles.dtype),
        in_specs=[
            pl.BlockSpec(memory_space=pltpu.SMEM),
            pl.BlockSpec(memory_space=pltpu.VMEM),
        ],
        out_specs=pl.BlockSpec(memory_space=pltpu.VMEM),
        compiler_params=pltpu.CompilerParams(vmem_limit_bytes=VMEM_LIMIT),
    )(src, grid_tiles)


def storage_row(q, row, ring):
    c = row % 2
    y = (row // 2) % ring
    z = row // (2 * ring)
    half = ring * ring
    if q < 2:
        return c * half + y * ring + z
    return c * half + z * ring + y


def place_kernel(quarters, ring, meta_ref, inc_ref, int_ref, ov_ref, part_ref):
    slots = inc_ref.shape[0]
    width = part_ref.shape[2]
    part_ref[...] = jnp.zeros(part_ref.shape, part_ref.dtype)

    def body(i, carry):
        pos = meta_ref[i]
        row = meta_ref[slots + i]
        col = meta_ref[2 * slots + i]

        @pl.when(pos >= 0)
        def _():
            tile = inc_ref[i]
            ov_ref[jnp.maximum(pos, 0)] = tile.T
            prod = jnp.dot(int_ref[jnp.maximum(col, 0)], tile, preferred_element_type=jnp.float32)
            for q in range(quarters):
                s = storage_row(q, jnp.maximum(row, 0), ring)
                part_ref[q, s] += prod[q * width : (q + 1) * width, :]

        return carry

    lax.fori_loop(0, slots, body, 0)


def place_and_contract(meta, incoming, int_table, owned, rows, quarters, ring):
    tile_width = incoming.shape[1]
    columns = int_table.shape[1]
    return pl.pallas_call(
        functools.partial(place_kernel, quarters, ring),
        out_shape=(
            jax.ShapeDtypeStruct((owned, tile_width, tile_width), incoming.dtype),
            jax.ShapeDtypeStruct((quarters, rows, columns // quarters, tile_width), jnp.float32),
        ),
        in_specs=[
            pl.BlockSpec(memory_space=pltpu.SMEM),
            pl.BlockSpec(memory_space=pltpu.VMEM),
            pl.BlockSpec(memory_space=pltpu.VMEM),
        ],
        out_specs=(
            pl.BlockSpec(memory_space=pltpu.VMEM),
            pl.BlockSpec(memory_space=pltpu.VMEM),
        ),
        compiler_params=pltpu.CompilerParams(vmem_limit_bytes=VMEM_LIMIT),
    )(meta, incoming, int_table)


def rs_kernel(ring, part_ref, out_ref, core_buf, red, rbuf1, acc1, fin1, rbuf2, acc2,
              core_send, core_recv, send1, recv1, send2, recv2):
    quarters, rows, tile_width, width = part_ref.shape
    half = rows // 2
    steps = ring - 1
    op = lax.axis_index("opair")
    v = lax.axis_index("vpair")
    c = v % 2
    y = (v // 2) % ring
    z = v // (2 * ring)

    def dev(zz, yy, cc):
        return (op, (zz * ring + yy) * 2 + cc)

    sib = dev(z, y, 1 - c)
    y_up = dev(z, (y + 1) % ring, c)
    y_dn = dev(z, (y + ring - 1) % ring, c)
    z_up = dev((z + 1) % ring, y, c)
    z_dn = dev((z + ring - 1) % ring, y, c)

    barrier = pltpu.get_barrier_semaphore()
    for peer in (sib, y_up, y_dn, z_up, z_dn):
        pl.semaphore_signal(barrier, inc=1, device_id=peer, device_id_type=MESH)
    pl.semaphore_wait(barrier, 5)

    core_copy = pltpu.make_async_remote_copy(
        src_ref=part_ref.at[:, pl.ds((1 - c) * half, half)],
        dst_ref=core_buf,
        send_sem=core_send,
        recv_sem=core_recv,
        device_id=sib,
        device_id_type=MESH,
    )
    core_copy.start()
    core_copy.wait()

    def core_sum(k, carry):
        q = k // half
        i = k % half
        red[q, i] = part_ref[q, c * half + i] + core_buf[q, i]
        return carry

    lax.fori_loop(0, quarters * half, core_sum, 0)

    def plan(q):
        d = 1 if q % 2 == 0 else -1
        if q < 2:
            return d, y, z, (y_up if d > 0 else y_dn), (z_up if d > 0 else z_dn)
        return d, z, y, (z_up if d > 0 else z_dn), (y_up if d > 0 else y_dn)

    for s in range(steps):
        copies = []
        for q in range(quarters):
            d, a, b, first, second = plan(q)
            blk = (a - d * (s + 1) + 2 * ring) % ring
            if s == 0:
                src = red.at[q, pl.ds(blk * ring, ring)]
            else:
                src = acc1.at[q, s - 1]
            cp = pltpu.make_async_remote_copy(
                src_ref=src,
                dst_ref=rbuf1.at[q, s],
                send_sem=send1.at[q, s],
                recv_sem=recv1.at[q, s],
                device_id=first,
                device_id_type=MESH,
            )
            cp.start()
            copies.append(cp)
        for q in range(quarters):
            copies[q].wait()
            d, a, b, first, second = plan(q)
            blk = (a - d * (s + 2) + 3 * ring) % ring
            for j in range(ring):
                total = rbuf1[q, s, j] + red[q, blk * ring + j]
                if s < steps - 1:
                    acc1[q, s, j] = total
                else:
                    fin1[q, j] = total

    for s in range(steps):
        copies = []
        for q in range(quarters):
            d, a, b, first, second = plan(q)
            blk = (b - d * (s + 1) + 2 * ring) % ring
            if s == 0:
                src = fin1.at[q, blk]
            else:
                src = acc2.at[q, s - 1]
            cp = pltpu.make_async_remote_copy(
                src_ref=src,
                dst_ref=rbuf2.at[q, s],
                send_sem=send2.at[q, s],
                recv_sem=recv2.at[q, s],
                device_id=second,
                device_id_type=MESH,
            )
            cp.start()
            copies.append(cp)
        for q in range(quarters):
            copies[q].wait()
            d, a, b, first, second = plan(q)
            blk = (b - d * (s + 2) + 3 * ring) % ring
            total = rbuf2[q, s] + fin1[q, blk]
            if s < steps - 1:
                acc2[q, s] = total
            else:
                out_ref[q] = total


def reduce_scatter(part, ring):
    quarters, rows, tile_width, width = part.shape
    half = rows // 2
    steps = ring - 1
    f32 = jnp.float32
    return pl.pallas_call(
        functools.partial(rs_kernel, ring),
        out_shape=jax.ShapeDtypeStruct((quarters, tile_width, width), f32),
        in_specs=[pl.BlockSpec(memory_space=pltpu.VMEM)],
        out_specs=pl.BlockSpec(memory_space=pltpu.VMEM),
        scratch_shapes=[
            pltpu.VMEM((quarters, half, tile_width, width), f32),
            pltpu.VMEM((quarters, half, tile_width, width), f32),
            pltpu.VMEM((quarters, steps, ring, tile_width, width), f32),
            pltpu.VMEM((quarters, steps - 1, ring, tile_width, width), f32),
            pltpu.VMEM((quarters, ring, tile_width, width), f32),
            pltpu.VMEM((quarters, steps, tile_width, width), f32),
            pltpu.VMEM((quarters, steps - 1, tile_width, width), f32),
            pltpu.SemaphoreType.DMA(()),
            pltpu.SemaphoreType.DMA(()),
            pltpu.SemaphoreType.DMA((quarters, steps)),
            pltpu.SemaphoreType.DMA((quarters, steps)),
            pltpu.SemaphoreType.DMA((quarters, steps)),
            pltpu.SemaphoreType.DMA((quarters, steps)),
        ],
        compiler_params=pltpu.CompilerParams(
            collective_id=0, has_side_effects=True, vmem_limit_bytes=VMEM_LIMIT
        ),
    )(part)


def on_device(grid_tiles, tile_rows, tile_cols, tile_owner, integrals):
    op_count = lax.axis_size("opair")
    vp_count = lax.axis_size("vpair")
    devices = op_count * vp_count
    slot_count, tile_width, _ = grid_tiles.shape
    owned = slot_count // 2
    capacity = slot_count // devices
    kc_local = integrals.shape[0] // tile_width
    int_table = jnp.swapaxes(integrals.reshape(kc_local, tile_width, integrals.shape[1]), 1, 2)
    live_slots = tile_owner >= 0
    target = jnp.where(live_slots, tile_owner // owned, devices)
    matches = (target[:, None] == jnp.arange(devices, dtype=jnp.int32)[None, :]).astype(jnp.int32)
    earlier = jnp.sum((jnp.cumsum(matches, axis=0) - matches) * matches, axis=1)
    placing = jnp.where(live_slots, target * capacity + earlier, devices * capacity)
    src = (
        jnp.full((devices * capacity + 1,), -1, jnp.int32)
        .at[placing]
        .set(jnp.arange(slot_count, dtype=jnp.int32))[: devices * capacity]
    )
    departing_tiles = gather_tiles(src, grid_tiles)
    everything = lax.all_gather(
        jnp.stack([tile_owner, tile_rows, tile_cols]), ("opair", "vpair"), axis=0, tiled=False
    )
    incoming = lax.all_to_all(
        departing_tiles, ("opair", "vpair"), split_axis=0, concat_axis=0, tiled=True
    )
    me = lax.axis_index("opair") * vp_count + lax.axis_index("vpair")
    g_owner = everything[:, 0]
    mine = (g_owner >= 0) & (g_owner // owned == me)
    mine_i = mine.astype(jnp.int32)
    rank = jnp.cumsum(mine_i, axis=1) - mine_i
    fields = jnp.stack([g_owner % owned, everything[:, 1] % RT_OP, everything[:, 2] % kc_local], axis=-1)
    picked = []
    for k in range(capacity):
        chosen = mine & (rank == k)
        found = jnp.any(chosen, axis=1)
        value = jnp.sum(jnp.where(chosen[:, :, None], fields, 0), axis=1)
        picked.append(jnp.where(found[:, None], value, -1))
    arrived = jnp.stack(picked, axis=1).reshape(slot_count, 3)
    meta = jnp.transpose(arrived).reshape(-1)
    ring = 4
    ov_tiles, partial_value = place_and_contract(
        meta, incoming, int_table, owned, RT_OP, QUARTERS, ring
    )
    cycle_t = reduce_scatter(partial_value, ring)
    cycle_sum = jnp.transpose(cycle_t.reshape(-1, tile_width))
    return (ov_tiles, cycle_sum)


def solution(mesh):
    in_specs = (
        P(("opair", "vpair"), None, None),
        P(("opair", "vpair")),
        P(("opair", "vpair")),
        P(("opair", "vpair")),
        P("vpair", None),
    )
    out_specs = (P(("opair", "vpair"), None, None), P(("opair", "vpair"), None))
    return jax.shard_map(
        on_device, mesh=mesh, in_specs=in_specs, out_specs=out_specs, check_vma=False
    )
```

```python
import functools

import jax
import jax.numpy as jnp
from jax import lax
from jax.experimental import pallas as pl
from jax.experimental.pallas import tpu as pltpu
from jax.sharding import PartitionSpec as P

RT_OP = 32
QUARTERS = 4
MESH = pl.DeviceIdType.MESH
VMEM_LIMIT = 60 * 1024 * 1024


def gather_kernel(src_ref, grid_ref, out_ref):
    zero = jnp.zeros(out_ref.shape[1:], out_ref.dtype)

    def body(j, carry):
        s = src_ref[j]

        @pl.when(s >= 0)
        def _():
            out_ref[j] = grid_ref[jnp.maximum(s, 0)]

        @pl.when(s < 0)
        def _():
            out_ref[j] = zero

        return carry

    lax.fori_loop(0, out_ref.shape[0], body, 0)


def gather_tiles(src, grid_tiles):
    return pl.pallas_call(
        gather_kernel,
        out_shape=jax.ShapeDtypeStruct(grid_tiles.shape, grid_tiles.dtype),
        in_specs=[
            pl.BlockSpec(memory_space=pltpu.SMEM),
            pl.BlockSpec(memory_space=pltpu.VMEM),
        ],
        out_specs=pl.BlockSpec(memory_space=pltpu.VMEM),
        compiler_params=pltpu.CompilerParams(vmem_limit_bytes=VMEM_LIMIT),
    )(src, grid_tiles)


def storage_row(q, row, ring):
    c = row % 2
    y = (row // 2) % ring
    z = row // (2 * ring)
    half = ring * ring
    if q < 2:
        return c * half + y * ring + z
    return c * half + z * ring + y


def place_kernel(quarters, ring, with_ov, meta_ref, inc_ref, int_ref, *outs):
    part_ref = outs[-1]
    slots = inc_ref.shape[0]
    half = part_ref.shape[1]
    width = part_ref.shape[2]
    want = meta_ref[3 * slots]
    part_ref[...] = jnp.zeros(part_ref.shape, part_ref.dtype)

    def body(i, carry):
        pos = meta_ref[i]
        row = jnp.maximum(meta_ref[slots + i], 0)
        col = jnp.maximum(meta_ref[2 * slots + i], 0)

        if with_ov:

            @pl.when(pos >= 0)
            def _():
                outs[0][jnp.maximum(pos, 0)] = inc_ref[i].T

        @pl.when((pos >= 0) & (row % 2 == want))
        def _():
            prod = jnp.dot(int_ref[col], inc_ref[i], preferred_element_type=jnp.float32)
            for q in range(quarters):
                s = storage_row(q, row, ring) - want * half
                part_ref[q, s] += prod[q * width : (q + 1) * width, :]

        return carry

    lax.fori_loop(0, slots, body, 0)


def place_and_contract(meta, incoming, int_table, owned, rows, quarters, ring, with_ov):
    tile_width = incoming.shape[1]
    columns = int_table.shape[1]
    part_shape = jax.ShapeDtypeStruct((quarters, rows // 2, columns // quarters, tile_width), jnp.float32)
    vmem = pl.BlockSpec(memory_space=pltpu.VMEM)
    if with_ov:
        out_shape = (jax.ShapeDtypeStruct((owned, tile_width, tile_width), incoming.dtype), part_shape)
        out_specs = (vmem, vmem)
    else:
        out_shape = (part_shape,)
        out_specs = (vmem,)
    return pl.pallas_call(
        functools.partial(place_kernel, quarters, ring, with_ov),
        out_shape=out_shape,
        in_specs=[pl.BlockSpec(memory_space=pltpu.SMEM), vmem, vmem],
        out_specs=out_specs,
        compiler_params=pltpu.CompilerParams(vmem_limit_bytes=VMEM_LIMIT),
        cost_estimate=pl.CostEstimate(
            flops=2 * tile_width * tile_width * columns * owned // 2,
            bytes_accessed=incoming.size * 2 + int_table.size * 2 + part_shape.size * 4,
            transcendentals=0,
        ),
    )(meta, incoming, int_table)


def rs_kernel(ring, part_ref, core_buf, out_ref, red, rbuf1, acc1, fin1, rbuf2, acc2,
              send1, recv1, send2, recv2):
    quarters, half, tile_width, width = part_ref.shape
    steps = ring - 1
    op = lax.axis_index("opair")
    v = lax.axis_index("vpair")
    c = v % 2
    y = (v // 2) % ring
    z = v // (2 * ring)

    def dev(zz, yy, cc):
        return (op, (zz * ring + yy) * 2 + cc)

    y_up = dev(z, (y + 1) % ring, c)
    y_dn = dev(z, (y + ring - 1) % ring, c)
    z_up = dev((z + 1) % ring, y, c)
    z_dn = dev((z + ring - 1) % ring, y, c)

    barrier = pltpu.get_barrier_semaphore()
    for peer in (y_up, y_dn, z_up, z_dn):
        pl.semaphore_signal(barrier, inc=1, device_id=peer, device_id_type=MESH)

    def core_sum(k, carry):
        q = k // half
        i = k % half
        red[q, i] = part_ref[q, i] + core_buf[q, i]
        return carry

    lax.fori_loop(0, quarters * half, core_sum, 0)
    pl.semaphore_wait(barrier, 4)

    def plan(q):
        d = 1 if q % 2 == 0 else -1
        if q < 2:
            return d, y, z, (y_up if d > 0 else y_dn), (z_up if d > 0 else z_dn)
        return d, z, y, (z_up if d > 0 else z_dn), (y_up if d > 0 else y_dn)

    for s in range(steps):
        copies = []
        for q in range(quarters):
            d, a, b, first, second = plan(q)
            blk = (a - d * (s + 1) + 2 * ring) % ring
            if s == 0:
                src = red.at[q, pl.ds(blk * ring, ring)]
            else:
                src = acc1.at[q, s - 1]
            cp = pltpu.make_async_remote_copy(
                src_ref=src,
                dst_ref=rbuf1.at[q, s],
                send_sem=send1.at[q, s],
                recv_sem=recv1.at[q, s],
                device_id=first,
                device_id_type=MESH,
            )
            cp.start()
            copies.append(cp)
        for q in range(quarters):
            copies[q].wait()
            d, a, b, first, second = plan(q)
            blk = (a - d * (s + 2) + 3 * ring) % ring
            for j in range(ring):
                total = rbuf1[q, s, j] + red[q, blk * ring + j]
                if s < steps - 1:
                    acc1[q, s, j] = total
                else:
                    fin1[q, j] = total

    for s in range(steps):
        copies = []
        for q in range(quarters):
            d, a, b, first, second = plan(q)
            blk = (b - d * (s + 1) + 2 * ring) % ring
            if s == 0:
                src = fin1.at[q, blk]
            else:
                src = acc2.at[q, s - 1]
            cp = pltpu.make_async_remote_copy(
                src_ref=src,
                dst_ref=rbuf2.at[q, s],
                send_sem=send2.at[q, s],
                recv_sem=recv2.at[q, s],
                device_id=second,
                device_id_type=MESH,
            )
            cp.start()
            copies.append(cp)
        for q in range(quarters):
            copies[q].wait()
            d, a, b, first, second = plan(q)
            blk = (b - d * (s + 2) + 3 * ring) % ring
            total = rbuf2[q, s] + fin1[q, blk]
            if s < steps - 1:
                acc2[q, s] = total
            else:
                out_ref[q] = total


def reduce_scatter(part, core_part, ring):
    quarters, half, tile_width, width = part.shape
    steps = ring - 1
    f32 = jnp.float32
    vmem = pl.BlockSpec(memory_space=pltpu.VMEM)
    return pl.pallas_call(
        functools.partial(rs_kernel, ring),
        out_shape=jax.ShapeDtypeStruct((quarters, tile_width, width), f32),
        in_specs=[vmem, vmem],
        out_specs=vmem,
        scratch_shapes=[
            pltpu.VMEM((quarters, half, tile_width, width), f32),
            pltpu.VMEM((quarters, steps, ring, tile_width, width), f32),
            pltpu.VMEM((quarters, steps - 1, ring, tile_width, width), f32),
            pltpu.VMEM((quarters, ring, tile_width, width), f32),
            pltpu.VMEM((quarters, steps, tile_width, width), f32),
            pltpu.VMEM((quarters, steps - 1, tile_width, width), f32),
            pltpu.SemaphoreType.DMA((quarters, steps)),
            pltpu.SemaphoreType.DMA((quarters, steps)),
            pltpu.SemaphoreType.DMA((quarters, steps)),
            pltpu.SemaphoreType.DMA((quarters, steps)),
        ],
        compiler_params=pltpu.CompilerParams(
            collective_id=0, has_side_effects=True, vmem_limit_bytes=VMEM_LIMIT
        ),
    )(part, core_part)


def on_device(grid_tiles, tile_rows, tile_cols, tile_owner, integrals):
    op_count = lax.axis_size("opair")
    vp_count = lax.axis_size("vpair")
    devices = op_count * vp_count
    slot_count, tile_width, _ = grid_tiles.shape
    owned = slot_count // 2
    capacity = slot_count // devices
    kc_local = integrals.shape[0] // tile_width
    int_table = jnp.swapaxes(integrals.reshape(kc_local, tile_width, integrals.shape[1]), 1, 2)
    live_slots = tile_owner >= 0
    target = jnp.where(live_slots, tile_owner // owned, devices)
    matches = (target[:, None] == jnp.arange(devices, dtype=jnp.int32)[None, :]).astype(jnp.int32)
    earlier = jnp.sum((jnp.cumsum(matches, axis=0) - matches) * matches, axis=1)
    placing = jnp.where(live_slots, target * capacity + earlier, devices * capacity)
    src = (
        jnp.full((devices * capacity + 1,), -1, jnp.int32)
        .at[placing]
        .set(jnp.arange(slot_count, dtype=jnp.int32))[: devices * capacity]
    )
    departing_tiles = gather_tiles(src, grid_tiles)
    label_rows = jnp.stack([tile_owner % owned, tile_rows % RT_OP, tile_cols % kc_local], axis=1)
    labels = jnp.where((src >= 0)[:, None], jnp.take(label_rows, jnp.maximum(src, 0), axis=0), -1)
    arrived = lax.all_to_all(labels, ("opair", "vpair"), split_axis=0, concat_axis=0, tiled=True)
    incoming = lax.all_to_all(
        departing_tiles, ("opair", "vpair"), split_axis=0, concat_axis=0, tiled=True
    )
    ring = 4
    side = lax.axis_index("vpair") % 2
    flat = jnp.transpose(arrived).reshape(-1)
    meta_sib = jnp.concatenate([flat, (1 - side)[None].astype(jnp.int32)])
    meta_own = jnp.concatenate([flat, side[None].astype(jnp.int32)])
    ov_tiles, part_sib = place_and_contract(
        meta_sib, incoming, int_table, owned, RT_OP, QUARTERS, ring, True
    )
    pairs = [(v, v ^ 1) for v in range(vp_count)]
    core_part = lax.ppermute(part_sib, "vpair", perm=pairs)
    (part_own,) = place_and_contract(
        meta_own, incoming, int_table, owned, RT_OP, QUARTERS, ring, False
    )
    cycle_t = reduce_scatter(part_own, core_part, ring)
    cycle_sum = jnp.transpose(cycle_t.reshape(-1, tile_width))
    return (ov_tiles, cycle_sum)


def solution(mesh):
    in_specs = (
        P(("opair", "vpair"), None, None),
        P(("opair", "vpair")),
        P(("opair", "vpair")),
        P(("opair", "vpair")),
        P("vpair", None),
    )
    out_specs = (P(("opair", "vpair"), None, None), P(("opair", "vpair"), None))
    return jax.shard_map(
        on_device, mesh=mesh, in_specs=in_specs, out_specs=out_specs, check_vma=False
    )
```

```python
import functools

import jax
import jax.numpy as jnp
from jax import lax
from jax.experimental import pallas as pl
from jax.experimental.pallas import tpu as pltpu
from jax.sharding import PartitionSpec as P

RT_OP = 32
QUARTERS = 4
MESH = pl.DeviceIdType.MESH
VMEM_LIMIT = 60 * 1024 * 1024


def exchange_kernel(devices, vp_count, capacity, src_ref, grid_ref, recv_ref, send_buf,
                    send_sems, recv_sems, local_sem):
    op = lax.axis_index("opair")
    me = op * vp_count + lax.axis_index("vpair")

    def peer(k):
        d = (me + k) % devices
        return d, (d // vp_count, d % vp_count)

    barrier = pltpu.get_barrier_semaphore()

    def greet(k, carry):
        _, where = peer(k)
        pl.semaphore_signal(barrier, inc=1, device_id=where, device_id_type=MESH)
        return carry

    lax.fori_loop(1, devices, greet, 0)

    def gather(j, carry):
        send_buf[j] = grid_ref[jnp.maximum(src_ref[j], 0)]
        return carry

    lax.fori_loop(0, send_buf.shape[0], gather, 0)
    pl.semaphore_wait(barrier, devices - 1)

    def copy_to(k):
        d, where = peer(k)
        return pltpu.make_async_remote_copy(
            src_ref=send_buf.at[pl.ds(d * capacity, capacity)],
            dst_ref=recv_ref.at[pl.ds(me * capacity, capacity)],
            send_sem=send_sems.at[k],
            recv_sem=recv_sems.at[k],
            device_id=where,
            device_id_type=MESH,
        )

    def start(k, carry):
        copy_to(k).start()
        return carry

    lax.fori_loop(1, devices, start, 0)
    local = pltpu.make_async_copy(
        send_buf.at[pl.ds(me * capacity, capacity)],
        recv_ref.at[pl.ds(me * capacity, capacity)],
        local_sem,
    )
    local.start()

    def finish(k, carry):
        copy_to(k).wait()
        return carry

    lax.fori_loop(1, devices, finish, 0)
    local.wait()


def exchange(src, grid_tiles, devices, vp_count, capacity):
    return pl.pallas_call(
        functools.partial(exchange_kernel, devices, vp_count, capacity),
        out_shape=jax.ShapeDtypeStruct(grid_tiles.shape, grid_tiles.dtype),
        in_specs=[
            pl.BlockSpec(memory_space=pltpu.SMEM),
            pl.BlockSpec(memory_space=pltpu.VMEM),
        ],
        out_specs=pl.BlockSpec(memory_space=pltpu.VMEM),
        scratch_shapes=[
            pltpu.VMEM(grid_tiles.shape, grid_tiles.dtype),
            pltpu.SemaphoreType.DMA((devices,)),
            pltpu.SemaphoreType.DMA((devices,)),
            pltpu.SemaphoreType.DMA(()),
        ],
        compiler_params=pltpu.CompilerParams(
            collective_id=1, has_side_effects=True, vmem_limit_bytes=VMEM_LIMIT
        ),
    )(src, grid_tiles)


def storage_row(q, row, ring):
    c = row % 2
    y = (row // 2) % ring
    z = row // (2 * ring)
    half = ring * ring
    if q < 2:
        return c * half + y * ring + z
    return c * half + z * ring + y


def place_kernel(quarters, ring, meta_ref, inc_ref, int_ref, ov_ref, part_ref):
    slots = inc_ref.shape[0]
    width = part_ref.shape[2]
    part_ref[...] = jnp.zeros(part_ref.shape, part_ref.dtype)

    def body(i, carry):
        pos = meta_ref[i]
        row = meta_ref[slots + i]
        col = meta_ref[2 * slots + i]

        @pl.when(pos >= 0)
        def _():
            tile = inc_ref[i]
            ov_ref[jnp.maximum(pos, 0)] = tile.T
            prod = jnp.dot(int_ref[jnp.maximum(col, 0)], tile, preferred_element_type=jnp.float32)
            for q in range(quarters):
                s = storage_row(q, jnp.maximum(row, 0), ring)
                part_ref[q, s] += prod[q * width : (q + 1) * width, :]

        return carry

    lax.fori_loop(0, slots, body, 0)


def place_and_contract(meta, incoming, int_table, owned, rows, quarters, ring):
    tile_width = incoming.shape[1]
    columns = int_table.shape[1]
    return pl.pallas_call(
        functools.partial(place_kernel, quarters, ring),
        out_shape=(
            jax.ShapeDtypeStruct((owned, tile_width, tile_width), incoming.dtype),
            jax.ShapeDtypeStruct((quarters, rows, columns // quarters, tile_width), jnp.float32),
        ),
        in_specs=[
            pl.BlockSpec(memory_space=pltpu.SMEM),
            pl.BlockSpec(memory_space=pltpu.VMEM),
            pl.BlockSpec(memory_space=pltpu.VMEM),
        ],
        out_specs=(
            pl.BlockSpec(memory_space=pltpu.VMEM),
            pl.BlockSpec(memory_space=pltpu.VMEM),
        ),
        compiler_params=pltpu.CompilerParams(vmem_limit_bytes=VMEM_LIMIT),
    )(meta, incoming, int_table)


def rs_kernel(ring, part_ref, out_ref, core_buf, red, rbuf1, acc1, fin1, rbuf2, acc2,
              core_send, core_recv, send1, recv1, send2, recv2):
    quarters, rows, tile_width, width = part_ref.shape
    half = rows // 2
    steps = ring - 1
    op = lax.axis_index("opair")
    v = lax.axis_index("vpair")
    c = v % 2
    y = (v // 2) % ring
    z = v // (2 * ring)

    def dev(zz, yy, cc):
        return (op, (zz * ring + yy) * 2 + cc)

    sib = dev(z, y, 1 - c)
    y_up = dev(z, (y + 1) % ring, c)
    y_dn = dev(z, (y + ring - 1) % ring, c)
    z_up = dev((z + 1) % ring, y, c)
    z_dn = dev((z + ring - 1) % ring, y, c)

    barrier = pltpu.get_barrier_semaphore()
    for peer in (sib, y_up, y_dn, z_up, z_dn):
        pl.semaphore_signal(barrier, inc=1, device_id=peer, device_id_type=MESH)
    pl.semaphore_wait(barrier, 5)

    core_copy = pltpu.make_async_remote_copy(
        src_ref=part_ref.at[:, pl.ds((1 - c) * half, half)],
        dst_ref=core_buf,
        send_sem=core_send,
        recv_sem=core_recv,
        device_id=sib,
        device_id_type=MESH,
    )
    core_copy.start()
    core_copy.wait()

    def core_sum(k, carry):
        q = k // half
        i = k % half
        red[q, i] = part_ref[q, c * half + i] + core_buf[q, i]
        return carry

    lax.fori_loop(0, quarters * half, core_sum, 0)

    def plan(q):
        d = 1 if q % 2 == 0 else -1
        if q < 2:
            return d, y, z, (y_up if d > 0 else y_dn), (z_up if d > 0 else z_dn)
        return d, z, y, (z_up if d > 0 else z_dn), (y_up if d > 0 else y_dn)

    for s in range(steps):
        copies = []
        for q in range(quarters):
            d, a, b, first, second = plan(q)
            blk = (a - d * (s + 1) + 2 * ring) % ring
            if s == 0:
                src = red.at[q, pl.ds(blk * ring, ring)]
            else:
                src = acc1.at[q, s - 1]
            cp = pltpu.make_async_remote_copy(
                src_ref=src,
                dst_ref=rbuf1.at[q, s],
                send_sem=send1.at[q, s],
                recv_sem=recv1.at[q, s],
                device_id=first,
                device_id_type=MESH,
            )
            cp.start()
            copies.append(cp)
        for q in range(quarters):
            copies[q].wait()
            d, a, b, first, second = plan(q)
            blk = (a - d * (s + 2) + 3 * ring) % ring
            for j in range(ring):
                total = rbuf1[q, s, j] + red[q, blk * ring + j]
                if s < steps - 1:
                    acc1[q, s, j] = total
                else:
                    fin1[q, j] = total

    for s in range(steps):
        copies = []
        for q in range(quarters):
            d, a, b, first, second = plan(q)
            blk = (b - d * (s + 1) + 2 * ring) % ring
            if s == 0:
                src = fin1.at[q, blk]
            else:
                src = acc2.at[q, s - 1]
            cp = pltpu.make_async_remote_copy(
                src_ref=src,
                dst_ref=rbuf2.at[q, s],
                send_sem=send2.at[q, s],
                recv_sem=recv2.at[q, s],
                device_id=second,
                device_id_type=MESH,
            )
            cp.start()
            copies.append(cp)
        for q in range(quarters):
            copies[q].wait()
            d, a, b, first, second = plan(q)
            blk = (b - d * (s + 2) + 3 * ring) % ring
            total = rbuf2[q, s] + fin1[q, blk]
            if s < steps - 1:
                acc2[q, s] = total
            else:
                out_ref[q] = total


def reduce_scatter(part, ring):
    quarters, rows, tile_width, width = part.shape
    half = rows // 2
    steps = ring - 1
    f32 = jnp.float32
    return pl.pallas_call(
        functools.partial(rs_kernel, ring),
        out_shape=jax.ShapeDtypeStruct((quarters, tile_width, width), f32),
        in_specs=[pl.BlockSpec(memory_space=pltpu.VMEM)],
        out_specs=pl.BlockSpec(memory_space=pltpu.VMEM),
        scratch_shapes=[
            pltpu.VMEM((quarters, half, tile_width, width), f32),
            pltpu.VMEM((quarters, half, tile_width, width), f32),
            pltpu.VMEM((quarters, steps, ring, tile_width, width), f32),
            pltpu.VMEM((quarters, steps - 1, ring, tile_width, width), f32),
            pltpu.VMEM((quarters, ring, tile_width, width), f32),
            pltpu.VMEM((quarters, steps, tile_width, width), f32),
            pltpu.VMEM((quarters, steps - 1, tile_width, width), f32),
            pltpu.SemaphoreType.DMA(()),
            pltpu.SemaphoreType.DMA(()),
            pltpu.SemaphoreType.DMA((quarters, steps)),
            pltpu.SemaphoreType.DMA((quarters, steps)),
            pltpu.SemaphoreType.DMA((quarters, steps)),
            pltpu.SemaphoreType.DMA((quarters, steps)),
        ],
        compiler_params=pltpu.CompilerParams(
            collective_id=0, has_side_effects=True, vmem_limit_bytes=VMEM_LIMIT
        ),
    )(part)


def on_device(grid_tiles, tile_rows, tile_cols, tile_owner, integrals):
    op_count = lax.axis_size("opair")
    vp_count = lax.axis_size("vpair")
    devices = op_count * vp_count
    slot_count, tile_width, _ = grid_tiles.shape
    owned = slot_count // 2
    capacity = slot_count // devices
    kc_local = integrals.shape[0] // tile_width
    int_table = jnp.swapaxes(integrals.reshape(kc_local, tile_width, integrals.shape[1]), 1, 2)
    live_slots = tile_owner >= 0
    target = jnp.where(live_slots, tile_owner // owned, devices)
    matches = (target[:, None] == jnp.arange(devices, dtype=jnp.int32)[None, :]).astype(jnp.int32)
    earlier = jnp.sum((jnp.cumsum(matches, axis=0) - matches) * matches, axis=1)
    placing = jnp.where(live_slots, target * capacity + earlier, devices * capacity)
    src = (
        jnp.full((devices * capacity + 1,), -1, jnp.int32)
        .at[placing]
        .set(jnp.arange(slot_count, dtype=jnp.int32))[: devices * capacity]
    )
    label_rows = jnp.stack([tile_owner % owned, tile_rows % RT_OP, tile_cols % kc_local], axis=1)
    labels = jnp.where((src >= 0)[:, None], jnp.take(label_rows, jnp.maximum(src, 0), axis=0), -1)
    arrived = lax.all_to_all(labels, ("opair", "vpair"), split_axis=0, concat_axis=0, tiled=True)
    incoming = exchange(src, grid_tiles, devices, vp_count, capacity)
    meta = jnp.transpose(arrived).reshape(-1)
    ring = 4
    ov_tiles, partial_value = place_and_contract(
        meta, incoming, int_table, owned, RT_OP, QUARTERS, ring
    )
    cycle_t = reduce_scatter(partial_value, ring)
    cycle_sum = jnp.transpose(cycle_t.reshape(-1, tile_width))
    return (ov_tiles, cycle_sum)


def solution(mesh):
    in_specs = (
        P(("opair", "vpair"), None, None),
        P(("opair", "vpair")),
        P(("opair", "vpair")),
        P(("opair", "vpair")),
        P("vpair", None),
    )
    out_specs = (P(("opair", "vpair"), None, None), P(("opair", "vpair"), None))
    return jax.shard_map(
        on_device, mesh=mesh, in_specs=in_specs, out_specs=out_specs, check_vma=False
    )
```

```python
import functools

import jax
import jax.numpy as jnp
from jax import lax
from jax.experimental import pallas as pl
from jax.experimental.pallas import tpu as pltpu
from jax.sharding import PartitionSpec as P

RT_OP = 32
QUARTERS = 4
MESH = pl.DeviceIdType.MESH
VMEM_LIMIT = 60 * 1024 * 1024


def gather_kernel(src_ref, grid_ref, out_ref):
    zero = jnp.zeros(out_ref.shape[1:], out_ref.dtype)

    def body(j, carry):
        s = src_ref[j]

        @pl.when(s >= 0)
        def _():
            out_ref[j] = grid_ref[jnp.maximum(s, 0)]

        @pl.when(s < 0)
        def _():
            out_ref[j] = zero

        return carry

    lax.fori_loop(0, out_ref.shape[0], body, 0)


def gather_tiles(src, grid_tiles):
    return pl.pallas_call(
        gather_kernel,
        out_shape=jax.ShapeDtypeStruct(grid_tiles.shape, grid_tiles.dtype),
        in_specs=[
            pl.BlockSpec(memory_space=pltpu.SMEM),
            pl.BlockSpec(memory_space=pltpu.VMEM),
        ],
        out_specs=pl.BlockSpec(memory_space=pltpu.VMEM),
        compiler_params=pltpu.CompilerParams(vmem_limit_bytes=VMEM_LIMIT),
    )(src, grid_tiles)


def storage_row(q, row, ring):
    c = row % 2
    y = (row // 2) % ring
    z = row // (2 * ring)
    half = ring * ring
    if q < 2:
        return c * half + y * ring + z
    return c * half + z * ring + y


def place_kernel(quarters, ring, meta_ref, inc_ref, int_ref, ov_ref, part_ref):
    slots = inc_ref.shape[0]
    width = part_ref.shape[2]
    part_ref[...] = jnp.zeros(part_ref.shape, part_ref.dtype)

    def body(i, carry):
        pos = meta_ref[i]
        row = meta_ref[slots + i]
        col = meta_ref[2 * slots + i]

        @pl.when(pos >= 0)
        def _():
            tile = inc_ref[i]
            ov_ref[jnp.maximum(pos, 0)] = tile.T
            for q in range(quarters):
                s = storage_row(q, jnp.maximum(row, 0), ring)
                block = int_ref[jnp.maximum(col, 0), pl.ds(q * width, width), :]
                part_ref[q, s] += jnp.dot(block, tile, preferred_element_type=jnp.float32)

        return carry

    lax.fori_loop(0, slots, body, 0)


def place_and_contract(meta, incoming, int_table, owned, rows, quarters, ring):
    tile_width = incoming.shape[1]
    columns = int_table.shape[1]
    return pl.pallas_call(
        functools.partial(place_kernel, quarters, ring),
        out_shape=(
            jax.ShapeDtypeStruct((owned, tile_width, tile_width), incoming.dtype),
            jax.ShapeDtypeStruct((quarters, rows, columns // quarters, tile_width), jnp.float32),
        ),
        in_specs=[
            pl.BlockSpec(memory_space=pltpu.SMEM),
            pl.BlockSpec(memory_space=pltpu.VMEM),
            pl.BlockSpec(memory_space=pltpu.VMEM),
        ],
        out_specs=(
            pl.BlockSpec(memory_space=pltpu.VMEM),
            pl.BlockSpec(memory_space=pltpu.VMEM),
        ),
        compiler_params=pltpu.CompilerParams(vmem_limit_bytes=VMEM_LIMIT),
    )(meta, incoming, int_table)


def rs_kernel(ring, part_ref, out_ref, core_buf, red, rbuf1, acc1, fin1, rbuf2, acc2,
              core_send, core_recv, send1, recv1, send2, recv2):
    quarters, rows, tile_width, width = part_ref.shape
    half = rows // 2
    steps = ring - 1
    op = lax.axis_index("opair")
    v = lax.axis_index("vpair")
    c = v % 2
    y = (v // 2) % ring
    z = v // (2 * ring)

    def dev(zz, yy, cc):
        return (op, (zz * ring + yy) * 2 + cc)

    sib = dev(z, y, 1 - c)
    y_up = dev(z, (y + 1) % ring, c)
    y_dn = dev(z, (y + ring - 1) % ring, c)
    z_up = dev((z + 1) % ring, y, c)
    z_dn = dev((z + ring - 1) % ring, y, c)

    barrier = pltpu.get_barrier_semaphore()
    for peer in (sib, y_up, y_dn, z_up, z_dn):
        pl.semaphore_signal(barrier, inc=1, device_id=peer, device_id_type=MESH)
    pl.semaphore_wait(barrier, 5)

    core_copy = pltpu.make_async_remote_copy(
        src_ref=part_ref.at[:, pl.ds((1 - c) * half, half)],
        dst_ref=core_buf,
        send_sem=core_send,
        recv_sem=core_recv,
        device_id=sib,
        device_id_type=MESH,
    )
    core_copy.start()
    core_copy.wait()

    def core_sum(k, carry):
        q = k // half
        i = k % half
        red[q, i] = part_ref[q, c * half + i] + core_buf[q, i]
        return carry

    lax.fori_loop(0, quarters * half, core_sum, 0)

    def plan(q):
        d = 1 if q % 2 == 0 else -1
        if q < 2:
            return d, y, z, (y_up if d > 0 else y_dn), (z_up if d > 0 else z_dn)
        return d, z, y, (z_up if d > 0 else z_dn), (y_up if d > 0 else y_dn)

    for s in range(steps):
        copies = []
        for q in range(quarters):
            d, a, b, first, second = plan(q)
            blk = (a - d * (s + 1) + 2 * ring) % ring
            if s == 0:
                src = red.at[q, pl.ds(blk * ring, ring)]
            else:
                src = acc1.at[q, s - 1]
            cp = pltpu.make_async_remote_copy(
                src_ref=src,
                dst_ref=rbuf1.at[q, s],
                send_sem=send1.at[q, s],
                recv_sem=recv1.at[q, s],
                device_id=first,
                device_id_type=MESH,
            )
            cp.start()
            copies.append(cp)
        for q in range(quarters):
            copies[q].wait()
            d, a, b, first, second = plan(q)
            blk = (a - d * (s + 2) + 3 * ring) % ring
            for j in range(ring):
                total = rbuf1[q, s, j] + red[q, blk * ring + j]
                if s < steps - 1:
                    acc1[q, s, j] = total
                else:
                    fin1[q, j] = total

    for s in range(steps):
        copies = []
        for q in range(quarters):
            d, a, b, first, second = plan(q)
            blk = (b - d * (s + 1) + 2 * ring) % ring
            if s == 0:
                src = fin1.at[q, blk]
            else:
                src = acc2.at[q, s - 1]
            cp = pltpu.make_async_remote_copy(
                src_ref=src,
                dst_ref=rbuf2.at[q, s],
                send_sem=send2.at[q, s],
                recv_sem=recv2.at[q, s],
                device_id=second,
                device_id_type=MESH,
            )
            cp.start()
            copies.append(cp)
        for q in range(quarters):
            copies[q].wait()
            d, a, b, first, second = plan(q)
            blk = (b - d * (s + 2) + 3 * ring) % ring
            total = rbuf2[q, s] + fin1[q, blk]
            if s < steps - 1:
                acc2[q, s] = total
            else:
                out_ref[q] = total


def reduce_scatter(part, ring):
    quarters, rows, tile_width, width = part.shape
    half = rows // 2
    steps = ring - 1
    f32 = jnp.float32
    return pl.pallas_call(
        functools.partial(rs_kernel, ring),
        out_shape=jax.ShapeDtypeStruct((quarters, tile_width, width), f32),
        in_specs=[pl.BlockSpec(memory_space=pltpu.VMEM)],
        out_specs=pl.BlockSpec(memory_space=pltpu.VMEM),
        scratch_shapes=[
            pltpu.VMEM((quarters, half, tile_width, width), f32),
            pltpu.VMEM((quarters, half, tile_width, width), f32),
            pltpu.VMEM((quarters, steps, ring, tile_width, width), f32),
            pltpu.VMEM((quarters, steps - 1, ring, tile_width, width), f32),
            pltpu.VMEM((quarters, ring, tile_width, width), f32),
            pltpu.VMEM((quarters, steps, tile_width, width), f32),
            pltpu.VMEM((quarters, steps - 1, tile_width, width), f32),
            pltpu.SemaphoreType.DMA(()),
            pltpu.SemaphoreType.DMA(()),
            pltpu.SemaphoreType.DMA((quarters, steps)),
            pltpu.SemaphoreType.DMA((quarters, steps)),
            pltpu.SemaphoreType.DMA((quarters, steps)),
            pltpu.SemaphoreType.DMA((quarters, steps)),
        ],
        compiler_params=pltpu.CompilerParams(
            collective_id=0, has_side_effects=True, vmem_limit_bytes=VMEM_LIMIT
        ),
    )(part)


def on_device(grid_tiles, tile_rows, tile_cols, tile_owner, integrals):
    op_count = lax.axis_size("opair")
    vp_count = lax.axis_size("vpair")
    devices = op_count * vp_count
    slot_count, tile_width, _ = grid_tiles.shape
    owned = slot_count // 2
    capacity = slot_count // devices
    kc_local = integrals.shape[0] // tile_width
    int_table = jnp.swapaxes(integrals.reshape(kc_local, tile_width, integrals.shape[1]), 1, 2)
    live_slots = tile_owner >= 0
    target = jnp.where(live_slots, tile_owner // owned, devices)
    matches = (target[:, None] == jnp.arange(devices, dtype=jnp.int32)[None, :]).astype(jnp.int32)
    earlier = jnp.sum((jnp.cumsum(matches, axis=0) - matches) * matches, axis=1)
    placing = jnp.where(live_slots, target * capacity + earlier, devices * capacity)
    src = (
        jnp.full((devices * capacity + 1,), -1, jnp.int32)
        .at[placing]
        .set(jnp.arange(slot_count, dtype=jnp.int32))[: devices * capacity]
    )
    departing_tiles = gather_tiles(src, grid_tiles)
    label_rows = jnp.stack([tile_owner % owned, tile_rows % RT_OP, tile_cols % kc_local], axis=1)
    labels = jnp.where((src >= 0)[:, None], jnp.take(label_rows, jnp.maximum(src, 0), axis=0), -1)
    arrived = lax.all_to_all(labels, ("opair", "vpair"), split_axis=0, concat_axis=0, tiled=True)
    incoming = lax.all_to_all(
        departing_tiles, ("opair", "vpair"), split_axis=0, concat_axis=0, tiled=True
    )
    meta = jnp.transpose(arrived).reshape(-1)
    ring = 4
    ov_tiles, partial_value = place_and_contract(
        meta, incoming, int_table, owned, RT_OP, QUARTERS, ring
    )
    cycle_t = reduce_scatter(partial_value, ring)
    cycle_sum = jnp.transpose(cycle_t.reshape(-1, tile_width))
    return (ov_tiles, cycle_sum)


def solution(mesh):
    in_specs = (
        P(("opair", "vpair"), None, None),
        P(("opair", "vpair")),
        P(("opair", "vpair")),
        P(("opair", "vpair")),
        P("vpair", None),
    )
    out_specs = (P(("opair", "vpair"), None, None), P(("opair", "vpair"), None))
    return jax.shard_map(
        on_device, mesh=mesh, in_specs=in_specs, out_specs=out_specs, check_vma=False
    )
```

```python
import functools

import jax
import jax.numpy as jnp
from jax import lax
from jax.experimental import pallas as pl
from jax.experimental.pallas import tpu as pltpu
from jax.sharding import PartitionSpec as P

RT_OP = 32
QUARTERS = 4
MESH = pl.DeviceIdType.MESH
VMEM_LIMIT = 60 * 1024 * 1024


def gather_kernel(src_ref, grid_ref, out_ref):
    zero = jnp.zeros(out_ref.shape[1:], out_ref.dtype)

    def body(j, carry):
        s = src_ref[j]

        @pl.when(s >= 0)
        def _():
            out_ref[j] = grid_ref[jnp.maximum(s, 0)]

        @pl.when(s < 0)
        def _():
            out_ref[j] = zero

        return carry

    lax.fori_loop(0, out_ref.shape[0], body, 0)


def gather_tiles(src, grid_tiles):
    return pl.pallas_call(
        gather_kernel,
        out_shape=jax.ShapeDtypeStruct(grid_tiles.shape, grid_tiles.dtype),
        in_specs=[
            pl.BlockSpec(memory_space=pltpu.SMEM),
            pl.BlockSpec(memory_space=pltpu.VMEM),
        ],
        out_specs=pl.BlockSpec(memory_space=pltpu.VMEM),
        compiler_params=pltpu.CompilerParams(vmem_limit_bytes=VMEM_LIMIT),
    )(src, grid_tiles)


def storage_row(q, row, ring):
    c = row % 2
    y = (row // 2) % ring
    z = row // (2 * ring)
    half = ring * ring
    if q < 2:
        return c * half + y * ring + z
    return c * half + z * ring + y


def place_kernel(quarters, ring, meta_ref, inc_ref, int_ref, ov_ref, part_ref):
    slots = inc_ref.shape[0]
    width = part_ref.shape[2]
    part_ref[...] = jnp.zeros(part_ref.shape, part_ref.dtype)

    def body(i, carry):
        pos = meta_ref[i]
        row = meta_ref[slots + i]
        col = meta_ref[2 * slots + i]

        @pl.when(pos >= 0)
        def _():
            tile = inc_ref[i]
            ov_ref[jnp.maximum(pos, 0)] = tile.T
            for q in range(quarters):
                s = storage_row(q, jnp.maximum(row, 0), ring)
                block = int_ref[jnp.maximum(col, 0), pl.ds(q * width, width), :]
                part_ref[q, s] += jnp.dot(block, tile, preferred_element_type=jnp.float32)

        return carry

    lax.fori_loop(0, slots, body, 0)


def place_and_contract(meta, incoming, int_table, owned, rows, quarters, ring):
    tile_width = incoming.shape[1]
    columns = int_table.shape[1]
    return pl.pallas_call(
        functools.partial(place_kernel, quarters, ring),
        out_shape=(
            jax.ShapeDtypeStruct((owned, tile_width, tile_width), incoming.dtype),
            jax.ShapeDtypeStruct((quarters, rows, columns // quarters, tile_width), jnp.float32),
        ),
        in_specs=[
            pl.BlockSpec(memory_space=pltpu.SMEM),
            pl.BlockSpec(memory_space=pltpu.VMEM),
            pl.BlockSpec(memory_space=pltpu.VMEM),
        ],
        out_specs=(
            pl.BlockSpec(memory_space=pltpu.VMEM),
            pl.BlockSpec(memory_space=pltpu.VMEM),
        ),
        compiler_params=pltpu.CompilerParams(vmem_limit_bytes=VMEM_LIMIT),
    )(meta, incoming, int_table)


def rs_kernel(ring, part_ref, out_ref, core_buf, red, rbuf1, acc1, fin1, rbuf2, acc2,
              core_send, core_recv, send1, recv1, send2, recv2):
    quarters, rows, tile_width, width = part_ref.shape
    half = rows // 2
    steps = ring - 1
    op = lax.axis_index("opair")
    v = lax.axis_index("vpair")
    c = v % 2
    y = (v // 2) % ring
    z = v // (2 * ring)

    def dev(zz, yy, cc):
        return (op, (zz * ring + yy) * 2 + cc)

    sib = dev(z, y, 1 - c)
    y_up = dev(z, (y + 1) % ring, c)
    y_dn = dev(z, (y + ring - 1) % ring, c)
    z_up = dev((z + 1) % ring, y, c)
    z_dn = dev((z + ring - 1) % ring, y, c)

    barrier = pltpu.get_barrier_semaphore()
    for peer in (sib, y_up, y_dn, z_up, z_dn):
        pl.semaphore_signal(barrier, inc=1, device_id=peer, device_id_type=MESH)
    pl.semaphore_wait(barrier, 5)

    def plan(q):
        d = 1 if q % 2 == 0 else -1
        if q < 2:
            return d, y, z, (y_up if d > 0 else y_dn), (z_up if d > 0 else z_dn)
        return d, z, y, (z_up if d > 0 else z_dn), (y_up if d > 0 else y_dn)

    def core_copy(q):
        return pltpu.make_async_remote_copy(
            src_ref=part_ref.at[q, pl.ds((1 - c) * half, half)],
            dst_ref=core_buf.at[q],
            send_sem=core_send.at[q],
            recv_sem=core_recv.at[q],
            device_id=sib,
            device_id_type=MESH,
        )

    def first_copy(q, s):
        d, a, b, first, second = plan(q)
        if s == 0:
            blk = (a - d + 2 * ring) % ring
            src = red.at[q, pl.ds(blk * ring, ring)]
        else:
            src = acc1.at[q, s - 1]
        return pltpu.make_async_remote_copy(
            src_ref=src,
            dst_ref=rbuf1.at[q, s],
            send_sem=send1.at[q, s],
            recv_sem=recv1.at[q, s],
            device_id=first,
            device_id_type=MESH,
        )

    def second_copy(q, s):
        d, a, b, first, second = plan(q)
        if s == 0:
            src = fin1.at[q, (b - d + 2 * ring) % ring]
        else:
            src = acc2.at[q, s - 1]
        return pltpu.make_async_remote_copy(
            src_ref=src,
            dst_ref=rbuf2.at[q, s],
            send_sem=send2.at[q, s],
            recv_sem=recv2.at[q, s],
            device_id=second,
            device_id_type=MESH,
        )

    for q in range(quarters):
        core_copy(q).start()

    for q in range(quarters):
        core_copy(q).wait()

        def core_sum(i, carry):
            red[q, i] = part_ref[q, c * half + i] + core_buf[q, i]
            return carry

        lax.fori_loop(0, half, core_sum, 0)
        first_copy(q, 0).start()

    for s in range(steps):
        for q in range(quarters):
            first_copy(q, s).wait()
            d, a, b, first, second = plan(q)
            blk = (a - d * (s + 2) + 3 * ring) % ring
            for j in range(ring):
                total = rbuf1[q, s, j] + red[q, blk * ring + j]
                if s < steps - 1:
                    acc1[q, s, j] = total
                else:
                    fin1[q, j] = total
            if s < steps - 1:
                first_copy(q, s + 1).start()
            else:
                second_copy(q, 0).start()

    for s in range(steps):
        for q in range(quarters):
            second_copy(q, s).wait()
            d, a, b, first, second = plan(q)
            blk = (b - d * (s + 2) + 3 * ring) % ring
            total = rbuf2[q, s] + fin1[q, blk]
            if s < steps - 1:
                acc2[q, s] = total
                second_copy(q, s + 1).start()
            else:
                out_ref[q] = total


def reduce_scatter(part, ring):
    quarters, rows, tile_width, width = part.shape
    half = rows // 2
    steps = ring - 1
    f32 = jnp.float32
    return pl.pallas_call(
        functools.partial(rs_kernel, ring),
        out_shape=jax.ShapeDtypeStruct((quarters, tile_width, width), f32),
        in_specs=[pl.BlockSpec(memory_space=pltpu.VMEM)],
        out_specs=pl.BlockSpec(memory_space=pltpu.VMEM),
        scratch_shapes=[
            pltpu.VMEM((quarters, half, tile_width, width), f32),
            pltpu.VMEM((quarters, half, tile_width, width), f32),
            pltpu.VMEM((quarters, steps, ring, tile_width, width), f32),
            pltpu.VMEM((quarters, steps - 1, ring, tile_width, width), f32),
            pltpu.VMEM((quarters, ring, tile_width, width), f32),
            pltpu.VMEM((quarters, steps, tile_width, width), f32),
            pltpu.VMEM((quarters, steps - 1, tile_width, width), f32),
            pltpu.SemaphoreType.DMA((quarters,)),
            pltpu.SemaphoreType.DMA((quarters,)),
            pltpu.SemaphoreType.DMA((quarters, steps)),
            pltpu.SemaphoreType.DMA((quarters, steps)),
            pltpu.SemaphoreType.DMA((quarters, steps)),
            pltpu.SemaphoreType.DMA((quarters, steps)),
        ],
        compiler_params=pltpu.CompilerParams(
            collective_id=0, has_side_effects=True, vmem_limit_bytes=VMEM_LIMIT
        ),
    )(part)


def on_device(grid_tiles, tile_rows, tile_cols, tile_owner, integrals):
    op_count = lax.axis_size("opair")
    vp_count = lax.axis_size("vpair")
    devices = op_count * vp_count
    slot_count, tile_width, _ = grid_tiles.shape
    owned = slot_count // 2
    capacity = slot_count // devices
    kc_local = integrals.shape[0] // tile_width
    int_table = jnp.swapaxes(integrals.reshape(kc_local, tile_width, integrals.shape[1]), 1, 2)
    live_slots = tile_owner >= 0
    target = jnp.where(live_slots, tile_owner // owned, devices)
    matches = (target[:, None] == jnp.arange(devices, dtype=jnp.int32)[None, :]).astype(jnp.int32)
    earlier = jnp.sum((jnp.cumsum(matches, axis=0) - matches) * matches, axis=1)
    placing = jnp.where(live_slots, target * capacity + earlier, devices * capacity)
    src = (
        jnp.full((devices * capacity + 1,), -1, jnp.int32)
        .at[placing]
        .set(jnp.arange(slot_count, dtype=jnp.int32))[: devices * capacity]
    )
    departing_tiles = gather_tiles(src, grid_tiles)
    label_rows = jnp.stack([tile_owner % owned, tile_rows % RT_OP, tile_cols % kc_local], axis=1)
    labels = jnp.where((src >= 0)[:, None], jnp.take(label_rows, jnp.maximum(src, 0), axis=0), -1)
    arrived = lax.all_to_all(labels, ("opair", "vpair"), split_axis=0, concat_axis=0, tiled=True)
    incoming = lax.all_to_all(
        departing_tiles, ("opair", "vpair"), split_axis=0, concat_axis=0, tiled=True
    )
    meta = jnp.transpose(arrived).reshape(-1)
    ring = 4
    ov_tiles, partial_value = place_and_contract(
        meta, incoming, int_table, owned, RT_OP, QUARTERS, ring
    )
    cycle_t = reduce_scatter(partial_value, ring)
    cycle_sum = jnp.transpose(cycle_t.reshape(-1, tile_width))
    return (ov_tiles, cycle_sum)


def solution(mesh):
    in_specs = (
        P(("opair", "vpair"), None, None),
        P(("opair", "vpair")),
        P(("opair", "vpair")),
        P(("opair", "vpair")),
        P("vpair", None),
    )
    out_specs = (P(("opair", "vpair"), None, None), P(("opair", "vpair"), None))
    return jax.shard_map(
        on_device, mesh=mesh, in_specs=in_specs, out_specs=out_specs, check_vma=False
    )
```

```python
import functools

import jax
import jax.numpy as jnp
from jax import lax
from jax.experimental import pallas as pl
from jax.experimental.pallas import tpu as pltpu
from jax.sharding import PartitionSpec as P

RT_OP = 32
QUARTERS = 4
MESH = pl.DeviceIdType.MESH
VMEM_LIMIT = 60 * 1024 * 1024


def gather_kernel(src_ref, grid_ref, out_ref):
    zero = jnp.zeros(out_ref.shape[1:], out_ref.dtype)

    def body(j, carry):
        s = src_ref[j]

        @pl.when(s >= 0)
        def _():
            out_ref[j] = grid_ref[jnp.maximum(s, 0)]

        @pl.when(s < 0)
        def _():
            out_ref[j] = zero

        return carry

    lax.fori_loop(0, out_ref.shape[0], body, 0)


def gather_tiles(src, grid_tiles):
    return pl.pallas_call(
        gather_kernel,
        out_shape=jax.ShapeDtypeStruct(grid_tiles.shape, grid_tiles.dtype),
        in_specs=[
            pl.BlockSpec(memory_space=pltpu.SMEM),
            pl.BlockSpec(memory_space=pltpu.VMEM),
        ],
        out_specs=pl.BlockSpec(memory_space=pltpu.VMEM),
        compiler_params=pltpu.CompilerParams(vmem_limit_bytes=VMEM_LIMIT),
    )(src, grid_tiles)


def storage_row(q, row, ring):
    c = row % 2
    y = (row // 2) % ring
    z = row // (2 * ring)
    half = ring * ring
    if q < 2:
        return c * half + y * ring + z
    return c * half + z * ring + y


def place_kernel(quarters, ring, meta_ref, inc_ref, int_ref, ov_ref, part_ref):
    slots = inc_ref.shape[0]
    width = part_ref.shape[2]
    rows = part_ref.shape[1]
    zero = jnp.zeros(part_ref.shape[2:], part_ref.dtype)

    def clear(r, carry):
        @pl.when(meta_ref[4 * slots + r] > 0)
        def _():
            for q in range(quarters):
                part_ref[q, storage_row(q, r, ring)] = zero

        return carry

    lax.fori_loop(0, rows, clear, 0)

    def body(i, carry):
        pos = meta_ref[i]
        row = meta_ref[slots + i]
        col = meta_ref[2 * slots + i]

        @pl.when(pos >= 0)
        def _():
            tile = inc_ref[i]
            ov_ref[jnp.maximum(pos, 0)] = tile.T
            first = meta_ref[3 * slots + i] > 0
            for q in range(quarters):
                s = storage_row(q, jnp.maximum(row, 0), ring)
                block = int_ref[jnp.maximum(col, 0), pl.ds(q * width, width), :]
                prod = jnp.dot(block, tile, preferred_element_type=jnp.float32)

                @pl.when(first)
                def _():
                    part_ref[q, s] = prod

                @pl.when(jnp.logical_not(first))
                def _():
                    part_ref[q, s] += prod

        return carry

    lax.fori_loop(0, slots, body, 0)


def place_and_contract(meta, incoming, int_table, owned, rows, quarters, ring):
    tile_width = incoming.shape[1]
    columns = int_table.shape[1]
    return pl.pallas_call(
        functools.partial(place_kernel, quarters, ring),
        out_shape=(
            jax.ShapeDtypeStruct((owned, tile_width, tile_width), incoming.dtype),
            jax.ShapeDtypeStruct((quarters, rows, columns // quarters, tile_width), jnp.float32),
        ),
        in_specs=[
            pl.BlockSpec(memory_space=pltpu.SMEM),
            pl.BlockSpec(memory_space=pltpu.VMEM),
            pl.BlockSpec(memory_space=pltpu.VMEM),
        ],
        out_specs=(
            pl.BlockSpec(memory_space=pltpu.VMEM),
            pl.BlockSpec(memory_space=pltpu.VMEM),
        ),
        compiler_params=pltpu.CompilerParams(vmem_limit_bytes=VMEM_LIMIT),
    )(meta, incoming, int_table)


def rs_kernel(ring, part_ref, out_ref, core_buf, red, rbuf1, acc1, fin1, rbuf2, acc2,
              core_send, core_recv, send1, recv1, send2, recv2):
    quarters, rows, tile_width, width = part_ref.shape
    half = rows // 2
    steps = ring - 1
    op = lax.axis_index("opair")
    v = lax.axis_index("vpair")
    c = v % 2
    y = (v // 2) % ring
    z = v // (2 * ring)

    def dev(zz, yy, cc):
        return (op, (zz * ring + yy) * 2 + cc)

    sib = dev(z, y, 1 - c)
    y_up = dev(z, (y + 1) % ring, c)
    y_dn = dev(z, (y + ring - 1) % ring, c)
    z_up = dev((z + 1) % ring, y, c)
    z_dn = dev((z + ring - 1) % ring, y, c)

    barrier = pltpu.get_barrier_semaphore()
    for peer in (sib, y_up, y_dn, z_up, z_dn):
        pl.semaphore_signal(barrier, inc=1, device_id=peer, device_id_type=MESH)
    pl.semaphore_wait(barrier, 5)

    def plan(q):
        d = 1 if q % 2 == 0 else -1
        if q < 2:
            return d, y, z, (y_up if d > 0 else y_dn), (z_up if d > 0 else z_dn)
        return d, z, y, (z_up if d > 0 else z_dn), (y_up if d > 0 else y_dn)

    def core_copy(q):
        return pltpu.make_async_remote_copy(
            src_ref=part_ref.at[q, pl.ds((1 - c) * half, half)],
            dst_ref=core_buf.at[q],
            send_sem=core_send.at[q],
            recv_sem=core_recv.at[q],
            device_id=sib,
            device_id_type=MESH,
        )

    def first_copy(q, s):
        d, a, b, first, second = plan(q)
        if s == 0:
            blk = (a - d + 2 * ring) % ring
            src = red.at[q, pl.ds(blk * ring, ring)]
        else:
            src = acc1.at[q, s - 1]
        return pltpu.make_async_remote_copy(
            src_ref=src,
            dst_ref=rbuf1.at[q, s],
            send_sem=send1.at[q, s],
            recv_sem=recv1.at[q, s],
            device_id=first,
            device_id_type=MESH,
        )

    def second_copy(q, s):
        d, a, b, first, second = plan(q)
        if s == 0:
            src = fin1.at[q, (b - d + 2 * ring) % ring]
        else:
            src = acc2.at[q, s - 1]
        return pltpu.make_async_remote_copy(
            src_ref=src,
            dst_ref=rbuf2.at[q, s],
            send_sem=send2.at[q, s],
            recv_sem=recv2.at[q, s],
            device_id=second,
            device_id_type=MESH,
        )

    for q in range(quarters):
        core_copy(q).start()

    for q in range(quarters):
        core_copy(q).wait()

        def core_sum(i, carry):
            red[q, i] = part_ref[q, c * half + i] + core_buf[q, i]
            return carry

        lax.fori_loop(0, half, core_sum, 0)
        first_copy(q, 0).start()

    for s in range(steps):
        for q in range(quarters):
            first_copy(q, s).wait()
            d, a, b, first, second = plan(q)
            blk = (a - d * (s + 2) + 3 * ring) % ring
            for j in range(ring):
                total = rbuf1[q, s, j] + red[q, blk * ring + j]
                if s < steps - 1:
                    acc1[q, s, j] = total
                else:
                    fin1[q, j] = total
            if s < steps - 1:
                first_copy(q, s + 1).start()
            else:
                second_copy(q, 0).start()

    for s in range(steps):
        for q in range(quarters):
            second_copy(q, s).wait()
            d, a, b, first, second = plan(q)
            blk = (b - d * (s + 2) + 3 * ring) % ring
            total = rbuf2[q, s] + fin1[q, blk]
            if s < steps - 1:
                acc2[q, s] = total
                second_copy(q, s + 1).start()
            else:
                out_ref[q] = total


def reduce_scatter(part, ring):
    quarters, rows, tile_width, width = part.shape
    half = rows // 2
    steps = ring - 1
    f32 = jnp.float32
    return pl.pallas_call(
        functools.partial(rs_kernel, ring),
        out_shape=jax.ShapeDtypeStruct((quarters, tile_width, width), f32),
        in_specs=[pl.BlockSpec(memory_space=pltpu.VMEM)],
        out_specs=pl.BlockSpec(memory_space=pltpu.VMEM),
        scratch_shapes=[
            pltpu.VMEM((quarters, half, tile_width, width), f32),
            pltpu.VMEM((quarters, half, tile_width, width), f32),
            pltpu.VMEM((quarters, steps, ring, tile_width, width), f32),
            pltpu.VMEM((quarters, steps - 1, ring, tile_width, width), f32),
            pltpu.VMEM((quarters, ring, tile_width, width), f32),
            pltpu.VMEM((quarters, steps, tile_width, width), f32),
            pltpu.VMEM((quarters, steps - 1, tile_width, width), f32),
            pltpu.SemaphoreType.DMA((quarters,)),
            pltpu.SemaphoreType.DMA((quarters,)),
            pltpu.SemaphoreType.DMA((quarters, steps)),
            pltpu.SemaphoreType.DMA((quarters, steps)),
            pltpu.SemaphoreType.DMA((quarters, steps)),
            pltpu.SemaphoreType.DMA((quarters, steps)),
        ],
        compiler_params=pltpu.CompilerParams(
            collective_id=0, has_side_effects=True, vmem_limit_bytes=VMEM_LIMIT
        ),
    )(part)


def on_device(grid_tiles, tile_rows, tile_cols, tile_owner, integrals):
    op_count = lax.axis_size("opair")
    vp_count = lax.axis_size("vpair")
    devices = op_count * vp_count
    slot_count, tile_width, _ = grid_tiles.shape
    owned = slot_count // 2
    capacity = slot_count // devices
    kc_local = integrals.shape[0] // tile_width
    int_table = jnp.swapaxes(integrals.reshape(kc_local, tile_width, integrals.shape[1]), 1, 2)
    live_slots = tile_owner >= 0
    target = jnp.where(live_slots, tile_owner // owned, devices)
    matches = (target[:, None] == jnp.arange(devices, dtype=jnp.int32)[None, :]).astype(jnp.int32)
    earlier = jnp.sum((jnp.cumsum(matches, axis=0) - matches) * matches, axis=1)
    placing = jnp.where(live_slots, target * capacity + earlier, devices * capacity)
    src = (
        jnp.full((devices * capacity + 1,), -1, jnp.int32)
        .at[placing]
        .set(jnp.arange(slot_count, dtype=jnp.int32))[: devices * capacity]
    )
    departing_tiles = gather_tiles(src, grid_tiles)
    label_rows = jnp.stack([tile_owner % owned, tile_rows % RT_OP, tile_cols % kc_local], axis=1)
    labels = jnp.where((src >= 0)[:, None], jnp.take(label_rows, jnp.maximum(src, 0), axis=0), -1)
    arrived = lax.all_to_all(labels, ("opair", "vpair"), split_axis=0, concat_axis=0, tiled=True)
    incoming = lax.all_to_all(
        departing_tiles, ("opair", "vpair"), split_axis=0, concat_axis=0, tiled=True
    )
    valid = arrived[:, 0] >= 0
    row_in = arrived[:, 1]
    slot_ids = jnp.arange(slot_count, dtype=jnp.int32)
    earlier_same = (row_in[None, :] == row_in[:, None]) & valid[None, :] & (slot_ids[None, :] < slot_ids[:, None])
    first = (valid & ~jnp.any(earlier_same, axis=1)).astype(jnp.int32)
    row_ids = jnp.arange(RT_OP, dtype=jnp.int32)
    empty = (~jnp.any((row_in[None, :] == row_ids[:, None]) & valid[None, :], axis=1)).astype(jnp.int32)
    meta = jnp.concatenate([jnp.transpose(arrived).reshape(-1), first, empty])
    ring = 4
    ov_tiles, partial_value = place_and_contract(
        meta, incoming, int_table, owned, RT_OP, QUARTERS, ring
    )
    cycle_t = reduce_scatter(partial_value, ring)
    cycle_sum = jnp.transpose(cycle_t.reshape(-1, tile_width))
    return (ov_tiles, cycle_sum)


def solution(mesh):
    in_specs = (
        P(("opair", "vpair"), None, None),
        P(("opair", "vpair")),
        P(("opair", "vpair")),
        P(("opair", "vpair")),
        P("vpair", None),
    )
    out_specs = (P(("opair", "vpair"), None, None), P(("opair", "vpair"), None))
    return jax.shard_map(
        on_device, mesh=mesh, in_specs=in_specs, out_specs=out_specs, check_vma=False
    )
```

```python
import functools

import jax
import jax.numpy as jnp
from jax import lax
from jax.experimental import pallas as pl
from jax.experimental.pallas import tpu as pltpu
from jax.sharding import PartitionSpec as P

RT_OP = 32
QUARTERS = 8
MESH = pl.DeviceIdType.MESH
VMEM_LIMIT = 60 * 1024 * 1024


def gather_kernel(src_ref, grid_ref, out_ref):
    zero = jnp.zeros(out_ref.shape[1:], out_ref.dtype)

    def body(j, carry):
        s = src_ref[j]

        @pl.when(s >= 0)
        def _():
            out_ref[j] = grid_ref[jnp.maximum(s, 0)]

        @pl.when(s < 0)
        def _():
            out_ref[j] = zero

        return carry

    lax.fori_loop(0, out_ref.shape[0], body, 0)


def gather_tiles(src, grid_tiles):
    return pl.pallas_call(
        gather_kernel,
        out_shape=jax.ShapeDtypeStruct(grid_tiles.shape, grid_tiles.dtype),
        in_specs=[
            pl.BlockSpec(memory_space=pltpu.SMEM),
            pl.BlockSpec(memory_space=pltpu.VMEM),
        ],
        out_specs=pl.BlockSpec(memory_space=pltpu.VMEM),
        compiler_params=pltpu.CompilerParams(vmem_limit_bytes=VMEM_LIMIT),
    )(src, grid_tiles)


def storage_row(q, row, ring):
    c = row % 2
    y = (row // 2) % ring
    z = row // (2 * ring)
    half = ring * ring
    if q < QUARTERS // 2:
        return c * half + y * ring + z
    return c * half + z * ring + y


def place_kernel(quarters, ring, meta_ref, inc_ref, int_ref, ov_ref, part_ref):
    slots = inc_ref.shape[0]
    width = part_ref.shape[2]
    part_ref[...] = jnp.zeros(part_ref.shape, part_ref.dtype)

    def body(i, carry):
        pos = meta_ref[i]
        row = meta_ref[slots + i]
        col = meta_ref[2 * slots + i]

        @pl.when(pos >= 0)
        def _():
            tile = inc_ref[i]
            ov_ref[jnp.maximum(pos, 0)] = tile.T
            for q in range(quarters // 2):
                block = int_ref[jnp.maximum(col, 0), pl.ds(2 * q * width, 2 * width), :]
                prod = jnp.dot(block, tile, preferred_element_type=jnp.float32)
                for h in range(2):
                    k = 2 * q + h
                    s = storage_row(k, jnp.maximum(row, 0), ring)
                    part_ref[k, s] += prod[h * width : (h + 1) * width, :]

        return carry

    lax.fori_loop(0, slots, body, 0)


def place_and_contract(meta, incoming, int_table, owned, rows, quarters, ring):
    tile_width = incoming.shape[1]
    columns = int_table.shape[1]
    return pl.pallas_call(
        functools.partial(place_kernel, quarters, ring),
        out_shape=(
            jax.ShapeDtypeStruct((owned, tile_width, tile_width), incoming.dtype),
            jax.ShapeDtypeStruct((quarters, rows, columns // quarters, tile_width), jnp.float32),
        ),
        in_specs=[
            pl.BlockSpec(memory_space=pltpu.SMEM),
            pl.BlockSpec(memory_space=pltpu.VMEM),
            pl.BlockSpec(memory_space=pltpu.VMEM),
        ],
        out_specs=(
            pl.BlockSpec(memory_space=pltpu.VMEM),
            pl.BlockSpec(memory_space=pltpu.VMEM),
        ),
        compiler_params=pltpu.CompilerParams(vmem_limit_bytes=VMEM_LIMIT),
    )(meta, incoming, int_table)


def rs_kernel(ring, part_ref, out_ref, core_buf, red, rbuf1, acc1, fin1, rbuf2, acc2,
              core_send, core_recv, send1, recv1, send2, recv2):
    quarters, rows, tile_width, width = part_ref.shape
    half = rows // 2
    steps = ring - 1
    op = lax.axis_index("opair")
    v = lax.axis_index("vpair")
    c = v % 2
    y = (v // 2) % ring
    z = v // (2 * ring)

    def dev(zz, yy, cc):
        return (op, (zz * ring + yy) * 2 + cc)

    sib = dev(z, y, 1 - c)
    y_up = dev(z, (y + 1) % ring, c)
    y_dn = dev(z, (y + ring - 1) % ring, c)
    z_up = dev((z + 1) % ring, y, c)
    z_dn = dev((z + ring - 1) % ring, y, c)

    barrier = pltpu.get_barrier_semaphore()
    for peer in (sib, y_up, y_dn, z_up, z_dn):
        pl.semaphore_signal(barrier, inc=1, device_id=peer, device_id_type=MESH)
    pl.semaphore_wait(barrier, 5)

    def plan(q):
        d = 1 if q % 2 == 0 else -1
        if q < quarters // 2:
            return d, y, z, (y_up if d > 0 else y_dn), (z_up if d > 0 else z_dn)
        return d, z, y, (z_up if d > 0 else z_dn), (y_up if d > 0 else y_dn)

    def core_copy(q):
        return pltpu.make_async_remote_copy(
            src_ref=part_ref.at[q, pl.ds((1 - c) * half, half)],
            dst_ref=core_buf.at[q],
            send_sem=core_send.at[q],
            recv_sem=core_recv.at[q],
            device_id=sib,
            device_id_type=MESH,
        )

    def first_copy(q, s):
        d, a, b, first, second = plan(q)
        if s == 0:
            blk = (a - d + 2 * ring) % ring
            src = red.at[q, pl.ds(blk * ring, ring)]
        else:
            src = acc1.at[q, s - 1]
        return pltpu.make_async_remote_copy(
            src_ref=src,
            dst_ref=rbuf1.at[q, s],
            send_sem=send1.at[q, s],
            recv_sem=recv1.at[q, s],
            device_id=first,
            device_id_type=MESH,
        )

    def second_copy(q, s):
        d, a, b, first, second = plan(q)
        if s == 0:
            src = fin1.at[q, (b - d + 2 * ring) % ring]
        else:
            src = acc2.at[q, s - 1]
        return pltpu.make_async_remote_copy(
            src_ref=src,
            dst_ref=rbuf2.at[q, s],
            send_sem=send2.at[q, s],
            recv_sem=recv2.at[q, s],
            device_id=second,
            device_id_type=MESH,
        )

    for q in range(quarters):
        core_copy(q).start()

    for q in range(quarters):
        core_copy(q).wait()

        def core_sum(i, carry):
            red[q, i] = part_ref[q, c * half + i] + core_buf[q, i]
            return carry

        lax.fori_loop(0, half, core_sum, 0)
        first_copy(q, 0).start()

    for s in range(steps):
        for q in range(quarters):
            first_copy(q, s).wait()
            d, a, b, first, second = plan(q)
            blk = (a - d * (s + 2) + 3 * ring) % ring
            for j in range(ring):
                total = rbuf1[q, s, j] + red[q, blk * ring + j]
                if s < steps - 1:
                    acc1[q, s, j] = total
                else:
                    fin1[q, j] = total
            if s < steps - 1:
                first_copy(q, s + 1).start()
            else:
                second_copy(q, 0).start()

    for s in range(steps):
        for q in range(quarters):
            second_copy(q, s).wait()
            d, a, b, first, second = plan(q)
            blk = (b - d * (s + 2) + 3 * ring) % ring
            total = rbuf2[q, s] + fin1[q, blk]
            if s < steps - 1:
                acc2[q, s] = total
                second_copy(q, s + 1).start()
            else:
                out_ref[q] = total


def reduce_scatter(part, ring):
    quarters, rows, tile_width, width = part.shape
    half = rows // 2
    steps = ring - 1
    f32 = jnp.float32
    return pl.pallas_call(
        functools.partial(rs_kernel, ring),
        out_shape=jax.ShapeDtypeStruct((quarters, tile_width, width), f32),
        in_specs=[pl.BlockSpec(memory_space=pltpu.VMEM)],
        out_specs=pl.BlockSpec(memory_space=pltpu.VMEM),
        scratch_shapes=[
            pltpu.VMEM((quarters, half, tile_width, width), f32),
            pltpu.VMEM((quarters, half, tile_width, width), f32),
            pltpu.VMEM((quarters, steps, ring, tile_width, width), f32),
            pltpu.VMEM((quarters, steps - 1, ring, tile_width, width), f32),
            pltpu.VMEM((quarters, ring, tile_width, width), f32),
            pltpu.VMEM((quarters, steps, tile_width, width), f32),
            pltpu.VMEM((quarters, steps - 1, tile_width, width), f32),
            pltpu.SemaphoreType.DMA((quarters,)),
            pltpu.SemaphoreType.DMA((quarters,)),
            pltpu.SemaphoreType.DMA((quarters, steps)),
            pltpu.SemaphoreType.DMA((quarters, steps)),
            pltpu.SemaphoreType.DMA((quarters, steps)),
            pltpu.SemaphoreType.DMA((quarters, steps)),
        ],
        compiler_params=pltpu.CompilerParams(
            collective_id=0, has_side_effects=True, vmem_limit_bytes=VMEM_LIMIT
        ),
    )(part)


def on_device(grid_tiles, tile_rows, tile_cols, tile_owner, integrals):
    op_count = lax.axis_size("opair")
    vp_count = lax.axis_size("vpair")
    devices = op_count * vp_count
    slot_count, tile_width, _ = grid_tiles.shape
    owned = slot_count // 2
    capacity = slot_count // devices
    kc_local = integrals.shape[0] // tile_width
    int_table = jnp.swapaxes(integrals.reshape(kc_local, tile_width, integrals.shape[1]), 1, 2)
    live_slots = tile_owner >= 0
    target = jnp.where(live_slots, tile_owner // owned, devices)
    matches = (target[:, None] == jnp.arange(devices, dtype=jnp.int32)[None, :]).astype(jnp.int32)
    earlier = jnp.sum((jnp.cumsum(matches, axis=0) - matches) * matches, axis=1)
    placing = jnp.where(live_slots, target * capacity + earlier, devices * capacity)
    src = (
        jnp.full((devices * capacity + 1,), -1, jnp.int32)
        .at[placing]
        .set(jnp.arange(slot_count, dtype=jnp.int32))[: devices * capacity]
    )
    departing_tiles = gather_tiles(src, grid_tiles)
    label_rows = jnp.stack([tile_owner % owned, tile_rows % RT_OP, tile_cols % kc_local], axis=1)
    labels = jnp.where((src >= 0)[:, None], jnp.take(label_rows, jnp.maximum(src, 0), axis=0), -1)
    arrived = lax.all_to_all(labels, ("opair", "vpair"), split_axis=0, concat_axis=0, tiled=True)
    incoming = lax.all_to_all(
        departing_tiles, ("opair", "vpair"), split_axis=0, concat_axis=0, tiled=True
    )
    meta = jnp.transpose(arrived).reshape(-1)
    ring = 4
    ov_tiles, partial_value = place_and_contract(
        meta, incoming, int_table, owned, RT_OP, QUARTERS, ring
    )
    cycle_t = reduce_scatter(partial_value, ring)
    cycle_sum = jnp.transpose(cycle_t.reshape(-1, tile_width))
    return (ov_tiles, cycle_sum)


def solution(mesh):
    in_specs = (
        P(("opair", "vpair"), None, None),
        P(("opair", "vpair")),
        P(("opair", "vpair")),
        P(("opair", "vpair")),
        P("vpair", None),
    )
    out_specs = (P(("opair", "vpair"), None, None), P(("opair", "vpair"), None))
    return jax.shard_map(
        on_device, mesh=mesh, in_specs=in_specs, out_specs=out_specs, check_vma=False
    )
```

```python
import functools

import jax
import jax.numpy as jnp
from jax import lax
from jax.experimental import pallas as pl
from jax.experimental.pallas import tpu as pltpu
from jax.sharding import PartitionSpec as P

RT_OP = 32
QUARTERS = 16
MESH = pl.DeviceIdType.MESH
VMEM_LIMIT = 60 * 1024 * 1024


def gather_kernel(src_ref, grid_ref, out_ref):
    zero = jnp.zeros(out_ref.shape[1:], out_ref.dtype)

    def body(j, carry):
        s = src_ref[j]

        @pl.when(s >= 0)
        def _():
            out_ref[j] = grid_ref[jnp.maximum(s, 0)]

        @pl.when(s < 0)
        def _():
            out_ref[j] = zero

        return carry

    lax.fori_loop(0, out_ref.shape[0], body, 0)


def gather_tiles(src, grid_tiles):
    return pl.pallas_call(
        gather_kernel,
        out_shape=jax.ShapeDtypeStruct(grid_tiles.shape, grid_tiles.dtype),
        in_specs=[
            pl.BlockSpec(memory_space=pltpu.SMEM),
            pl.BlockSpec(memory_space=pltpu.VMEM),
        ],
        out_specs=pl.BlockSpec(memory_space=pltpu.VMEM),
        compiler_params=pltpu.CompilerParams(vmem_limit_bytes=VMEM_LIMIT),
    )(src, grid_tiles)


def storage_row(q, row, ring):
    c = row % 2
    y = (row // 2) % ring
    z = row // (2 * ring)
    half = ring * ring
    if q < QUARTERS // 2:
        return c * half + y * ring + z
    return c * half + z * ring + y


def place_kernel(quarters, ring, meta_ref, inc_ref, int_ref, ov_ref, part_ref):
    slots = inc_ref.shape[0]
    width = part_ref.shape[2]
    part_ref[...] = jnp.zeros(part_ref.shape, part_ref.dtype)

    def body(i, carry):
        pos = meta_ref[i]
        row = meta_ref[slots + i]
        col = meta_ref[2 * slots + i]

        @pl.when(pos >= 0)
        def _():
            tile = inc_ref[i]
            ov_ref[jnp.maximum(pos, 0)] = tile.T
            per = quarters // 4
            for q in range(4):
                block = int_ref[jnp.maximum(col, 0), pl.ds(q * per * width, per * width), :]
                prod = jnp.dot(block, tile, preferred_element_type=jnp.float32)
                for h in range(per):
                    k = per * q + h
                    s = storage_row(k, jnp.maximum(row, 0), ring)
                    part_ref[k, s] += prod[h * width : (h + 1) * width, :]

        return carry

    lax.fori_loop(0, slots, body, 0)


def place_and_contract(meta, incoming, int_table, owned, rows, quarters, ring):
    tile_width = incoming.shape[1]
    columns = int_table.shape[1]
    return pl.pallas_call(
        functools.partial(place_kernel, quarters, ring),
        out_shape=(
            jax.ShapeDtypeStruct((owned, tile_width, tile_width), incoming.dtype),
            jax.ShapeDtypeStruct((quarters, rows, columns // quarters, tile_width), jnp.float32),
        ),
        in_specs=[
            pl.BlockSpec(memory_space=pltpu.SMEM),
            pl.BlockSpec(memory_space=pltpu.VMEM),
            pl.BlockSpec(memory_space=pltpu.VMEM),
        ],
        out_specs=(
            pl.BlockSpec(memory_space=pltpu.VMEM),
            pl.BlockSpec(memory_space=pltpu.VMEM),
        ),
        compiler_params=pltpu.CompilerParams(vmem_limit_bytes=VMEM_LIMIT),
    )(meta, incoming, int_table)


def rs_kernel(ring, part_ref, out_ref, core_buf, red, rbuf1, acc1, fin1, rbuf2, acc2,
              core_send, core_recv, send1, recv1, send2, recv2):
    quarters, rows, tile_width, width = part_ref.shape
    half = rows // 2
    steps = ring - 1
    op = lax.axis_index("opair")
    v = lax.axis_index("vpair")
    c = v % 2
    y = (v // 2) % ring
    z = v // (2 * ring)

    def dev(zz, yy, cc):
        return (op, (zz * ring + yy) * 2 + cc)

    sib = dev(z, y, 1 - c)
    y_up = dev(z, (y + 1) % ring, c)
    y_dn = dev(z, (y + ring - 1) % ring, c)
    z_up = dev((z + 1) % ring, y, c)
    z_dn = dev((z + ring - 1) % ring, y, c)

    barrier = pltpu.get_barrier_semaphore()
    for peer in (sib, y_up, y_dn, z_up, z_dn):
        pl.semaphore_signal(barrier, inc=1, device_id=peer, device_id_type=MESH)
    pl.semaphore_wait(barrier, 5)

    def plan(q):
        d = 1 if q % 2 == 0 else -1
        if q < quarters // 2:
            return d, y, z, (y_up if d > 0 else y_dn), (z_up if d > 0 else z_dn)
        return d, z, y, (z_up if d > 0 else z_dn), (y_up if d > 0 else y_dn)

    def core_copy(q):
        return pltpu.make_async_remote_copy(
            src_ref=part_ref.at[q, pl.ds((1 - c) * half, half)],
            dst_ref=core_buf.at[q],
            send_sem=core_send.at[q],
            recv_sem=core_recv.at[q],
            device_id=sib,
            device_id_type=MESH,
        )

    def first_copy(q, s):
        d, a, b, first, second = plan(q)
        if s == 0:
            blk = (a - d + 2 * ring) % ring
            src = red.at[q, pl.ds(blk * ring, ring)]
        else:
            src = acc1.at[q, s - 1]
        return pltpu.make_async_remote_copy(
            src_ref=src,
            dst_ref=rbuf1.at[q, s],
            send_sem=send1.at[q, s],
            recv_sem=recv1.at[q, s],
            device_id=first,
            device_id_type=MESH,
        )

    def second_copy(q, s):
        d, a, b, first, second = plan(q)
        if s == 0:
            src = fin1.at[q, (b - d + 2 * ring) % ring]
        else:
            src = acc2.at[q, s - 1]
        return pltpu.make_async_remote_copy(
            src_ref=src,
            dst_ref=rbuf2.at[q, s],
            send_sem=send2.at[q, s],
            recv_sem=recv2.at[q, s],
            device_id=second,
            device_id_type=MESH,
        )

    for q in range(quarters):
        core_copy(q).start()

    for q in range(quarters):
        core_copy(q).wait()

        def core_sum(i, carry):
            red[q, i] = part_ref[q, c * half + i] + core_buf[q, i]
            return carry

        lax.fori_loop(0, half, core_sum, 0)
        first_copy(q, 0).start()

    for s in range(steps):
        for q in range(quarters):
            first_copy(q, s).wait()
            d, a, b, first, second = plan(q)
            blk = (a - d * (s + 2) + 3 * ring) % ring
            for j in range(ring):
                total = rbuf1[q, s, j] + red[q, blk * ring + j]
                if s < steps - 1:
                    acc1[q, s, j] = total
                else:
                    fin1[q, j] = total
            if s < steps - 1:
                first_copy(q, s + 1).start()
            else:
                second_copy(q, 0).start()

    for s in range(steps):
        for q in range(quarters):
            second_copy(q, s).wait()
            d, a, b, first, second = plan(q)
            blk = (b - d * (s + 2) + 3 * ring) % ring
            total = rbuf2[q, s] + fin1[q, blk]
            if s < steps - 1:
                acc2[q, s] = total
                second_copy(q, s + 1).start()
            else:
                out_ref[q] = total


def reduce_scatter(part, ring):
    quarters, rows, tile_width, width = part.shape
    half = rows // 2
    steps = ring - 1
    f32 = jnp.float32
    return pl.pallas_call(
        functools.partial(rs_kernel, ring),
        out_shape=jax.ShapeDtypeStruct((quarters, tile_width, width), f32),
        in_specs=[pl.BlockSpec(memory_space=pltpu.VMEM)],
        out_specs=pl.BlockSpec(memory_space=pltpu.VMEM),
        scratch_shapes=[
            pltpu.VMEM((quarters, half, tile_width, width), f32),
            pltpu.VMEM((quarters, half, tile_width, width), f32),
            pltpu.VMEM((quarters, steps, ring, tile_width, width), f32),
            pltpu.VMEM((quarters, steps - 1, ring, tile_width, width), f32),
            pltpu.VMEM((quarters, ring, tile_width, width), f32),
            pltpu.VMEM((quarters, steps, tile_width, width), f32),
            pltpu.VMEM((quarters, steps - 1, tile_width, width), f32),
            pltpu.SemaphoreType.DMA((quarters,)),
            pltpu.SemaphoreType.DMA((quarters,)),
            pltpu.SemaphoreType.DMA((quarters, steps)),
            pltpu.SemaphoreType.DMA((quarters, steps)),
            pltpu.SemaphoreType.DMA((quarters, steps)),
            pltpu.SemaphoreType.DMA((quarters, steps)),
        ],
        compiler_params=pltpu.CompilerParams(
            collective_id=0, has_side_effects=True, vmem_limit_bytes=VMEM_LIMIT
        ),
    )(part)


def on_device(grid_tiles, tile_rows, tile_cols, tile_owner, integrals):
    op_count = lax.axis_size("opair")
    vp_count = lax.axis_size("vpair")
    devices = op_count * vp_count
    slot_count, tile_width, _ = grid_tiles.shape
    owned = slot_count // 2
    capacity = slot_count // devices
    kc_local = integrals.shape[0] // tile_width
    int_table = jnp.swapaxes(integrals.reshape(kc_local, tile_width, integrals.shape[1]), 1, 2)
    live_slots = tile_owner >= 0
    target = jnp.where(live_slots, tile_owner // owned, devices)
    matches = (target[:, None] == jnp.arange(devices, dtype=jnp.int32)[None, :]).astype(jnp.int32)
    earlier = jnp.sum((jnp.cumsum(matches, axis=0) - matches) * matches, axis=1)
    placing = jnp.where(live_slots, target * capacity + earlier, devices * capacity)
    src = (
        jnp.full((devices * capacity + 1,), -1, jnp.int32)
        .at[placing]
        .set(jnp.arange(slot_count, dtype=jnp.int32))[: devices * capacity]
    )
    departing_tiles = gather_tiles(src, grid_tiles)
    label_rows = jnp.stack([tile_owner % owned, tile_rows % RT_OP, tile_cols % kc_local], axis=1)
    labels = jnp.where((src >= 0)[:, None], jnp.take(label_rows, jnp.maximum(src, 0), axis=0), -1)
    arrived = lax.all_to_all(labels, ("opair", "vpair"), split_axis=0, concat_axis=0, tiled=True)
    incoming = lax.all_to_all(
        departing_tiles, ("opair", "vpair"), split_axis=0, concat_axis=0, tiled=True
    )
    meta = jnp.transpose(arrived).reshape(-1)
    ring = 4
    ov_tiles, partial_value = place_and_contract(
        meta, incoming, int_table, owned, RT_OP, QUARTERS, ring
    )
    cycle_t = reduce_scatter(partial_value, ring)
    cycle_sum = jnp.transpose(cycle_t.reshape(-1, tile_width))
    return (ov_tiles, cycle_sum)


def solution(mesh):
    in_specs = (
        P(("opair", "vpair"), None, None),
        P(("opair", "vpair")),
        P(("opair", "vpair")),
        P(("opair", "vpair")),
        P("vpair", None),
    )
    out_specs = (P(("opair", "vpair"), None, None), P(("opair", "vpair"), None))
    return jax.shard_map(
        on_device, mesh=mesh, in_specs=in_specs, out_specs=out_specs, check_vma=False
    )
```

```python
import functools

import jax
import jax.numpy as jnp
from jax import lax
from jax.experimental import pallas as pl
from jax.experimental.pallas import tpu as pltpu
from jax.sharding import PartitionSpec as P

RT_OP = 32
QUARTERS = 8
MESH = pl.DeviceIdType.MESH
VMEM_LIMIT = 60 * 1024 * 1024


def gather_kernel(src_ref, grid_ref, out_ref, sems):
    slots = out_ref.shape[0]

    def copy(j):
        return pltpu.make_async_copy(
            grid_ref.at[jnp.maximum(src_ref[j], 0)], out_ref.at[j], sems.at[j]
        )

    def start(j, carry):
        copy(j).start()
        return carry

    def finish(j, carry):
        copy(j).wait()
        return carry

    lax.fori_loop(0, slots, start, 0)
    lax.fori_loop(0, slots, finish, 0)


def gather_tiles(src, grid_tiles):
    return pl.pallas_call(
        gather_kernel,
        out_shape=jax.ShapeDtypeStruct(grid_tiles.shape, grid_tiles.dtype),
        in_specs=[
            pl.BlockSpec(memory_space=pltpu.SMEM),
            pl.BlockSpec(memory_space=pl.ANY),
        ],
        out_specs=pl.BlockSpec(memory_space=pltpu.VMEM),
        scratch_shapes=[pltpu.SemaphoreType.DMA((grid_tiles.shape[0],))],
        compiler_params=pltpu.CompilerParams(vmem_limit_bytes=VMEM_LIMIT),
    )(src, grid_tiles)


def storage_row(q, row, ring):
    c = row % 2
    y = (row // 2) % ring
    z = row // (2 * ring)
    half = ring * ring
    if q < QUARTERS // 2:
        return c * half + y * ring + z
    return c * half + z * ring + y


def place_kernel(quarters, ring, meta_ref, inc_ref, int_ref, ov_ref, part_ref):
    slots = inc_ref.shape[0]
    width = part_ref.shape[2]
    part_ref[...] = jnp.zeros(part_ref.shape, part_ref.dtype)

    def body(i, carry):
        pos = meta_ref[i]
        row = meta_ref[slots + i]
        col = meta_ref[2 * slots + i]

        @pl.when(pos >= 0)
        def _():
            tile = inc_ref[i]
            ov_ref[jnp.maximum(pos, 0)] = tile.T
            for q in range(quarters // 2):
                block = int_ref[jnp.maximum(col, 0), pl.ds(2 * q * width, 2 * width), :]
                prod = jnp.dot(block, tile, preferred_element_type=jnp.float32)
                for h in range(2):
                    k = 2 * q + h
                    s = storage_row(k, jnp.maximum(row, 0), ring)
                    part_ref[k, s] += prod[h * width : (h + 1) * width, :]

        return carry

    lax.fori_loop(0, slots, body, 0)


def place_and_contract(meta, incoming, int_table, owned, rows, quarters, ring):
    tile_width = incoming.shape[1]
    columns = int_table.shape[1]
    return pl.pallas_call(
        functools.partial(place_kernel, quarters, ring),
        out_shape=(
            jax.ShapeDtypeStruct((owned, tile_width, tile_width), incoming.dtype),
            jax.ShapeDtypeStruct((quarters, rows, columns // quarters, tile_width), jnp.float32),
        ),
        in_specs=[
            pl.BlockSpec(memory_space=pltpu.SMEM),
            pl.BlockSpec(memory_space=pltpu.VMEM),
            pl.BlockSpec(memory_space=pltpu.VMEM),
        ],
        out_specs=(
            pl.BlockSpec(memory_space=pltpu.VMEM),
            pl.BlockSpec(memory_space=pltpu.VMEM),
        ),
        compiler_params=pltpu.CompilerParams(vmem_limit_bytes=VMEM_LIMIT),
    )(meta, incoming, int_table)


def rs_kernel(ring, part_ref, out_ref, core_buf, red, rbuf1, acc1, fin1, rbuf2, acc2,
              core_send, core_recv, send1, recv1, send2, recv2):
    quarters, rows, tile_width, width = part_ref.shape
    half = rows // 2
    steps = ring - 1
    op = lax.axis_index("opair")
    v = lax.axis_index("vpair")
    c = v % 2
    y = (v // 2) % ring
    z = v // (2 * ring)

    def dev(zz, yy, cc):
        return (op, (zz * ring + yy) * 2 + cc)

    sib = dev(z, y, 1 - c)
    y_up = dev(z, (y + 1) % ring, c)
    y_dn = dev(z, (y + ring - 1) % ring, c)
    z_up = dev((z + 1) % ring, y, c)
    z_dn = dev((z + ring - 1) % ring, y, c)

    barrier = pltpu.get_barrier_semaphore()
    for peer in (sib, y_up, y_dn, z_up, z_dn):
        pl.semaphore_signal(barrier, inc=1, device_id=peer, device_id_type=MESH)
    pl.semaphore_wait(barrier, 5)

    def plan(q):
        d = 1 if q % 2 == 0 else -1
        if q < quarters // 2:
            return d, y, z, (y_up if d > 0 else y_dn), (z_up if d > 0 else z_dn)
        return d, z, y, (z_up if d > 0 else z_dn), (y_up if d > 0 else y_dn)

    def core_copy(q):
        return pltpu.make_async_remote_copy(
            src_ref=part_ref.at[q, pl.ds((1 - c) * half, half)],
            dst_ref=core_buf.at[q],
            send_sem=core_send.at[q],
            recv_sem=core_recv.at[q],
            device_id=sib,
            device_id_type=MESH,
        )

    def first_copy(q, s):
        d, a, b, first, second = plan(q)
        if s == 0:
            blk = (a - d + 2 * ring) % ring
            src = red.at[q, pl.ds(blk * ring, ring)]
        else:
            src = acc1.at[q, s - 1]
        return pltpu.make_async_remote_copy(
            src_ref=src,
            dst_ref=rbuf1.at[q, s],
            send_sem=send1.at[q, s],
            recv_sem=recv1.at[q, s],
            device_id=first,
            device_id_type=MESH,
        )

    def second_copy(q, s):
        d, a, b, first, second = plan(q)
        if s == 0:
            src = fin1.at[q, (b - d + 2 * ring) % ring]
        else:
            src = acc2.at[q, s - 1]
        return pltpu.make_async_remote_copy(
            src_ref=src,
            dst_ref=rbuf2.at[q, s],
            send_sem=send2.at[q, s],
            recv_sem=recv2.at[q, s],
            device_id=second,
            device_id_type=MESH,
        )

    for q in range(quarters):
        core_copy(q).start()

    for q in range(quarters):
        core_copy(q).wait()

        def core_sum(i, carry):
            red[q, i] = part_ref[q, c * half + i] + core_buf[q, i]
            return carry

        lax.fori_loop(0, half, core_sum, 0)
        first_copy(q, 0).start()

    for s in range(steps):
        for q in range(quarters):
            first_copy(q, s).wait()
            d, a, b, first, second = plan(q)
            blk = (a - d * (s + 2) + 3 * ring) % ring
            for j in range(ring):
                total = rbuf1[q, s, j] + red[q, blk * ring + j]
                if s < steps - 1:
                    acc1[q, s, j] = total
                else:
                    fin1[q, j] = total
            if s < steps - 1:
                first_copy(q, s + 1).start()
            else:
                second_copy(q, 0).start()

    for s in range(steps):
        for q in range(quarters):
            second_copy(q, s).wait()
            d, a, b, first, second = plan(q)
            blk = (b - d * (s + 2) + 3 * ring) % ring
            total = rbuf2[q, s] + fin1[q, blk]
            if s < steps - 1:
                acc2[q, s] = total
                second_copy(q, s + 1).start()
            else:
                out_ref[q] = total


def reduce_scatter(part, ring):
    quarters, rows, tile_width, width = part.shape
    half = rows // 2
    steps = ring - 1
    f32 = jnp.float32
    return pl.pallas_call(
        functools.partial(rs_kernel, ring),
        out_shape=jax.ShapeDtypeStruct((quarters, tile_width, width), f32),
        in_specs=[pl.BlockSpec(memory_space=pltpu.VMEM)],
        out_specs=pl.BlockSpec(memory_space=pltpu.VMEM),
        scratch_shapes=[
            pltpu.VMEM((quarters, half, tile_width, width), f32),
            pltpu.VMEM((quarters, half, tile_width, width), f32),
            pltpu.VMEM((quarters, steps, ring, tile_width, width), f32),
            pltpu.VMEM((quarters, steps - 1, ring, tile_width, width), f32),
            pltpu.VMEM((quarters, ring, tile_width, width), f32),
            pltpu.VMEM((quarters, steps, tile_width, width), f32),
            pltpu.VMEM((quarters, steps - 1, tile_width, width), f32),
            pltpu.SemaphoreType.DMA((quarters,)),
            pltpu.SemaphoreType.DMA((quarters,)),
            pltpu.SemaphoreType.DMA((quarters, steps)),
            pltpu.SemaphoreType.DMA((quarters, steps)),
            pltpu.SemaphoreType.DMA((quarters, steps)),
            pltpu.SemaphoreType.DMA((quarters, steps)),
        ],
        compiler_params=pltpu.CompilerParams(
            collective_id=0, has_side_effects=True, vmem_limit_bytes=VMEM_LIMIT
        ),
    )(part)


def on_device(grid_tiles, tile_rows, tile_cols, tile_owner, integrals):
    op_count = lax.axis_size("opair")
    vp_count = lax.axis_size("vpair")
    devices = op_count * vp_count
    slot_count, tile_width, _ = grid_tiles.shape
    owned = slot_count // 2
    capacity = slot_count // devices
    kc_local = integrals.shape[0] // tile_width
    int_table = jnp.swapaxes(integrals.reshape(kc_local, tile_width, integrals.shape[1]), 1, 2)
    live_slots = tile_owner >= 0
    target = jnp.where(live_slots, tile_owner // owned, devices)
    matches = (target[:, None] == jnp.arange(devices, dtype=jnp.int32)[None, :]).astype(jnp.int32)
    earlier = jnp.sum((jnp.cumsum(matches, axis=0) - matches) * matches, axis=1)
    placing = jnp.where(live_slots, target * capacity + earlier, devices * capacity)
    src = (
        jnp.full((devices * capacity + 1,), -1, jnp.int32)
        .at[placing]
        .set(jnp.arange(slot_count, dtype=jnp.int32))[: devices * capacity]
    )
    departing_tiles = gather_tiles(src, grid_tiles)
    label_rows = jnp.stack([tile_owner % owned, tile_rows % RT_OP, tile_cols % kc_local], axis=1)
    labels = jnp.where((src >= 0)[:, None], jnp.take(label_rows, jnp.maximum(src, 0), axis=0), -1)
    arrived = lax.all_to_all(labels, ("opair", "vpair"), split_axis=0, concat_axis=0, tiled=True)
    incoming = lax.all_to_all(
        departing_tiles, ("opair", "vpair"), split_axis=0, concat_axis=0, tiled=True
    )
    meta = jnp.transpose(arrived).reshape(-1)
    ring = 4
    ov_tiles, partial_value = place_and_contract(
        meta, incoming, int_table, owned, RT_OP, QUARTERS, ring
    )
    cycle_t = reduce_scatter(partial_value, ring)
    cycle_sum = jnp.transpose(cycle_t.reshape(-1, tile_width))
    return (ov_tiles, cycle_sum)


def solution(mesh):
    in_specs = (
        P(("opair", "vpair"), None, None),
        P(("opair", "vpair")),
        P(("opair", "vpair")),
        P(("opair", "vpair")),
        P("vpair", None),
    )
    out_specs = (P(("opair", "vpair"), None, None), P(("opair", "vpair"), None))
    return jax.shard_map(
        on_device, mesh=mesh, in_specs=in_specs, out_specs=out_specs, check_vma=False
    )
```

```python
import functools

import jax
import jax.numpy as jnp
from jax import lax
from jax.experimental import pallas as pl
from jax.experimental.pallas import tpu as pltpu
from jax.sharding import PartitionSpec as P

RT_OP = 32
QUARTERS = 8
MESH = pl.DeviceIdType.MESH
VMEM_LIMIT = 60 * 1024 * 1024


def gather_kernel(src_ref, grid_ref, out_ref):
    zero = jnp.zeros(out_ref.shape[1:], out_ref.dtype)

    def body(j, carry):
        s = src_ref[j]

        @pl.when(s >= 0)
        def _():
            out_ref[j] = grid_ref[jnp.maximum(s, 0)]

        @pl.when(s < 0)
        def _():
            out_ref[j] = zero

        return carry

    lax.fori_loop(0, out_ref.shape[0], body, 0)


def gather_tiles(src, grid_tiles):
    return pl.pallas_call(
        gather_kernel,
        out_shape=jax.ShapeDtypeStruct(grid_tiles.shape, grid_tiles.dtype),
        in_specs=[
            pl.BlockSpec(memory_space=pltpu.SMEM),
            pl.BlockSpec(memory_space=pltpu.VMEM),
        ],
        out_specs=pl.BlockSpec(memory_space=pltpu.VMEM),
        compiler_params=pltpu.CompilerParams(vmem_limit_bytes=VMEM_LIMIT),
    )(src, grid_tiles)


def storage_row(q, row, ring):
    c = row % 2
    y = (row // 2) % ring
    z = row // (2 * ring)
    half = ring * ring
    if q < QUARTERS // 2:
        return c * half + y * ring + z
    return c * half + z * ring + y


def place_kernel(quarters, ring, meta_ref, inc_ref, int_ref, ov_ref, part_ref):
    slots = inc_ref.shape[0]
    width = part_ref.shape[2]
    part_ref[...] = jnp.zeros(part_ref.shape, part_ref.dtype)

    def body(i, carry):
        pos = meta_ref[i]
        row = meta_ref[slots + i]
        col = meta_ref[2 * slots + i]

        @pl.when(pos >= 0)
        def _():
            tile = inc_ref[i]
            ov_ref[jnp.maximum(pos, 0)] = tile.T
            for q in range(quarters // 2):
                block = int_ref[jnp.maximum(col, 0), pl.ds(2 * q * width, 2 * width), :]
                prod = jnp.dot(block, tile, preferred_element_type=jnp.float32)
                for h in range(2):
                    k = 2 * q + h
                    s = storage_row(k, jnp.maximum(row, 0), ring)
                    part_ref[k, s] += prod[h * width : (h + 1) * width, :]

        return carry

    lax.fori_loop(0, slots, body, 0)


def place_and_contract(meta, incoming, int_table, owned, rows, quarters, ring):
    tile_width = incoming.shape[1]
    columns = int_table.shape[1]
    return pl.pallas_call(
        functools.partial(place_kernel, quarters, ring),
        out_shape=(
            jax.ShapeDtypeStruct((owned, tile_width, tile_width), incoming.dtype),
            jax.ShapeDtypeStruct((quarters, rows, columns // quarters, tile_width), jnp.float32),
        ),
        in_specs=[
            pl.BlockSpec(memory_space=pltpu.SMEM),
            pl.BlockSpec(memory_space=pltpu.VMEM),
            pl.BlockSpec(memory_space=pltpu.VMEM),
        ],
        out_specs=(
            pl.BlockSpec(memory_space=pltpu.VMEM),
            pl.BlockSpec(memory_space=pltpu.VMEM),
        ),
        compiler_params=pltpu.CompilerParams(vmem_limit_bytes=VMEM_LIMIT),
    )(meta, incoming, int_table)


def rs_kernel(ring, part_ref, out_ref, core_buf, red, rbuf1, acc1, fin1, rbuf2, acc2,
              core_send, core_recv, send1, recv1, send2, recv2):
    quarters, rows, tile_width, width = part_ref.shape
    half = rows // 2
    steps = ring - 1
    op = lax.axis_index("opair")
    v = lax.axis_index("vpair")
    c = v % 2
    y = (v // 2) % ring
    z = v // (2 * ring)

    def dev(zz, yy, cc):
        return (op, (zz * ring + yy) * 2 + cc)

    sib = dev(z, y, 1 - c)
    y_up = dev(z, (y + 1) % ring, c)
    y_dn = dev(z, (y + ring - 1) % ring, c)
    z_up = dev((z + 1) % ring, y, c)
    z_dn = dev((z + ring - 1) % ring, y, c)

    barrier = pltpu.get_barrier_semaphore()
    for peer in (sib, y_up, y_dn, z_up, z_dn):
        pl.semaphore_signal(barrier, inc=1, device_id=peer, device_id_type=MESH)
    pl.semaphore_wait(barrier, 5)

    def plan(q):
        d = 1 if q % 2 == 0 else -1
        if q < quarters // 2:
            return d, y, z, (y_up if d > 0 else y_dn), (z_up if d > 0 else z_dn)
        return d, z, y, (z_up if d > 0 else z_dn), (y_up if d > 0 else y_dn)

    def core_copy(q):
        return pltpu.make_async_remote_copy(
            src_ref=part_ref.at[q, pl.ds((1 - c) * half, half)],
            dst_ref=core_buf.at[q],
            send_sem=core_send.at[q],
            recv_sem=core_recv.at[q],
            device_id=sib,
            device_id_type=MESH,
        )

    def first_copy(q, s):
        d, a, b, first, second = plan(q)
        if s == 0:
            blk = (a - d + 2 * ring) % ring
            src = red.at[q, pl.ds(blk * ring, ring)]
        else:
            src = acc1.at[q, s - 1]
        return pltpu.make_async_remote_copy(
            src_ref=src,
            dst_ref=rbuf1.at[q, s],
            send_sem=send1.at[q, s],
            recv_sem=recv1.at[q, s],
            device_id=first,
            device_id_type=MESH,
        )

    def second_copy(q, s):
        d, a, b, first, second = plan(q)
        if s == 0:
            src = fin1.at[q, (b - d + 2 * ring) % ring]
        else:
            src = acc2.at[q, s - 1]
        return pltpu.make_async_remote_copy(
            src_ref=src,
            dst_ref=rbuf2.at[q, s],
            send_sem=send2.at[q, s],
            recv_sem=recv2.at[q, s],
            device_id=second,
            device_id_type=MESH,
        )

    ahead = 2
    for q in range(ahead):
        core_copy(q).start()

    for q in range(quarters):
        core_copy(q).wait()
        if q + ahead < quarters:
            core_copy(q + ahead).start()

        def core_sum(i, carry):
            red[q, i] = part_ref[q, c * half + i] + core_buf[q, i]
            return carry

        lax.fori_loop(0, half, core_sum, 0)
        first_copy(q, 0).start()

    for s in range(steps):
        for q in range(quarters):
            first_copy(q, s).wait()
            d, a, b, first, second = plan(q)
            blk = (a - d * (s + 2) + 3 * ring) % ring
            for j in range(ring):
                total = rbuf1[q, s, j] + red[q, blk * ring + j]
                if s < steps - 1:
                    acc1[q, s, j] = total
                else:
                    fin1[q, j] = total
            if s < steps - 1:
                first_copy(q, s + 1).start()
            else:
                second_copy(q, 0).start()

    for s in range(steps):
        for q in range(quarters):
            second_copy(q, s).wait()
            d, a, b, first, second = plan(q)
            blk = (b - d * (s + 2) + 3 * ring) % ring
            total = rbuf2[q, s] + fin1[q, blk]
            if s < steps - 1:
                acc2[q, s] = total
                second_copy(q, s + 1).start()
            else:
                out_ref[q] = total


def reduce_scatter(part, ring):
    quarters, rows, tile_width, width = part.shape
    half = rows // 2
    steps = ring - 1
    f32 = jnp.float32
    return pl.pallas_call(
        functools.partial(rs_kernel, ring),
        out_shape=jax.ShapeDtypeStruct((quarters, tile_width, width), f32),
        in_specs=[pl.BlockSpec(memory_space=pltpu.VMEM)],
        out_specs=pl.BlockSpec(memory_space=pltpu.VMEM),
        scratch_shapes=[
            pltpu.VMEM((quarters, half, tile_width, width), f32),
            pltpu.VMEM((quarters, half, tile_width, width), f32),
            pltpu.VMEM((quarters, steps, ring, tile_width, width), f32),
            pltpu.VMEM((quarters, steps - 1, ring, tile_width, width), f32),
            pltpu.VMEM((quarters, ring, tile_width, width), f32),
            pltpu.VMEM((quarters, steps, tile_width, width), f32),
            pltpu.VMEM((quarters, steps - 1, tile_width, width), f32),
            pltpu.SemaphoreType.DMA((quarters,)),
            pltpu.SemaphoreType.DMA((quarters,)),
            pltpu.SemaphoreType.DMA((quarters, steps)),
            pltpu.SemaphoreType.DMA((quarters, steps)),
            pltpu.SemaphoreType.DMA((quarters, steps)),
            pltpu.SemaphoreType.DMA((quarters, steps)),
        ],
        compiler_params=pltpu.CompilerParams(
            collective_id=0, has_side_effects=True, vmem_limit_bytes=VMEM_LIMIT
        ),
    )(part)


def on_device(grid_tiles, tile_rows, tile_cols, tile_owner, integrals):
    op_count = lax.axis_size("opair")
    vp_count = lax.axis_size("vpair")
    devices = op_count * vp_count
    slot_count, tile_width, _ = grid_tiles.shape
    owned = slot_count // 2
    capacity = slot_count // devices
    kc_local = integrals.shape[0] // tile_width
    int_table = jnp.swapaxes(integrals.reshape(kc_local, tile_width, integrals.shape[1]), 1, 2)
    live_slots = tile_owner >= 0
    target = jnp.where(live_slots, tile_owner // owned, devices)
    matches = (target[:, None] == jnp.arange(devices, dtype=jnp.int32)[None, :]).astype(jnp.int32)
    earlier = jnp.sum((jnp.cumsum(matches, axis=0) - matches) * matches, axis=1)
    placing = jnp.where(live_slots, target * capacity + earlier, devices * capacity)
    src = (
        jnp.full((devices * capacity + 1,), -1, jnp.int32)
        .at[placing]
        .set(jnp.arange(slot_count, dtype=jnp.int32))[: devices * capacity]
    )
    departing_tiles = gather_tiles(src, grid_tiles)
    label_rows = jnp.stack([tile_owner % owned, tile_rows % RT_OP, tile_cols % kc_local], axis=1)
    labels = jnp.where((src >= 0)[:, None], jnp.take(label_rows, jnp.maximum(src, 0), axis=0), -1)
    arrived = lax.all_to_all(labels, ("opair", "vpair"), split_axis=0, concat_axis=0, tiled=True)
    incoming = lax.all_to_all(
        departing_tiles, ("opair", "vpair"), split_axis=0, concat_axis=0, tiled=True
    )
    meta = jnp.transpose(arrived).reshape(-1)
    ring = 4
    ov_tiles, partial_value = place_and_contract(
        meta, incoming, int_table, owned, RT_OP, QUARTERS, ring
    )
    cycle_t = reduce_scatter(partial_value, ring)
    cycle_sum = jnp.transpose(cycle_t.reshape(-1, tile_width))
    return (ov_tiles, cycle_sum)


def solution(mesh):
    in_specs = (
        P(("opair", "vpair"), None, None),
        P(("opair", "vpair")),
        P(("opair", "vpair")),
        P(("opair", "vpair")),
        P("vpair", None),
    )
    out_specs = (P(("opair", "vpair"), None, None), P(("opair", "vpair"), None))
    return jax.shard_map(
        on_device, mesh=mesh, in_specs=in_specs, out_specs=out_specs, check_vma=False
    )
```

```python
import functools

import jax
import jax.numpy as jnp
from jax import lax
from jax.experimental import pallas as pl
from jax.experimental.pallas import tpu as pltpu
from jax.sharding import PartitionSpec as P

RT_OP = 32
QUARTERS = 8
MESH = pl.DeviceIdType.MESH
VMEM_LIMIT = 60 * 1024 * 1024


def gather_kernel(src_ref, grid_ref, out_ref):
    zero = jnp.zeros(out_ref.shape[1:], out_ref.dtype)

    def body(j, carry):
        s = src_ref[j]

        @pl.when(s >= 0)
        def _():
            out_ref[j] = grid_ref[jnp.maximum(s, 0)]

        @pl.when(s < 0)
        def _():
            out_ref[j] = zero

        return carry

    lax.fori_loop(0, out_ref.shape[0], body, 0)


def gather_tiles(src, grid_tiles):
    return pl.pallas_call(
        gather_kernel,
        out_shape=jax.ShapeDtypeStruct(grid_tiles.shape, grid_tiles.dtype),
        in_specs=[
            pl.BlockSpec(memory_space=pltpu.SMEM),
            pl.BlockSpec(memory_space=pltpu.VMEM),
        ],
        out_specs=pl.BlockSpec(memory_space=pltpu.VMEM),
        compiler_params=pltpu.CompilerParams(vmem_limit_bytes=VMEM_LIMIT),
    )(src, grid_tiles)


def storage_row(q, row, ring):
    c = row % 2
    y = (row // 2) % ring
    z = row // (2 * ring)
    half = ring * ring
    if q < QUARTERS // 2:
        return c * half + y * ring + z
    return c * half + z * ring + y


def place_kernel(quarters, ring, meta_ref, inc_ref, int_ref, ov_ref, part_ref):
    slots = inc_ref.shape[0]
    width = part_ref.shape[2]
    part_ref[...] = jnp.zeros(part_ref.shape, part_ref.dtype)

    def body(i, carry):
        pos = meta_ref[i]
        row = meta_ref[slots + i]
        col = meta_ref[2 * slots + i]

        @pl.when(pos >= 0)
        def _():
            tile = inc_ref[i]
            ov_ref[jnp.maximum(pos, 0)] = tile.T
            for q in range(quarters // 2):
                block = int_ref[jnp.maximum(col, 0), pl.ds(2 * q * width, 2 * width), :]
                prod = jnp.dot(block, tile, preferred_element_type=jnp.float32)
                for h in range(2):
                    k = 2 * q + h
                    s = storage_row(k, jnp.maximum(row, 0), ring)
                    part_ref[k, s] += prod[h * width : (h + 1) * width, :]

        return carry

    lax.fori_loop(0, slots, body, 0)


def place_and_contract(meta, incoming, int_table, owned, rows, quarters, ring):
    tile_width = incoming.shape[1]
    columns = int_table.shape[1]
    return pl.pallas_call(
        functools.partial(place_kernel, quarters, ring),
        out_shape=(
            jax.ShapeDtypeStruct((owned, tile_width, tile_width), incoming.dtype),
            jax.ShapeDtypeStruct((quarters, rows, columns // quarters, tile_width), jnp.float32),
        ),
        in_specs=[
            pl.BlockSpec(memory_space=pltpu.SMEM),
            pl.BlockSpec(memory_space=pltpu.VMEM),
            pl.BlockSpec(memory_space=pltpu.VMEM),
        ],
        out_specs=(
            pl.BlockSpec(memory_space=pltpu.VMEM),
            pl.BlockSpec(memory_space=pltpu.VMEM),
        ),
        compiler_params=pltpu.CompilerParams(vmem_limit_bytes=VMEM_LIMIT),
    )(meta, incoming, int_table)


def rs_kernel(ring, part_ref, out_ref, core_buf, red, rbuf1, acc1, fin1, rbuf2, acc2,
              core_send, core_recv, send1, recv1, send2, recv2):
    quarters, rows, tile_width, width = part_ref.shape
    half = rows // 2
    steps = ring - 1
    op = lax.axis_index("opair")
    v = lax.axis_index("vpair")
    c = v % 2
    y = (v // 2) % ring
    z = v // (2 * ring)

    def dev(zz, yy, cc):
        return (op, (zz * ring + yy) * 2 + cc)

    sib = dev(z, y, 1 - c)
    y_up = dev(z, (y + 1) % ring, c)
    y_dn = dev(z, (y + ring - 1) % ring, c)
    z_up = dev((z + 1) % ring, y, c)
    z_dn = dev((z + ring - 1) % ring, y, c)

    barrier = pltpu.get_barrier_semaphore()
    for peer in (sib, y_up, y_dn, z_up, z_dn):
        pl.semaphore_signal(barrier, inc=1, device_id=peer, device_id_type=MESH)
    pl.semaphore_wait(barrier, 5)

    def plan(q):
        d = 1 if q % 2 == 0 else -1
        if q < quarters // 2:
            return d, y, z, (y_up if d > 0 else y_dn), (z_up if d > 0 else z_dn)
        return d, z, y, (z_up if d > 0 else z_dn), (y_up if d > 0 else y_dn)

    def core_copy(q):
        return pltpu.make_async_remote_copy(
            src_ref=part_ref.at[q, pl.ds((1 - c) * half, half)],
            dst_ref=core_buf.at[q],
            send_sem=core_send.at[q],
            recv_sem=core_recv.at[q],
            device_id=sib,
            device_id_type=MESH,
        )

    def first_copy(q, s):
        d, a, b, first, second = plan(q)
        if s == 0:
            blk = (a - d + 2 * ring) % ring
            src = red.at[q, pl.ds(blk * ring, ring)]
        else:
            src = acc1.at[q, s - 1]
        return pltpu.make_async_remote_copy(
            src_ref=src,
            dst_ref=rbuf1.at[q, s],
            send_sem=send1.at[q, s],
            recv_sem=recv1.at[q, s],
            device_id=first,
            device_id_type=MESH,
        )

    def second_copy(q, s):
        d, a, b, first, second = plan(q)
        if s == 0:
            src = fin1.at[q, (b - d + 2 * ring) % ring]
        else:
            src = acc2.at[q, s - 1]
        return pltpu.make_async_remote_copy(
            src_ref=src,
            dst_ref=rbuf2.at[q, s],
            send_sem=send2.at[q, s],
            recv_sem=recv2.at[q, s],
            device_id=second,
            device_id_type=MESH,
        )

    ahead = 2
    for q in range(ahead):
        core_copy(q).start()

    for q in range(quarters):
        core_copy(q).wait()
        if q + ahead < quarters:
            core_copy(q + ahead).start()

        def core_sum(i, carry):
            red[q, i] = part_ref[q, c * half + i] + core_buf[q, i]
            return carry

        lax.fori_loop(0, half, core_sum, 0)
        first_copy(q, 0).start()

    for s in range(steps):
        for q in range(quarters):
            first_copy(q, s).wait()
            d, a, b, first, second = plan(q)
            blk = (a - d * (s + 2) + 3 * ring) % ring
            for j in range(ring):
                total = rbuf1[q, s, j] + red[q, blk * ring + j]
                if s < steps - 1:
                    acc1[q, s, j] = total
                else:
                    fin1[q, j] = total
            if s < steps - 1:
                first_copy(q, s + 1).start()
            else:
                second_copy(q, 0).start()

    for s in range(steps):
        for q in range(quarters):
            second_copy(q, s).wait()
            d, a, b, first, second = plan(q)
            blk = (b - d * (s + 2) + 3 * ring) % ring
            total = rbuf2[q, s] + fin1[q, blk]
            if s < steps - 1:
                acc2[q, s] = total
                second_copy(q, s + 1).start()
            else:
                out_ref[:, q * tile_width : (q + 1) * tile_width] = total.T


def reduce_scatter(part, ring):
    quarters, rows, tile_width, width = part.shape
    half = rows // 2
    steps = ring - 1
    f32 = jnp.float32
    return pl.pallas_call(
        functools.partial(rs_kernel, ring),
        out_shape=jax.ShapeDtypeStruct((width, quarters * tile_width), f32),
        in_specs=[pl.BlockSpec(memory_space=pltpu.VMEM)],
        out_specs=pl.BlockSpec(memory_space=pltpu.VMEM),
        scratch_shapes=[
            pltpu.VMEM((quarters, half, tile_width, width), f32),
            pltpu.VMEM((quarters, half, tile_width, width), f32),
            pltpu.VMEM((quarters, steps, ring, tile_width, width), f32),
            pltpu.VMEM((quarters, steps - 1, ring, tile_width, width), f32),
            pltpu.VMEM((quarters, ring, tile_width, width), f32),
            pltpu.VMEM((quarters, steps, tile_width, width), f32),
            pltpu.VMEM((quarters, steps - 1, tile_width, width), f32),
            pltpu.SemaphoreType.DMA((quarters,)),
            pltpu.SemaphoreType.DMA((quarters,)),
            pltpu.SemaphoreType.DMA((quarters, steps)),
            pltpu.SemaphoreType.DMA((quarters, steps)),
            pltpu.SemaphoreType.DMA((quarters, steps)),
            pltpu.SemaphoreType.DMA((quarters, steps)),
        ],
        compiler_params=pltpu.CompilerParams(
            collective_id=0, has_side_effects=True, vmem_limit_bytes=VMEM_LIMIT
        ),
    )(part)


def on_device(grid_tiles, tile_rows, tile_cols, tile_owner, integrals):
    op_count = lax.axis_size("opair")
    vp_count = lax.axis_size("vpair")
    devices = op_count * vp_count
    slot_count, tile_width, _ = grid_tiles.shape
    owned = slot_count // 2
    capacity = slot_count // devices
    kc_local = integrals.shape[0] // tile_width
    int_table = jnp.swapaxes(integrals.reshape(kc_local, tile_width, integrals.shape[1]), 1, 2)
    live_slots = tile_owner >= 0
    target = jnp.where(live_slots, tile_owner // owned, devices)
    matches = (target[:, None] == jnp.arange(devices, dtype=jnp.int32)[None, :]).astype(jnp.int32)
    earlier = jnp.sum((jnp.cumsum(matches, axis=0) - matches) * matches, axis=1)
    placing = jnp.where(live_slots, target * capacity + earlier, devices * capacity)
    src = (
        jnp.full((devices * capacity + 1,), -1, jnp.int32)
        .at[placing]
        .set(jnp.arange(slot_count, dtype=jnp.int32))[: devices * capacity]
    )
    departing_tiles = gather_tiles(src, grid_tiles)
    label_rows = jnp.stack([tile_owner % owned, tile_rows % RT_OP, tile_cols % kc_local], axis=1)
    labels = jnp.where((src >= 0)[:, None], jnp.take(label_rows, jnp.maximum(src, 0), axis=0), -1)
    arrived = lax.all_to_all(labels, ("opair", "vpair"), split_axis=0, concat_axis=0, tiled=True)
    incoming = lax.all_to_all(
        departing_tiles, ("opair", "vpair"), split_axis=0, concat_axis=0, tiled=True
    )
    meta = jnp.transpose(arrived).reshape(-1)
    ring = 4
    ov_tiles, partial_value = place_and_contract(
        meta, incoming, int_table, owned, RT_OP, QUARTERS, ring
    )
    cycle_t = reduce_scatter(partial_value, ring)
    cycle_sum = cycle_t
    return (ov_tiles, cycle_sum)


def solution(mesh):
    in_specs = (
        P(("opair", "vpair"), None, None),
        P(("opair", "vpair")),
        P(("opair", "vpair")),
        P(("opair", "vpair")),
        P("vpair", None),
    )
    out_specs = (P(("opair", "vpair"), None, None), P(("opair", "vpair"), None))
    return jax.shard_map(
        on_device, mesh=mesh, in_specs=in_specs, out_specs=out_specs, check_vma=False
    )
```

```python
import functools

import jax
import jax.numpy as jnp
from jax import lax
from jax.experimental import pallas as pl
from jax.experimental.pallas import tpu as pltpu
from jax.sharding import PartitionSpec as P

RT_OP = 32
QUARTERS = 8
MESH = pl.DeviceIdType.MESH
VMEM_LIMIT = 60 * 1024 * 1024


def gather_kernel(src_ref, grid_ref, out_ref):
    zero = jnp.zeros(out_ref.shape[1:], out_ref.dtype)

    def body(j, carry):
        s = src_ref[j]

        @pl.when(s >= 0)
        def _():
            out_ref[j] = grid_ref[jnp.maximum(s, 0)]

        @pl.when(s < 0)
        def _():
            out_ref[j] = zero

        return carry

    lax.fori_loop(0, out_ref.shape[0], body, 0)


def gather_tiles(src, grid_tiles):
    return pl.pallas_call(
        gather_kernel,
        out_shape=jax.ShapeDtypeStruct(grid_tiles.shape, grid_tiles.dtype),
        in_specs=[
            pl.BlockSpec(memory_space=pltpu.SMEM),
            pl.BlockSpec(memory_space=pltpu.VMEM),
        ],
        out_specs=pl.BlockSpec(memory_space=pltpu.VMEM),
        compiler_params=pltpu.CompilerParams(vmem_limit_bytes=VMEM_LIMIT),
    )(src, grid_tiles)


def storage_row(q, row, ring):
    c = row % 2
    y = (row // 2) % ring
    z = row // (2 * ring)
    half = ring * ring
    if q < QUARTERS // 2:
        return c * half + y * ring + z
    return c * half + z * ring + y


def place_kernel(quarters, ring, meta_ref, inc_ref, int_ref, ov_ref, part_ref):
    slots = inc_ref.shape[0]
    width = part_ref.shape[2]
    rows = part_ref.shape[1]
    zero = jnp.zeros(part_ref.shape[2:], part_ref.dtype)

    def clear(r, carry):
        @pl.when(meta_ref[4 * slots + r] > 0)
        def _():
            for q in range(quarters):
                part_ref[q, storage_row(q, r, ring)] = zero

        return carry

    lax.fori_loop(0, rows, clear, 0)

    def body(i, carry):
        pos = meta_ref[i]
        row = meta_ref[slots + i]
        col = meta_ref[2 * slots + i]

        @pl.when(pos >= 0)
        def _():
            tile = inc_ref[i]
            first = meta_ref[3 * slots + i] > 0
            ov_ref[jnp.maximum(pos, 0)] = tile.T
            for q in range(quarters // 2):
                block = int_ref[jnp.maximum(col, 0), pl.ds(2 * q * width, 2 * width), :]
                prod = jnp.dot(block, tile, preferred_element_type=jnp.float32)
                for h in range(2):
                    k = 2 * q + h
                    s = storage_row(k, jnp.maximum(row, 0), ring)
                    piece = prod[h * width : (h + 1) * width, :]
                    part_ref[k, s] = jnp.where(first, piece, part_ref[k, s] + piece)

        return carry

    lax.fori_loop(0, slots, body, 0)


def place_and_contract(meta, incoming, int_table, owned, rows, quarters, ring):
    tile_width = incoming.shape[1]
    columns = int_table.shape[1]
    return pl.pallas_call(
        functools.partial(place_kernel, quarters, ring),
        out_shape=(
            jax.ShapeDtypeStruct((owned, tile_width, tile_width), incoming.dtype),
            jax.ShapeDtypeStruct((quarters, rows, columns // quarters, tile_width), jnp.float32),
        ),
        in_specs=[
            pl.BlockSpec(memory_space=pltpu.SMEM),
            pl.BlockSpec(memory_space=pltpu.VMEM),
            pl.BlockSpec(memory_space=pltpu.VMEM),
        ],
        out_specs=(
            pl.BlockSpec(memory_space=pltpu.VMEM),
            pl.BlockSpec(memory_space=pltpu.VMEM),
        ),
        compiler_params=pltpu.CompilerParams(vmem_limit_bytes=VMEM_LIMIT),
    )(meta, incoming, int_table)


def rs_kernel(ring, part_ref, out_ref, core_buf, red, rbuf1, acc1, fin1, rbuf2, acc2,
              core_send, core_recv, send1, recv1, send2, recv2):
    quarters, rows, tile_width, width = part_ref.shape
    half = rows // 2
    steps = ring - 1
    op = lax.axis_index("opair")
    v = lax.axis_index("vpair")
    c = v % 2
    y = (v // 2) % ring
    z = v // (2 * ring)

    def dev(zz, yy, cc):
        return (op, (zz * ring + yy) * 2 + cc)

    sib = dev(z, y, 1 - c)
    y_up = dev(z, (y + 1) % ring, c)
    y_dn = dev(z, (y + ring - 1) % ring, c)
    z_up = dev((z + 1) % ring, y, c)
    z_dn = dev((z + ring - 1) % ring, y, c)

    barrier = pltpu.get_barrier_semaphore()
    for peer in (sib, y_up, y_dn, z_up, z_dn):
        pl.semaphore_signal(barrier, inc=1, device_id=peer, device_id_type=MESH)
    pl.semaphore_wait(barrier, 5)

    def plan(q):
        d = 1 if q % 2 == 0 else -1
        if q < quarters // 2:
            return d, y, z, (y_up if d > 0 else y_dn), (z_up if d > 0 else z_dn)
        return d, z, y, (z_up if d > 0 else z_dn), (y_up if d > 0 else y_dn)

    def core_copy(q):
        return pltpu.make_async_remote_copy(
            src_ref=part_ref.at[q, pl.ds((1 - c) * half, half)],
            dst_ref=core_buf.at[q],
            send_sem=core_send.at[q],
            recv_sem=core_recv.at[q],
            device_id=sib,
            device_id_type=MESH,
        )

    def first_copy(q, s):
        d, a, b, first, second = plan(q)
        if s == 0:
            blk = (a - d + 2 * ring) % ring
            src = red.at[q, pl.ds(blk * ring, ring)]
        else:
            src = acc1.at[q, s - 1]
        return pltpu.make_async_remote_copy(
            src_ref=src,
            dst_ref=rbuf1.at[q, s],
            send_sem=send1.at[q, s],
            recv_sem=recv1.at[q, s],
            device_id=first,
            device_id_type=MESH,
        )

    def second_copy(q, s):
        d, a, b, first, second = plan(q)
        if s == 0:
            src = fin1.at[q, (b - d + 2 * ring) % ring]
        else:
            src = acc2.at[q, s - 1]
        return pltpu.make_async_remote_copy(
            src_ref=src,
            dst_ref=rbuf2.at[q, s],
            send_sem=send2.at[q, s],
            recv_sem=recv2.at[q, s],
            device_id=second,
            device_id_type=MESH,
        )

    ahead = 2
    for q in range(ahead):
        core_copy(q).start()

    for q in range(quarters):
        core_copy(q).wait()
        if q + ahead < quarters:
            core_copy(q + ahead).start()

        def core_sum(i, carry):
            red[q, i] = part_ref[q, c * half + i] + core_buf[q, i]
            return carry

        lax.fori_loop(0, half, core_sum, 0)
        first_copy(q, 0).start()

    for s in range(steps):
        for q in range(quarters):
            first_copy(q, s).wait()
            d, a, b, first, second = plan(q)
            blk = (a - d * (s + 2) + 3 * ring) % ring
            for j in range(ring):
                total = rbuf1[q, s, j] + red[q, blk * ring + j]
                if s < steps - 1:
                    acc1[q, s, j] = total
                else:
                    fin1[q, j] = total
            if s < steps - 1:
                first_copy(q, s + 1).start()
            else:
                second_copy(q, 0).start()

    for s in range(steps):
        for q in range(quarters):
            second_copy(q, s).wait()
            d, a, b, first, second = plan(q)
            blk = (b - d * (s + 2) + 3 * ring) % ring
            total = rbuf2[q, s] + fin1[q, blk]
            if s < steps - 1:
                acc2[q, s] = total
                second_copy(q, s + 1).start()
            else:
                out_ref[q] = total


def reduce_scatter(part, ring):
    quarters, rows, tile_width, width = part.shape
    half = rows // 2
    steps = ring - 1
    f32 = jnp.float32
    return pl.pallas_call(
        functools.partial(rs_kernel, ring),
        out_shape=jax.ShapeDtypeStruct((quarters, tile_width, width), f32),
        in_specs=[pl.BlockSpec(memory_space=pltpu.VMEM)],
        out_specs=pl.BlockSpec(memory_space=pltpu.VMEM),
        scratch_shapes=[
            pltpu.VMEM((quarters, half, tile_width, width), f32),
            pltpu.VMEM((quarters, half, tile_width, width), f32),
            pltpu.VMEM((quarters, steps, ring, tile_width, width), f32),
            pltpu.VMEM((quarters, steps - 1, ring, tile_width, width), f32),
            pltpu.VMEM((quarters, ring, tile_width, width), f32),
            pltpu.VMEM((quarters, steps, tile_width, width), f32),
            pltpu.VMEM((quarters, steps - 1, tile_width, width), f32),
            pltpu.SemaphoreType.DMA((quarters,)),
            pltpu.SemaphoreType.DMA((quarters,)),
            pltpu.SemaphoreType.DMA((quarters, steps)),
            pltpu.SemaphoreType.DMA((quarters, steps)),
            pltpu.SemaphoreType.DMA((quarters, steps)),
            pltpu.SemaphoreType.DMA((quarters, steps)),
        ],
        compiler_params=pltpu.CompilerParams(
            collective_id=0, has_side_effects=True, vmem_limit_bytes=VMEM_LIMIT
        ),
    )(part)


def on_device(grid_tiles, tile_rows, tile_cols, tile_owner, integrals):
    op_count = lax.axis_size("opair")
    vp_count = lax.axis_size("vpair")
    devices = op_count * vp_count
    slot_count, tile_width, _ = grid_tiles.shape
    owned = slot_count // 2
    capacity = slot_count // devices
    kc_local = integrals.shape[0] // tile_width
    int_table = jnp.swapaxes(integrals.reshape(kc_local, tile_width, integrals.shape[1]), 1, 2)
    live_slots = tile_owner >= 0
    target = jnp.where(live_slots, tile_owner // owned, devices)
    matches = (target[:, None] == jnp.arange(devices, dtype=jnp.int32)[None, :]).astype(jnp.int32)
    earlier = jnp.sum((jnp.cumsum(matches, axis=0) - matches) * matches, axis=1)
    placing = jnp.where(live_slots, target * capacity + earlier, devices * capacity)
    src = (
        jnp.full((devices * capacity + 1,), -1, jnp.int32)
        .at[placing]
        .set(jnp.arange(slot_count, dtype=jnp.int32))[: devices * capacity]
    )
    departing_tiles = gather_tiles(src, grid_tiles)
    label_rows = jnp.stack([tile_owner % owned, tile_rows % RT_OP, tile_cols % kc_local], axis=1)
    labels = jnp.where((src >= 0)[:, None], jnp.take(label_rows, jnp.maximum(src, 0), axis=0), -1)
    arrived = lax.all_to_all(labels, ("opair", "vpair"), split_axis=0, concat_axis=0, tiled=True)
    incoming = lax.all_to_all(
        departing_tiles, ("opair", "vpair"), split_axis=0, concat_axis=0, tiled=True
    )
    valid = arrived[:, 0] >= 0
    row_in = arrived[:, 1]
    slot_ids = jnp.arange(slot_count, dtype=jnp.int32)
    earlier_same = (row_in[None, :] == row_in[:, None]) & valid[None, :] & (slot_ids[None, :] < slot_ids[:, None])
    first = (valid & ~jnp.any(earlier_same, axis=1)).astype(jnp.int32)
    row_ids = jnp.arange(RT_OP, dtype=jnp.int32)
    empty = (~jnp.any((row_in[None, :] == row_ids[:, None]) & valid[None, :], axis=1)).astype(jnp.int32)
    meta = jnp.concatenate([jnp.transpose(arrived).reshape(-1), first, empty])
    ring = 4
    ov_tiles, partial_value = place_and_contract(
        meta, incoming, int_table, owned, RT_OP, QUARTERS, ring
    )
    cycle_t = reduce_scatter(partial_value, ring)
    cycle_sum = jnp.transpose(cycle_t.reshape(-1, tile_width))
    return (ov_tiles, cycle_sum)


def solution(mesh):
    in_specs = (
        P(("opair", "vpair"), None, None),
        P(("opair", "vpair")),
        P(("opair", "vpair")),
        P(("opair", "vpair")),
        P("vpair", None),
    )
    out_specs = (P(("opair", "vpair"), None, None), P(("opair", "vpair"), None))
    return jax.shard_map(
        on_device, mesh=mesh, in_specs=in_specs, out_specs=out_specs, check_vma=False
    )
```

```python
import functools

import jax
import jax.numpy as jnp
from jax import lax
from jax.experimental import pallas as pl
from jax.experimental.pallas import tpu as pltpu
from jax.sharding import PartitionSpec as P

RT_OP = 32
QUARTERS = 8
MESH = pl.DeviceIdType.MESH
VMEM_LIMIT = 60 * 1024 * 1024


def gather_kernel(src_ref, grid_ref, out_ref):
    zero = jnp.zeros(out_ref.shape[1:], out_ref.dtype)

    def body(j, carry):
        s = src_ref[j]

        @pl.when(s >= 0)
        def _():
            out_ref[j] = grid_ref[jnp.maximum(s, 0)]

        @pl.when(s < 0)
        def _():
            out_ref[j] = zero

        return carry

    lax.fori_loop(0, out_ref.shape[0], body, 0)


def gather_tiles(src, grid_tiles):
    return pl.pallas_call(
        gather_kernel,
        out_shape=jax.ShapeDtypeStruct(grid_tiles.shape, grid_tiles.dtype),
        in_specs=[
            pl.BlockSpec(memory_space=pltpu.SMEM),
            pl.BlockSpec(memory_space=pltpu.VMEM),
        ],
        out_specs=pl.BlockSpec(memory_space=pltpu.VMEM),
        compiler_params=pltpu.CompilerParams(vmem_limit_bytes=VMEM_LIMIT),
    )(src, grid_tiles)


def storage_row(q, row, ring):
    c = row % 2
    y = (row // 2) % ring
    z = row // (2 * ring)
    half = ring * ring
    if q < QUARTERS // 2:
        return c * half + y * ring + z
    return c * half + z * ring + y


def place_kernel(quarters, ring, meta_ref, inc_ref, int_ref, ov_ref, part_ref):
    slots = inc_ref.shape[0]
    width = part_ref.shape[2]
    part_ref[...] = jnp.zeros(part_ref.shape, part_ref.dtype)

    def body(i, carry):
        pos = meta_ref[i]
        row = meta_ref[slots + i]
        col = meta_ref[2 * slots + i]

        @pl.when(pos >= 0)
        def _():
            tile = inc_ref[i]
            ov_ref[jnp.maximum(pos, 0)] = tile.T
            for k in range(quarters):
                block = int_ref[jnp.maximum(col, 0), pl.ds(k * width, width), :]
                s = storage_row(k, jnp.maximum(row, 0), ring)
                part_ref[k, s] += jnp.dot(block, tile, preferred_element_type=jnp.float32)

        return carry

    lax.fori_loop(0, slots, body, 0)


def place_and_contract(meta, incoming, int_table, owned, rows, quarters, ring):
    tile_width = incoming.shape[1]
    columns = int_table.shape[1]
    return pl.pallas_call(
        functools.partial(place_kernel, quarters, ring),
        out_shape=(
            jax.ShapeDtypeStruct((owned, tile_width, tile_width), incoming.dtype),
            jax.ShapeDtypeStruct((quarters, rows, columns // quarters, tile_width), jnp.float32),
        ),
        in_specs=[
            pl.BlockSpec(memory_space=pltpu.SMEM),
            pl.BlockSpec(memory_space=pltpu.VMEM),
            pl.BlockSpec(memory_space=pltpu.VMEM),
        ],
        out_specs=(
            pl.BlockSpec(memory_space=pltpu.VMEM),
            pl.BlockSpec(memory_space=pltpu.VMEM),
        ),
        compiler_params=pltpu.CompilerParams(vmem_limit_bytes=VMEM_LIMIT),
    )(meta, incoming, int_table)


def rs_kernel(ring, part_ref, out_ref, core_buf, red, rbuf1, acc1, fin1, rbuf2, acc2,
              core_send, core_recv, send1, recv1, send2, recv2):
    quarters, rows, tile_width, width = part_ref.shape
    half = rows // 2
    steps = ring - 1
    op = lax.axis_index("opair")
    v = lax.axis_index("vpair")
    c = v % 2
    y = (v // 2) % ring
    z = v // (2 * ring)

    def dev(zz, yy, cc):
        return (op, (zz * ring + yy) * 2 + cc)

    sib = dev(z, y, 1 - c)
    y_up = dev(z, (y + 1) % ring, c)
    y_dn = dev(z, (y + ring - 1) % ring, c)
    z_up = dev((z + 1) % ring, y, c)
    z_dn = dev((z + ring - 1) % ring, y, c)

    barrier = pltpu.get_barrier_semaphore()
    for peer in (sib, y_up, y_dn, z_up, z_dn):
        pl.semaphore_signal(barrier, inc=1, device_id=peer, device_id_type=MESH)
    pl.semaphore_wait(barrier, 5)

    def plan(q):
        d = 1 if q % 2 == 0 else -1
        if q < quarters // 2:
            return d, y, z, (y_up if d > 0 else y_dn), (z_up if d > 0 else z_dn)
        return d, z, y, (z_up if d > 0 else z_dn), (y_up if d > 0 else y_dn)

    def core_copy(q):
        return pltpu.make_async_remote_copy(
            src_ref=part_ref.at[q, pl.ds((1 - c) * half, half)],
            dst_ref=core_buf.at[q],
            send_sem=core_send.at[q],
            recv_sem=core_recv.at[q],
            device_id=sib,
            device_id_type=MESH,
        )

    def first_copy(q, s):
        d, a, b, first, second = plan(q)
        if s == 0:
            blk = (a - d + 2 * ring) % ring
            src = red.at[q, pl.ds(blk * ring, ring)]
        else:
            src = acc1.at[q, s - 1]
        return pltpu.make_async_remote_copy(
            src_ref=src,
            dst_ref=rbuf1.at[q, s],
            send_sem=send1.at[q, s],
            recv_sem=recv1.at[q, s],
            device_id=first,
            device_id_type=MESH,
        )

    def second_copy(q, s):
        d, a, b, first, second = plan(q)
        if s == 0:
            src = fin1.at[q, (b - d + 2 * ring) % ring]
        else:
            src = acc2.at[q, s - 1]
        return pltpu.make_async_remote_copy(
            src_ref=src,
            dst_ref=rbuf2.at[q, s],
            send_sem=send2.at[q, s],
            recv_sem=recv2.at[q, s],
            device_id=second,
            device_id_type=MESH,
        )

    ahead = 2
    for q in range(ahead):
        core_copy(q).start()

    for q in range(quarters):
        core_copy(q).wait()
        if q + ahead < quarters:
            core_copy(q + ahead).start()

        def core_sum(i, carry):
            red[q, i] = part_ref[q, c * half + i] + core_buf[q, i]
            return carry

        lax.fori_loop(0, half, core_sum, 0)
        first_copy(q, 0).start()

    for s in range(steps):
        for q in range(quarters):
            first_copy(q, s).wait()
            d, a, b, first, second = plan(q)
            blk = (a - d * (s + 2) + 3 * ring) % ring
            for j in range(ring):
                total = rbuf1[q, s, j] + red[q, blk * ring + j]
                if s < steps - 1:
                    acc1[q, s, j] = total
                else:
                    fin1[q, j] = total
            if s < steps - 1:
                first_copy(q, s + 1).start()
            else:
                second_copy(q, 0).start()

    for s in range(steps):
        for q in range(quarters):
            second_copy(q, s).wait()
            d, a, b, first, second = plan(q)
            blk = (b - d * (s + 2) + 3 * ring) % ring
            total = rbuf2[q, s] + fin1[q, blk]
            if s < steps - 1:
                acc2[q, s] = total
                second_copy(q, s + 1).start()
            else:
                out_ref[q] = total


def reduce_scatter(part, ring):
    quarters, rows, tile_width, width = part.shape
    half = rows // 2
    steps = ring - 1
    f32 = jnp.float32
    return pl.pallas_call(
        functools.partial(rs_kernel, ring),
        out_shape=jax.ShapeDtypeStruct((quarters, tile_width, width), f32),
        in_specs=[pl.BlockSpec(memory_space=pltpu.VMEM)],
        out_specs=pl.BlockSpec(memory_space=pltpu.VMEM),
        scratch_shapes=[
            pltpu.VMEM((quarters, half, tile_width, width), f32),
            pltpu.VMEM((quarters, half, tile_width, width), f32),
            pltpu.VMEM((quarters, steps, ring, tile_width, width), f32),
            pltpu.VMEM((quarters, steps - 1, ring, tile_width, width), f32),
            pltpu.VMEM((quarters, ring, tile_width, width), f32),
            pltpu.VMEM((quarters, steps, tile_width, width), f32),
            pltpu.VMEM((quarters, steps - 1, tile_width, width), f32),
            pltpu.SemaphoreType.DMA((quarters,)),
            pltpu.SemaphoreType.DMA((quarters,)),
            pltpu.SemaphoreType.DMA((quarters, steps)),
            pltpu.SemaphoreType.DMA((quarters, steps)),
            pltpu.SemaphoreType.DMA((quarters, steps)),
            pltpu.SemaphoreType.DMA((quarters, steps)),
        ],
        compiler_params=pltpu.CompilerParams(
            collective_id=0, has_side_effects=True, vmem_limit_bytes=VMEM_LIMIT
        ),
    )(part)


def on_device(grid_tiles, tile_rows, tile_cols, tile_owner, integrals):
    op_count = lax.axis_size("opair")
    vp_count = lax.axis_size("vpair")
    devices = op_count * vp_count
    slot_count, tile_width, _ = grid_tiles.shape
    owned = slot_count // 2
    capacity = slot_count // devices
    kc_local = integrals.shape[0] // tile_width
    int_table = jnp.swapaxes(integrals.reshape(kc_local, tile_width, integrals.shape[1]), 1, 2)
    live_slots = tile_owner >= 0
    target = jnp.where(live_slots, tile_owner // owned, devices)
    matches = (target[:, None] == jnp.arange(devices, dtype=jnp.int32)[None, :]).astype(jnp.int32)
    earlier = jnp.sum((jnp.cumsum(matches, axis=0) - matches) * matches, axis=1)
    placing = jnp.where(live_slots, target * capacity + earlier, devices * capacity)
    src = (
        jnp.full((devices * capacity + 1,), -1, jnp.int32)
        .at[placing]
        .set(jnp.arange(slot_count, dtype=jnp.int32))[: devices * capacity]
    )
    departing_tiles = gather_tiles(src, grid_tiles)
    label_rows = jnp.stack([tile_owner % owned, tile_rows % RT_OP, tile_cols % kc_local], axis=1)
    labels = jnp.where((src >= 0)[:, None], jnp.take(label_rows, jnp.maximum(src, 0), axis=0), -1)
    arrived = lax.all_to_all(labels, ("opair", "vpair"), split_axis=0, concat_axis=0, tiled=True)
    incoming = lax.all_to_all(
        departing_tiles, ("opair", "vpair"), split_axis=0, concat_axis=0, tiled=True
    )
    meta = jnp.transpose(arrived).reshape(-1)
    ring = 4
    ov_tiles, partial_value = place_and_contract(
        meta, incoming, int_table, owned, RT_OP, QUARTERS, ring
    )
    cycle_t = reduce_scatter(partial_value, ring)
    cycle_sum = jnp.transpose(cycle_t.reshape(-1, tile_width))
    return (ov_tiles, cycle_sum)


def solution(mesh):
    in_specs = (
        P(("opair", "vpair"), None, None),
        P(("opair", "vpair")),
        P(("opair", "vpair")),
        P(("opair", "vpair")),
        P("vpair", None),
    )
    out_specs = (P(("opair", "vpair"), None, None), P(("opair", "vpair"), None))
    return jax.shard_map(
        on_device, mesh=mesh, in_specs=in_specs, out_specs=out_specs, check_vma=False
    )
```

```python
import functools

import jax
import jax.numpy as jnp
from jax import lax
from jax.experimental import pallas as pl
from jax.experimental.pallas import tpu as pltpu
from jax.sharding import PartitionSpec as P

RT_OP = 32
QUARTERS = 8
MESH = pl.DeviceIdType.MESH
VMEM_LIMIT = 60 * 1024 * 1024


def gather_kernel(src_ref, grid_ref, out_ref):
    zero = jnp.zeros(out_ref.shape[1:], out_ref.dtype)

    def body(j, carry):
        s = src_ref[j]

        @pl.when(s >= 0)
        def _():
            out_ref[j] = grid_ref[jnp.maximum(s, 0)]

        @pl.when(s < 0)
        def _():
            out_ref[j] = zero

        return carry

    lax.fori_loop(0, out_ref.shape[0], body, 0)


def gather_tiles(src, grid_tiles):
    return pl.pallas_call(
        gather_kernel,
        out_shape=jax.ShapeDtypeStruct(grid_tiles.shape, grid_tiles.dtype),
        in_specs=[
            pl.BlockSpec(memory_space=pltpu.SMEM),
            pl.BlockSpec(memory_space=pltpu.VMEM),
        ],
        out_specs=pl.BlockSpec(memory_space=pltpu.VMEM),
        compiler_params=pltpu.CompilerParams(vmem_limit_bytes=VMEM_LIMIT),
    )(src, grid_tiles)


def storage_row(q, row, ring):
    c = row % 2
    y = (row // 2) % ring
    z = row // (2 * ring)
    half = ring * ring
    if q < QUARTERS // 2:
        return c * half + y * ring + z
    return c * half + z * ring + y


def place_kernel(quarters, ring, meta_ref, inc_ref, int_ref, ov_ref, part_ref):
    slots = inc_ref.shape[0]
    width = part_ref.shape[2]
    part_ref[...] = jnp.zeros(part_ref.shape, part_ref.dtype)

    def body(i, carry):
        pos = meta_ref[i]
        row = meta_ref[slots + i]
        col = meta_ref[2 * slots + i]

        @pl.when(pos >= 0)
        def _():
            tile = inc_ref[i]
            ov_ref[jnp.maximum(pos, 0)] = tile.T
            for q in range(quarters // 2):
                block = int_ref[jnp.maximum(col, 0), pl.ds(2 * q * width, 2 * width), :]
                prod = jnp.dot(block, tile, preferred_element_type=jnp.float32)
                for h in range(2):
                    k = 2 * q + h
                    s = storage_row(k, jnp.maximum(row, 0), ring)
                    part_ref[k, s] += prod[h * width : (h + 1) * width, :]

        return carry

    lax.fori_loop(0, slots, body, 0)


def place_and_contract(meta, incoming, int_table, owned, rows, quarters, ring):
    tile_width = incoming.shape[1]
    columns = int_table.shape[1]
    return pl.pallas_call(
        functools.partial(place_kernel, quarters, ring),
        out_shape=(
            jax.ShapeDtypeStruct((owned, tile_width, tile_width), incoming.dtype),
            jax.ShapeDtypeStruct((quarters, rows, columns // quarters, tile_width), jnp.float32),
        ),
        in_specs=[
            pl.BlockSpec(memory_space=pltpu.SMEM),
            pl.BlockSpec(memory_space=pltpu.VMEM),
            pl.BlockSpec(memory_space=pltpu.VMEM),
        ],
        out_specs=(
            pl.BlockSpec(memory_space=pltpu.VMEM),
            pl.BlockSpec(memory_space=pltpu.VMEM),
        ),
        compiler_params=pltpu.CompilerParams(vmem_limit_bytes=VMEM_LIMIT),
    )(meta, incoming, int_table)


def rs_kernel(ring, part_ref, out_ref, core_buf, red, rbuf1, acc1, fin1, rbuf2, acc2,
              core_send, core_recv, send1, recv1, send2, recv2):
    quarters, rows, tile_width, width = part_ref.shape
    half = rows // 2
    steps = ring - 1
    op = lax.axis_index("opair")
    v = lax.axis_index("vpair")
    c = v % 2
    y = (v // 2) % ring
    z = v // (2 * ring)

    def dev(zz, yy, cc):
        return (op, (zz * ring + yy) * 2 + cc)

    sib = dev(z, y, 1 - c)
    y_up = dev(z, (y + 1) % ring, c)
    y_dn = dev(z, (y + ring - 1) % ring, c)
    z_up = dev((z + 1) % ring, y, c)
    z_dn = dev((z + ring - 1) % ring, y, c)

    barrier = pltpu.get_barrier_semaphore()
    for peer in (sib, y_up, y_dn, z_up, z_dn):
        pl.semaphore_signal(barrier, inc=1, device_id=peer, device_id_type=MESH)
    pl.semaphore_wait(barrier, 5)

    def plan(q):
        d = 1 if q % 2 == 0 else -1
        if q < quarters // 2:
            return d, y, z, (y_up if d > 0 else y_dn), (z_up if d > 0 else z_dn)
        return d, z, y, (z_up if d > 0 else z_dn), (y_up if d > 0 else y_dn)

    def core_copy(q):
        return pltpu.make_async_remote_copy(
            src_ref=part_ref.at[q, pl.ds((1 - c) * half, half)],
            dst_ref=core_buf.at[q],
            send_sem=core_send.at[q],
            recv_sem=core_recv.at[q],
            device_id=sib,
            device_id_type=MESH,
        )

    def first_copy(q, s):
        d, a, b, first, second = plan(q)
        if s == 0:
            blk = (a - d + 2 * ring) % ring
            src = red.at[q, pl.ds(blk * ring, ring)]
        else:
            src = acc1.at[q, s - 1]
        return pltpu.make_async_remote_copy(
            src_ref=src,
            dst_ref=rbuf1.at[q, s],
            send_sem=send1.at[q, s],
            recv_sem=recv1.at[q, s],
            device_id=first,
            device_id_type=MESH,
        )

    def second_copy(q, s):
        d, a, b, first, second = plan(q)
        if s == 0:
            src = fin1.at[q, (b - d + 2 * ring) % ring]
        else:
            src = acc2.at[q, s - 1]
        return pltpu.make_async_remote_copy(
            src_ref=src,
            dst_ref=rbuf2.at[q, s],
            send_sem=send2.at[q, s],
            recv_sem=recv2.at[q, s],
            device_id=second,
            device_id_type=MESH,
        )

    ahead = 2
    order = [q for pair in zip(range(quarters // 2), range(quarters // 2, quarters)) for q in pair]
    for n in range(ahead):
        core_copy(order[n]).start()

    for n, q in enumerate(order):
        core_copy(q).wait()
        if n + ahead < quarters:
            core_copy(order[n + ahead]).start()

        def core_sum(i, carry):
            red[q, i] = part_ref[q, c * half + i] + core_buf[q, i]
            return carry

        lax.fori_loop(0, half, core_sum, 0)
        first_copy(q, 0).start()

    for s in range(steps):
        for q in order:
            first_copy(q, s).wait()
            d, a, b, first, second = plan(q)
            blk = (a - d * (s + 2) + 3 * ring) % ring
            for j in range(ring):
                total = rbuf1[q, s, j] + red[q, blk * ring + j]
                if s < steps - 1:
                    acc1[q, s, j] = total
                else:
                    fin1[q, j] = total
            if s < steps - 1:
                first_copy(q, s + 1).start()
            else:
                second_copy(q, 0).start()

    for s in range(steps):
        for q in range(quarters):
            second_copy(q, s).wait()
            d, a, b, first, second = plan(q)
            blk = (b - d * (s + 2) + 3 * ring) % ring
            total = rbuf2[q, s] + fin1[q, blk]
            if s < steps - 1:
                acc2[q, s] = total
                second_copy(q, s + 1).start()
            else:
                out_ref[q] = total


def reduce_scatter(part, ring):
    quarters, rows, tile_width, width = part.shape
    half = rows // 2
    steps = ring - 1
    f32 = jnp.float32
    return pl.pallas_call(
        functools.partial(rs_kernel, ring),
        out_shape=jax.ShapeDtypeStruct((quarters, tile_width, width), f32),
        in_specs=[pl.BlockSpec(memory_space=pltpu.VMEM)],
        out_specs=pl.BlockSpec(memory_space=pltpu.VMEM),
        scratch_shapes=[
            pltpu.VMEM((quarters, half, tile_width, width), f32),
            pltpu.VMEM((quarters, half, tile_width, width), f32),
            pltpu.VMEM((quarters, steps, ring, tile_width, width), f32),
            pltpu.VMEM((quarters, steps - 1, ring, tile_width, width), f32),
            pltpu.VMEM((quarters, ring, tile_width, width), f32),
            pltpu.VMEM((quarters, steps, tile_width, width), f32),
            pltpu.VMEM((quarters, steps - 1, tile_width, width), f32),
            pltpu.SemaphoreType.DMA((quarters,)),
            pltpu.SemaphoreType.DMA((quarters,)),
            pltpu.SemaphoreType.DMA((quarters, steps)),
            pltpu.SemaphoreType.DMA((quarters, steps)),
            pltpu.SemaphoreType.DMA((quarters, steps)),
            pltpu.SemaphoreType.DMA((quarters, steps)),
        ],
        compiler_params=pltpu.CompilerParams(
            collective_id=0, has_side_effects=True, vmem_limit_bytes=VMEM_LIMIT
        ),
    )(part)


def on_device(grid_tiles, tile_rows, tile_cols, tile_owner, integrals):
    op_count = lax.axis_size("opair")
    vp_count = lax.axis_size("vpair")
    devices = op_count * vp_count
    slot_count, tile_width, _ = grid_tiles.shape
    owned = slot_count // 2
    capacity = slot_count // devices
    kc_local = integrals.shape[0] // tile_width
    int_table = jnp.swapaxes(integrals.reshape(kc_local, tile_width, integrals.shape[1]), 1, 2)
    live_slots = tile_owner >= 0
    target = jnp.where(live_slots, tile_owner // owned, devices)
    matches = (target[:, None] == jnp.arange(devices, dtype=jnp.int32)[None, :]).astype(jnp.int32)
    earlier = jnp.sum((jnp.cumsum(matches, axis=0) - matches) * matches, axis=1)
    placing = jnp.where(live_slots, target * capacity + earlier, devices * capacity)
    src = (
        jnp.full((devices * capacity + 1,), -1, jnp.int32)
        .at[placing]
        .set(jnp.arange(slot_count, dtype=jnp.int32))[: devices * capacity]
    )
    departing_tiles = gather_tiles(src, grid_tiles)
    label_rows = jnp.stack([tile_owner % owned, tile_rows % RT_OP, tile_cols % kc_local], axis=1)
    labels = jnp.where((src >= 0)[:, None], jnp.take(label_rows, jnp.maximum(src, 0), axis=0), -1)
    arrived = lax.all_to_all(labels, ("opair", "vpair"), split_axis=0, concat_axis=0, tiled=True)
    incoming = lax.all_to_all(
        departing_tiles, ("opair", "vpair"), split_axis=0, concat_axis=0, tiled=True
    )
    meta = jnp.transpose(arrived).reshape(-1)
    ring = 4
    ov_tiles, partial_value = place_and_contract(
        meta, incoming, int_table, owned, RT_OP, QUARTERS, ring
    )
    cycle_t = reduce_scatter(partial_value, ring)
    cycle_sum = jnp.transpose(cycle_t.reshape(-1, tile_width))
    return (ov_tiles, cycle_sum)


def solution(mesh):
    in_specs = (
        P(("opair", "vpair"), None, None),
        P(("opair", "vpair")),
        P(("opair", "vpair")),
        P(("opair", "vpair")),
        P("vpair", None),
    )
    out_specs = (P(("opair", "vpair"), None, None), P(("opair", "vpair"), None))
    return jax.shard_map(
        on_device, mesh=mesh, in_specs=in_specs, out_specs=out_specs, check_vma=False
    )
```

```python
import functools

import jax
import jax.numpy as jnp
from jax import lax
from jax.experimental import pallas as pl
from jax.experimental.pallas import tpu as pltpu
from jax.sharding import PartitionSpec as P

RT_OP = 32
QUARTERS = 8
MESH = pl.DeviceIdType.MESH
VMEM_LIMIT = 60 * 1024 * 1024


def gather_kernel(src_ref, grid_ref, out_ref):
    zero = jnp.zeros(out_ref.shape[1:], out_ref.dtype)

    def body(j, carry):
        s = src_ref[j]

        @pl.when(s >= 0)
        def _():
            out_ref[j] = grid_ref[jnp.maximum(s, 0)]

        @pl.when(s < 0)
        def _():
            out_ref[j] = zero

        return carry

    lax.fori_loop(0, out_ref.shape[0], body, 0)


def gather_tiles(src, grid_tiles):
    return pl.pallas_call(
        gather_kernel,
        out_shape=jax.ShapeDtypeStruct(grid_tiles.shape, grid_tiles.dtype),
        in_specs=[
            pl.BlockSpec(memory_space=pltpu.SMEM),
            pl.BlockSpec(memory_space=pltpu.VMEM),
        ],
        out_specs=pl.BlockSpec(memory_space=pltpu.VMEM),
        compiler_params=pltpu.CompilerParams(vmem_limit_bytes=VMEM_LIMIT),
    )(src, grid_tiles)


def storage_row(q, row, ring):
    c = row % 2
    y = (row // 2) % ring
    z = row // (2 * ring)
    half = ring * ring
    if q < QUARTERS // 2:
        return c * half + y * ring + z
    return c * half + z * ring + y


def place_kernel(quarters, ring, meta_ref, inc_ref, int_ref, ov_ref, part_ref):
    slots = inc_ref.shape[0]
    width = part_ref.shape[2]
    part_ref[...] = jnp.zeros(part_ref.shape, part_ref.dtype)

    def body(i, carry):
        pos = meta_ref[i]
        row = meta_ref[slots + i]
        col = meta_ref[2 * slots + i]

        @pl.when(pos >= 0)
        def _():
            tile = inc_ref[i]
            ov_ref[jnp.maximum(pos, 0)] = tile.T
            for q in range(quarters // 2):
                block = int_ref[jnp.maximum(col, 0), pl.ds(2 * q * width, 2 * width), :]
                prod = jnp.dot(block, tile, preferred_element_type=jnp.float32)
                for h in range(2):
                    k = 2 * q + h
                    s = storage_row(k, jnp.maximum(row, 0), ring)
                    part_ref[k, s] += prod[h * width : (h + 1) * width, :]

        return carry

    lax.fori_loop(0, slots, body, 0)


def place_and_contract(meta, incoming, int_table, owned, rows, quarters, ring):
    tile_width = incoming.shape[1]
    columns = int_table.shape[1]
    return pl.pallas_call(
        functools.partial(place_kernel, quarters, ring),
        out_shape=(
            jax.ShapeDtypeStruct((owned, tile_width, tile_width), incoming.dtype),
            jax.ShapeDtypeStruct((quarters, rows, columns // quarters, tile_width), jnp.float32),
        ),
        in_specs=[
            pl.BlockSpec(memory_space=pltpu.SMEM),
            pl.BlockSpec(memory_space=pltpu.VMEM),
            pl.BlockSpec(memory_space=pltpu.VMEM),
        ],
        out_specs=(
            pl.BlockSpec(memory_space=pltpu.VMEM),
            pl.BlockSpec(memory_space=pltpu.VMEM),
        ),
        compiler_params=pltpu.CompilerParams(vmem_limit_bytes=VMEM_LIMIT),
    )(meta, incoming, int_table)


def rs_kernel(ring, part_ref, out_ref, core_buf, red, rbuf1, acc1, fin1, rbuf2, acc2,
              core_send, core_recv, send1, recv1, send2, recv2):
    quarters, rows, tile_width, width = part_ref.shape
    half = rows // 2
    steps = ring - 1
    op = lax.axis_index("opair")
    v = lax.axis_index("vpair")
    c = v % 2
    y = (v // 2) % ring
    z = v // (2 * ring)

    def dev(zz, yy, cc):
        return (op, (zz * ring + yy) * 2 + cc)

    sib = dev(z, y, 1 - c)
    y_up = dev(z, (y + 1) % ring, c)
    y_dn = dev(z, (y + ring - 1) % ring, c)
    z_up = dev((z + 1) % ring, y, c)
    z_dn = dev((z + ring - 1) % ring, y, c)

    barrier = pltpu.get_barrier_semaphore()
    for peer in (sib, y_up, y_dn, z_up, z_dn):
        pl.semaphore_signal(barrier, inc=1, device_id=peer, device_id_type=MESH)
    pl.semaphore_wait(barrier, 5)

    def plan(q):
        d = 1 if q % 2 == 0 else -1
        if q < quarters // 2:
            return d, y, z, (y_up if d > 0 else y_dn), (z_up if d > 0 else z_dn)
        return d, z, y, (z_up if d > 0 else z_dn), (y_up if d > 0 else y_dn)

    def core_copy(q):
        return pltpu.make_async_remote_copy(
            src_ref=part_ref.at[q, pl.ds((1 - c) * half, half)],
            dst_ref=core_buf.at[q],
            send_sem=core_send.at[q],
            recv_sem=core_recv.at[q],
            device_id=sib,
            device_id_type=MESH,
        )

    def first_copy(q, s):
        d, a, b, first, second = plan(q)
        if s == 0:
            blk = (a - d + 2 * ring) % ring
            src = red.at[q, pl.ds(blk * ring, ring)]
        else:
            src = acc1.at[q, s - 1]
        return pltpu.make_async_remote_copy(
            src_ref=src,
            dst_ref=rbuf1.at[q, s],
            send_sem=send1.at[q, s],
            recv_sem=recv1.at[q, s],
            device_id=first,
            device_id_type=MESH,
        )

    def second_copy(q, s):
        d, a, b, first, second = plan(q)
        if s == 0:
            src = fin1.at[q, (b - d + 2 * ring) % ring]
        else:
            src = acc2.at[q, s - 1]
        return pltpu.make_async_remote_copy(
            src_ref=src,
            dst_ref=rbuf2.at[q, s],
            send_sem=send2.at[q, s],
            recv_sem=recv2.at[q, s],
            device_id=second,
            device_id_type=MESH,
        )

    ahead = 2
    order = [q for pair in zip(range(quarters // 2), range(quarters // 2, quarters)) for q in pair]
    for n in range(ahead):
        core_copy(order[n]).start()

    for n, q in enumerate(order):
        core_copy(q).wait()
        if n + ahead < quarters:
            core_copy(order[n + ahead]).start()

        def core_sum(i, carry):
            red[q, i] = part_ref[q, c * half + i] + core_buf[q, i]
            return carry

        lax.fori_loop(0, half, core_sum, 0)
        first_copy(q, 0).start()

    for s in range(steps):
        for q in order:
            first_copy(q, s).wait()
            d, a, b, first, second = plan(q)
            blk = (a - d * (s + 2) + 3 * ring) % ring
            for j in range(ring):
                total = rbuf1[q, s, j] + red[q, blk * ring + j]
                if s < steps - 1:
                    acc1[q, s, j] = total
                else:
                    fin1[q, j] = total
            if s < steps - 1:
                first_copy(q, s + 1).start()
            else:
                second_copy(q, 0).start()

    for s in range(steps):
        for q in order:
            second_copy(q, s).wait()
            d, a, b, first, second = plan(q)
            blk = (b - d * (s + 2) + 3 * ring) % ring
            total = rbuf2[q, s] + fin1[q, blk]
            if s < steps - 1:
                acc2[q, s] = total
                second_copy(q, s + 1).start()
            else:
                out_ref[q] = total


def reduce_scatter(part, ring):
    quarters, rows, tile_width, width = part.shape
    half = rows // 2
    steps = ring - 1
    f32 = jnp.float32
    return pl.pallas_call(
        functools.partial(rs_kernel, ring),
        out_shape=jax.ShapeDtypeStruct((quarters, tile_width, width), f32),
        in_specs=[pl.BlockSpec(memory_space=pltpu.VMEM)],
        out_specs=pl.BlockSpec(memory_space=pltpu.VMEM),
        scratch_shapes=[
            pltpu.VMEM((quarters, half, tile_width, width), f32),
            pltpu.VMEM((quarters, half, tile_width, width), f32),
            pltpu.VMEM((quarters, steps, ring, tile_width, width), f32),
            pltpu.VMEM((quarters, steps - 1, ring, tile_width, width), f32),
            pltpu.VMEM((quarters, ring, tile_width, width), f32),
            pltpu.VMEM((quarters, steps, tile_width, width), f32),
            pltpu.VMEM((quarters, steps - 1, tile_width, width), f32),
            pltpu.SemaphoreType.DMA((quarters,)),
            pltpu.SemaphoreType.DMA((quarters,)),
            pltpu.SemaphoreType.DMA((quarters, steps)),
            pltpu.SemaphoreType.DMA((quarters, steps)),
            pltpu.SemaphoreType.DMA((quarters, steps)),
            pltpu.SemaphoreType.DMA((quarters, steps)),
        ],
        compiler_params=pltpu.CompilerParams(
            collective_id=0, has_side_effects=True, vmem_limit_bytes=VMEM_LIMIT
        ),
    )(part)


def on_device(grid_tiles, tile_rows, tile_cols, tile_owner, integrals):
    op_count = lax.axis_size("opair")
    vp_count = lax.axis_size("vpair")
    devices = op_count * vp_count
    slot_count, tile_width, _ = grid_tiles.shape
    owned = slot_count // 2
    capacity = slot_count // devices
    kc_local = integrals.shape[0] // tile_width
    int_table = jnp.swapaxes(integrals.reshape(kc_local, tile_width, integrals.shape[1]), 1, 2)
    live_slots = tile_owner >= 0
    target = jnp.where(live_slots, tile_owner // owned, devices)
    matches = (target[:, None] == jnp.arange(devices, dtype=jnp.int32)[None, :]).astype(jnp.int32)
    earlier = jnp.sum((jnp.cumsum(matches, axis=0) - matches) * matches, axis=1)
    placing = jnp.where(live_slots, target * capacity + earlier, devices * capacity)
    src = (
        jnp.full((devices * capacity + 1,), -1, jnp.int32)
        .at[placing]
        .set(jnp.arange(slot_count, dtype=jnp.int32))[: devices * capacity]
    )
    departing_tiles = gather_tiles(src, grid_tiles)
    label_rows = jnp.stack([tile_owner % owned, tile_rows % RT_OP, tile_cols % kc_local], axis=1)
    labels = jnp.where((src >= 0)[:, None], jnp.take(label_rows, jnp.maximum(src, 0), axis=0), -1)
    arrived = lax.all_to_all(labels, ("opair", "vpair"), split_axis=0, concat_axis=0, tiled=True)
    incoming = lax.all_to_all(
        departing_tiles, ("opair", "vpair"), split_axis=0, concat_axis=0, tiled=True
    )
    meta = jnp.transpose(arrived).reshape(-1)
    ring = 4
    ov_tiles, partial_value = place_and_contract(
        meta, incoming, int_table, owned, RT_OP, QUARTERS, ring
    )
    cycle_t = reduce_scatter(partial_value, ring)
    cycle_sum = jnp.transpose(cycle_t.reshape(-1, tile_width))
    return (ov_tiles, cycle_sum)


def solution(mesh):
    in_specs = (
        P(("opair", "vpair"), None, None),
        P(("opair", "vpair")),
        P(("opair", "vpair")),
        P(("opair", "vpair")),
        P("vpair", None),
    )
    out_specs = (P(("opair", "vpair"), None, None), P(("opair", "vpair"), None))
    return jax.shard_map(
        on_device, mesh=mesh, in_specs=in_specs, out_specs=out_specs, check_vma=False
    )
```
